32 devices in a mesh: dp: 32 (over z, y, x, core).
Axes of the slice: x: 2, y: 2, z: 4, core: 2. Of those that a mesh axis runs over, the one named last changes fastest.
Arguments:
- tokens: float32 [64, 197, 384], P('dp'), may hold values from -6 to 6
- params: float32 [1774080], P('dp'), as said below
- moment1: float32 [1774080], P('dp'), may hold values from -0.0625 to 0.0625
- moment2: float32 [1774080], P('dp'), may hold values from 1e-06 to 1e-05
- cotangent: float32 [64, 197, 384], P('dp'), may hold values from -6 to 6
Outputs:
- result: float32 [64, 197, 384], P('dp')
- grad_tokens: float32 [64, 197, 384], P('dp')
- grad_params: float32 [1774080], P('dp')
- new_params: float32 [1774080], P('dp')
- new_moment1: float32 [1774080], P('dp')
- new_moment2: float32 [1774080], P('dp')
The draws below stay inside these ranges and needn't reach their ends.
Inputs may be any that keep to these rules, and one draw needn't show every extreme that they name: `params`: finite floats.
All inputs are finite; a program needn't handle non-finite values.
Results may differ from the reference program's by a relative error of at most 0.0071.
The reference program's roundings to bfloat16 on the way count: a program that leaves them out, or rounds other values in their place, can miss the bound.
Values may be sent and summed in bfloat16 or wider, within the bound.
A program may use at most 128 MiB of HBM per device.

```python
import math
import jax
import jax.numpy as jnp
from jax import lax

D = 384
HEADS = 6
FF = 1536
SEQ = 197
IMG_MB = 1
STEP = 3
IMAGES = 64
TOKENS = 12608
NPARAM = 1774080


def draw_params(key, part):
    keys = jax.random.split(key, 6)
    w_qkv = jax.random.normal(keys[0], (D, 3 * D), jnp.float32) * D ** (-0.5)
    w_out = jax.random.normal(keys[1], (D, D), jnp.float32) * (3.2 * D ** (-0.5))
    w_up = jax.random.normal(keys[2], (D, FF), jnp.float32) * D ** (-0.5)
    w_down = jax.random.normal(keys[3], (FF, D), jnp.float32) * FF ** (-0.5)
    spread = jax.random.normal(keys[4], (8, D), jnp.float32)
    gain_rows = jnp.array([1.0, 0.0, 0.0, 0.0, 0.0, 1.0, 0.0, 0.0], jnp.float32)[:, None]
    spread_rows = jnp.array([0.1, 0.3, 0.3, 0.3, 0.3, 0.1, 0.3, 0.3], jnp.float32)[:, None]
    vectors = gain_rows + spread_rows * spread
    up_bias = jax.random.normal(keys[5], (FF,), jnp.float32) * 0.3
    return jnp.concatenate([w_qkv.reshape(-1), w_out.reshape(-1), w_up.reshape(-1), w_down.reshape(-1), vectors.reshape(-1), up_bias])


def block_scale(key, dims, pieces, low, largest):
    factor_of = 1.0
    for axis_at, blocks in pieces:
        steps = jax.random.uniform(jax.random.fold_in(jax.random.fold_in(key, 6), axis_at), (blocks,), jnp.float32, low / len(pieces), largest / len(pieces))
        factor_of = factor_of * jnp.repeat(jnp.exp(steps), dims[axis_at] // blocks).reshape((-1,) + (1,) * (len(dims) - 1 - axis_at))
    return factor_of


def centred(own_key, shape, scale, bound, pieces=(), kind=jnp.bfloat16):
    values = scale * jax.random.normal(own_key, shape, jnp.float32)
    if pieces:
        values = values * block_scale(own_key, shape, pieces, -0.22, 0.18)
    return jnp.clip(values, -bound, bound).astype(kind)


def setup_inputs(seed: int = 0) -> dict:
    seeds = jax.random.split(jax.random.key(seed), 6)
    return {
        "tokens": centred(seeds[0], (IMAGES, SEQ, D), 1.0, 6.0, ((0, 32),), jnp.float32),
        "params": draw_params(jax.random.fold_in(seeds[5], 71), 0),
        "moment1": centred(seeds[2], (NPARAM,), 0.01, 0.0625, ((0, 32),), jnp.float32),
        "moment2": jnp.clip(jnp.exp(math.log(9.999999747378752e-06) - 2.3025851 * jax.random.uniform(seeds[3], (NPARAM,), jnp.float32) ** block_scale(seeds[3], (NPARAM,), ((0, 32),), -0.2, 0.2)), 9.999999974752427e-07, 9.999999747378752e-06),
        "cotangent": centred(seeds[4], (IMAGES, SEQ, D), 1.0, 6.0, ((0, 32),), jnp.float32),
    }


def product(spec, left, right):
    return jnp.einsum(spec, left.astype(jnp.float32), right.astype(jnp.float32), precision=lax.Precision.HIGHEST)

def token_sum(left, right):
    return lax.dot_general(left, right, (((0,), (0,)), ((), ())), preferred_element_type=jnp.float32)

def times_t(left, right):
    return lax.dot_general(left, right, (((1,), (1,)), ((), ())), preferred_element_type=jnp.float32)

def layer_norm(values):
    center = values - lax.optimization_barrier(jnp.mean(values, axis=-1, keepdims=True))
    factor = lax.rsqrt(lax.optimization_barrier(jnp.mean(center * center, axis=-1, keepdims=True)) + 1e-06)
    return (center * factor, factor)

def norm_back(grad_hat, normed, factor):
    return factor * (grad_hat - lax.optimization_barrier(jnp.mean(grad_hat, axis=-1, keepdims=True)) - normed * lax.optimization_barrier(jnp.mean(grad_hat * normed, axis=-1, keepdims=True)))

def unpack(flat):
    first = 3 * D * D
    second = first + D * D
    third = second + D * FF
    fourth = third + FF * D
    fifth = fourth + 8 * D
    return (flat[:first].reshape(D, 3 * D), flat[first:second].reshape(D, D), flat[second:third].reshape(D, FF), flat[third:fourth].reshape(FF, D), flat[fourth:fifth].astype(jnp.float32).reshape(8, D), flat[fifth:].astype(jnp.float32))

def forward(tokens_mb, weights):
    w_qkv, w_out, w_up, w_down, vectors, up_bias = weights
    batch, length, width = tokens_mb.shape
    normed_in, scale_in = layer_norm(tokens_mb)
    attn_input = (normed_in * vectors[0] + vectors[1]).astype(jnp.bfloat16).reshape(-1, width)
    projected = jnp.dot(attn_input, w_qkv, preferred_element_type=jnp.float32)
    heads_shape = (batch, length, HEADS, width // HEADS)
    query_half = (projected[:, :width] + vectors[2]).astype(jnp.bfloat16).reshape(heads_shape)
    key_half = projected[:, width:2 * width].astype(jnp.bfloat16).reshape(heads_shape)
    value_half = (projected[:, 2 * width:] + vectors[3]).astype(jnp.bfloat16).reshape(heads_shape)
    scores = product('bqhe,bkhe->bhqk', query_half, key_half) * (width // HEADS) ** (-0.5)
    top = lax.optimization_barrier(jnp.max(scores, axis=-1, keepdims=True))
    raw_weights = jnp.exp(scores - top)
    total = lax.optimization_barrier(jnp.sum(raw_weights, axis=-1, keepdims=True))
    log_total = top + jnp.log(total)
    probs = (raw_weights / total).astype(jnp.bfloat16)
    context = product('bhqk,bkhe->bqhe', probs, value_half).astype(jnp.bfloat16).reshape(-1, width)
    hidden_mid = tokens_mb + (jnp.dot(context, w_out, preferred_element_type=jnp.float32) + vectors[4]).reshape(tokens_mb.shape)
    normed_mid, scale_mid = layer_norm(hidden_mid)
    mlp_input = (normed_mid * vectors[5] + vectors[6]).astype(jnp.bfloat16).reshape(-1, width)
    pre_act = jnp.dot(mlp_input, w_up, preferred_element_type=jnp.float32) + up_bias
    activated = jax.nn.gelu(pre_act, approximate=False).astype(jnp.bfloat16)
    result = hidden_mid + (jnp.dot(activated, w_down, preferred_element_type=jnp.float32) + vectors[7]).reshape(tokens_mb.shape)
    saved = (normed_in, scale_in, attn_input, query_half, key_half, value_half, log_total, context, normed_mid, scale_mid, mlp_input, pre_act, activated)
    return (result, saved)

def backward(saved, grad_result, weights):
    w_qkv, w_out, w_up, w_down, vectors, up_bias = weights
    normed_in, scale_in, attn_input, query_half, key_half, value_half, log_total, context, normed_mid, scale_mid, mlp_input, pre_act, activated = saved
    width = grad_result.shape[-1]
    grad_flat = grad_result.reshape(-1, width)
    grad_half = grad_flat.astype(jnp.bfloat16)
    grad_down = token_sum(activated, grad_half)
    grad_act = times_t(grad_half, w_down)
    slope = 0.5 * (1.0 + jax.scipy.special.erf(pre_act * 0.7071067811865476)) + pre_act * jnp.exp(-0.5 * pre_act * pre_act) * 0.3989422804014327
    grad_pre = grad_act * slope
    grad_pre_half = grad_pre.astype(jnp.bfloat16)
    grad_up = token_sum(mlp_input, grad_pre_half)
    grad_mlp_in = times_t(grad_pre_half, w_up)
    mid_flat = normed_mid.reshape(-1, width)
    grad_hidden = grad_result + norm_back((grad_mlp_in * vectors[5]).reshape(grad_result.shape), normed_mid, scale_mid)
    hidden_flat = grad_hidden.reshape(-1, width)
    hidden_half = hidden_flat.astype(jnp.bfloat16)
    grad_wout = token_sum(context, hidden_half)
    grad_context = times_t(hidden_half, w_out).astype(jnp.bfloat16).reshape(query_half.shape)
    scale_factor = (width // HEADS) ** (-0.5)
    scores = product('bqhe,bkhe->bhqk', query_half, key_half) * scale_factor
    probs_full = jnp.exp(scores - log_total)
    probs_half = probs_full.astype(jnp.bfloat16)
    grad_value = product('bhqk,bqhe->bkhe', probs_half, grad_context)
    grad_probs = product('bqhe,bkhe->bhqk', grad_context, value_half)
    delta = lax.optimization_barrier(jnp.sum(probs_full * grad_probs, axis=-1, keepdims=True))
    grad_scores = (probs_full * (grad_probs - delta) * scale_factor).astype(jnp.bfloat16)
    grad_query = product('bhqk,bkhe->bqhe', grad_scores, key_half).reshape(-1, width)
    grad_key = product('bhqk,bqhe->bkhe', grad_scores, query_half).reshape(-1, width)
    grad_value = grad_value.reshape(-1, width)
    proj_half = jnp.concatenate([grad_query, grad_key, grad_value], axis=1).astype(jnp.bfloat16)
    grad_wqkv = token_sum(attn_input, proj_half)
    grad_attn_in = times_t(proj_half, w_qkv)
    in_flat = normed_in.reshape(-1, width)
    grad_tokens = grad_hidden + norm_back((grad_attn_in * vectors[0]).reshape(grad_result.shape), normed_in, scale_in)
    vector_grads = jnp.stack([lax.optimization_barrier(jnp.sum(grad_attn_in * in_flat, axis=0)), lax.optimization_barrier(jnp.sum(grad_attn_in, axis=0)), lax.optimization_barrier(jnp.sum(grad_query, axis=0)), lax.optimization_barrier(jnp.sum(grad_value, axis=0)), lax.optimization_barrier(jnp.sum(hidden_flat, axis=0)), lax.optimization_barrier(jnp.sum(grad_mlp_in * mid_flat, axis=0)), lax.optimization_barrier(jnp.sum(grad_mlp_in, axis=0)), lax.optimization_barrier(jnp.sum(grad_flat, axis=0))])
    flat = jnp.concatenate([grad_wqkv.reshape(-1), grad_wout.reshape(-1), grad_up.reshape(-1), grad_down.reshape(-1), vector_grads.reshape(-1), lax.optimization_barrier(jnp.sum(grad_pre, axis=0))])
    return (grad_tokens, flat)

def adamw(params, grads, first, second, position):
    first_end = 3 * D * D
    second_end = first_end + D * D
    third_end = second_end + D * FF
    fourth_end = third_end + FF * D
    rate = jnp.where(position < first_end, 0.01, jnp.where(position < second_end, 0.1, jnp.where(position < third_end, 0.01, jnp.where(position < fourth_end, 0.005, 0.1))))
    first_new = 0.9 * first + 0.1 * grads
    second_new = 0.999 * second + 0.001 * grads * grads
    update = first_new / (1.0 - 0.9 ** STEP) / (jnp.sqrt(second_new / (1.0 - 0.999 ** STEP)) + 1e-08) + 0.1 * params
    return (params - rate * update, first_new, second_new)

def reference(tokens, params, moment1, moment2, cotangent):
    weights = unpack(params.astype(jnp.bfloat16))
    blocks = tokens.reshape(-1, IMG_MB, SEQ, D)
    grad_blocks = cotangent.reshape(-1, IMG_MB, SEQ, D)

    def one_block(total, items):
        block, grad_block = items
        result, saved = forward(block, weights)
        grad_in, flat = backward(saved, grad_block, weights)
        return (total + flat, (result, grad_in))
    total, (results, grads_in) = lax.scan(one_block, jnp.zeros(params.shape, jnp.float32), (blocks, grad_blocks))
    grad_params = total * (1.0 / math.sqrt(TOKENS))
    position = jnp.arange(params.shape[0], dtype=jnp.int32)
    new_params, new_first, new_second = adamw(params, grad_params, moment1, moment2, position)
    return (results.reshape(tokens.shape), grads_in.reshape(tokens.shape), grad_params, new_params, new_first, new_second)
```

```python
import math

import jax
import jax.numpy as jnp
from jax import lax
from jax.experimental import pallas as pl
from jax.experimental.pallas import tpu as pltpu
import functools
from jax.sharding import PartitionSpec as P

D = 384
HEADS = 6
FF = 1536
SEQ = 197
STEP = 3


LANES = 128
LINES = 4 * 1152 + 12


def plan(devices, share):
    bits = devices.bit_length() - 1
    rows = -(-(share + D - 1) // D)
    rows = -(-rows // 32) * 32
    far = list(range(bits - 1, 2, -1))
    orders = [far + [1, 2, 0], far + [2, 1, 0]]
    half = rows // 2
    if half % 16 == 0 and half > 16:
        first = -(-half // 2 // 16) * 16
        sizes = [first, first, half - first, half - first]
    else:
        sizes = [half, half]
    parts = []
    start = 0
    for index, size in enumerate(sizes):
        parts.append((start, size, orders[index % 2]))
        start += size
    return bits, rows, parts


def place(device, order):
    spot = 0
    for index, bit in enumerate(order):
        spot = spot + ((device // 2**bit) % 2) * 2**index
    return spot


def other(device, bit):
    step = 2**bit
    return device + step - 2 * step * ((device // step) % 2)


def greet(me, bits):
    barrier = pltpu.get_barrier_semaphore()
    for bit in range(bits):
        pl.semaphore_signal(
            barrier, inc=1, device_id=(other(me, bit),), device_id_type=pl.DeviceIdType.MESH
        )
    pl.semaphore_wait(barrier, bits)


def gather_kernel(devices, share, shard, w_qkv, w_out, w_up, w_down, tail, lines, *rest):
    bits, rows, parts = plan(devices, share)
    slots = rest[: len(parts)]
    local_sem, send_sem, recv_sem = rest[len(parts) :]
    me = lax.axis_index("dp")
    own = []
    for index, (start, size, order) in enumerate(parts):
        copy = pltpu.make_async_copy(
            shard.at[pl.ds(start, size)], slots[index].at[place(me, order)], local_sem.at[index]
        )
        copy.start()
        own.append(copy)
    greet(me, bits)
    for copy in own:
        copy.wait()
    waiting = [None] * len(parts)
    for stage in range(bits):
        for index, (start, size, order) in enumerate(parts):
            if waiting[index] is not None:
                waiting[index].wait()
            block = 2**stage
            begin = (place(me, order) // block) * block
            piece = slots[index].at[pl.ds(begin, block)]
            copy = pltpu.make_async_remote_copy(
                src_ref=piece,
                dst_ref=piece,
                send_sem=send_sem.at[index, stage],
                recv_sem=recv_sem.at[index, stage],
                device_id=(other(me, order[stage]),),
                device_id_type=pl.DeviceIdType.MESH,
            )
            copy.start()
            waiting[index] = copy
    for copy in waiting:
        copy.wait()
    chunks = D // LANES
    for device in range(devices):
        first = device * share // D
        shared = device * share % D != 0
        for index, (start, size, order) in enumerate(parts):
            spot = place(device, order)
            at = first + start
            for chunk in range(chunks):
                if start == 0 and shared:
                    before = lines[chunk, at : at + 1, :]
                lines[chunk, at : at + size, :] = slots[index][
                    spot, :, chunk * LANES : (chunk + 1) * LANES
                ].astype(jnp.float32)
                if start == 0 and shared:
                    lines[chunk, at : at + 1, :] = lines[chunk, at : at + 1, :] + before
    spread(lines, 0, w_qkv, 3)
    spread(lines, 1152, w_out, 1)
    spread(lines, 1536, w_up, 4)
    spread(lines, 3072, w_down, 1)
    spread(lines, 4608, tail, 1)


def spread(lines, first, out, times):
    height = out.shape[0]
    for column in range(times):
        for chunk in range(D // LANES):
            if times == 1:
                value = lines[chunk, first : first + height, :]
            else:
                value = lines[chunk, pl.ds(first + column, height, stride=times), :]
            at = column * D + chunk * LANES
            out[:, at : at + LANES] = value.astype(out.dtype)


def gather_weights(params, devices):
    share = params.shape[0]
    bits, rows, parts = plan(devices, share)
    offset = (lax.axis_index("dp") * share) % D
    flat = jnp.zeros((rows * D,), jnp.float32)
    flat = lax.dynamic_update_slice(flat, params, (offset,))
    shard = flat.reshape(rows, D).astype(jnp.bfloat16)
    vmem = pl.BlockSpec(memory_space=pltpu.VMEM)
    return pl.pallas_call(
        functools.partial(gather_kernel, devices, share),
        out_shape=(
            jax.ShapeDtypeStruct((D, 3 * D), jnp.bfloat16),
            jax.ShapeDtypeStruct((D, D), jnp.bfloat16),
            jax.ShapeDtypeStruct((D, FF), jnp.bfloat16),
            jax.ShapeDtypeStruct((FF, D), jnp.bfloat16),
            jax.ShapeDtypeStruct((16, D), jnp.float32),
        ),
        in_specs=[vmem],
        out_specs=[vmem] * 5,
        scratch_shapes=[pltpu.VMEM((D // LANES, LINES + rows + 24, LANES), jnp.float32)]
        + [pltpu.VMEM((devices, size, D), jnp.bfloat16) for _, size, _ in parts]
        + [
            pltpu.SemaphoreType.DMA((len(parts),)),
            pltpu.SemaphoreType.DMA((len(parts), bits)),
            pltpu.SemaphoreType.DMA((len(parts), bits)),
        ],
        compiler_params=pltpu.CompilerParams(
            collective_id=0, has_side_effects=True, vmem_limit_bytes=60 * 2**20
        ),
    )(shard)


def scatter_kernel(devices, share, g_qkv, g_out, g_up, g_down, g_tail, out, lines, *rest):
    bits, rows, parts = plan(devices, share)
    count = len(parts)
    slots, landed, sums = rest[:count], rest[count : 2 * count], rest[2 * count : 3 * count]
    send_sem, recv_sem = rest[3 * count :]
    me = lax.axis_index("dp")
    collect(lines, 0, g_qkv, 3)
    collect(lines, 1152, g_out, 1)
    collect(lines, 1536, g_up, 4)
    collect(lines, 3072, g_down, 1)
    collect(lines, 4608, g_tail, 1)
    lines[:, 4624:, :] = jnp.zeros_like(lines[:, 4624:, :])
    for device in range(devices):
        first = device * share // D
        for index, (start, size, order) in enumerate(parts):
            spot = place(device, order)
            at = first + start
            for chunk in range(D // LANES):
                slots[index][spot, :, chunk * LANES : (chunk + 1) * LANES] = lines[
                    chunk, at : at + size, :
                ].astype(jnp.bfloat16)
    greet(me, bits)
    waiting = [None] * count

    def send(index, stage):
        order = parts[index][2]
        block = 2**stage
        spot = place(me, order) // block
        away = spot + 1 - 2 * (spot % 2)
        copy = pltpu.make_async_remote_copy(
            src_ref=slots[index].at[pl.ds(away * block, block)],
            dst_ref=landed[index].at[pl.ds(block - 1, block)],
            send_sem=send_sem.at[index, stage],
            recv_sem=recv_sem.at[index, stage],
            device_id=(other(me, order[stage]),),
            device_id_type=pl.DeviceIdType.MESH,
        )
        copy.start()
        return copy

    for index in range(count):
        waiting[index] = send(index, bits - 1)
    for stage in range(bits - 1, -1, -1):
        for index, (start, size, order) in enumerate(parts):
            waiting[index].wait()
            block = 2**stage
            begin = (place(me, order) // block) * block
            if stage == 0:
                piece = sums[index][begin] if bits > 1 else slots[index][begin].astype(jnp.float32)
                out[start : start + size, :] = piece + landed[index][0].astype(jnp.float32)
                continue

            def add(step, carry, index=index, begin=begin, block=block, stage=stage):
                spot = begin + step
                if stage == bits - 1:
                    old = slots[index][spot].astype(jnp.float32)
                else:
                    old = sums[index][spot]
                new = old + landed[index][block - 1 + step].astype(jnp.float32)
                sums[index][spot] = new
                slots[index][spot] = new.astype(jnp.bfloat16)
                return carry

            lax.fori_loop(0, block, add, 0)
            waiting[index] = send(index, stage - 1)


def collect(lines, first, grads, times):
    height = grads.shape[0]
    for column in range(times):
        for chunk in range(D // LANES):
            at = column * D + chunk * LANES
            value = grads[:, at : at + LANES]
            if times == 1:
                lines[chunk, first : first + height, :] = value
            else:
                lines[chunk, pl.ds(first + column, height, stride=times), :] = value


def scatter_grads(grads, devices, share):
    bits, rows, parts = plan(devices, share)
    vmem = pl.BlockSpec(memory_space=pltpu.VMEM)
    total = pl.pallas_call(
        functools.partial(scatter_kernel, devices, share),
        out_shape=jax.ShapeDtypeStruct((rows, D), jnp.float32),
        in_specs=[vmem] * 5,
        out_specs=vmem,
        scratch_shapes=[pltpu.VMEM((D // LANES, LINES + rows + 24, LANES), jnp.float32)]
        + [pltpu.VMEM((devices, size, D), jnp.bfloat16) for _, size, _ in parts]
        + [pltpu.VMEM((devices, size, D), jnp.bfloat16) for _, size, _ in parts]
        + [pltpu.VMEM((devices, size, D), jnp.float32) for _, size, _ in parts]
        + [
            pltpu.SemaphoreType.DMA((len(parts), bits)),
            pltpu.SemaphoreType.DMA((len(parts), bits)),
        ],
        compiler_params=pltpu.CompilerParams(
            collective_id=1, has_side_effects=True, vmem_limit_bytes=63 * 2**20
        ),
    )(*grads)
    offset = (lax.axis_index("dp") * share) % D
    return lax.dynamic_slice(total.reshape(-1), (offset,), (share,))


PAD = 208


def dot_nn(left, right):
    return lax.dot_general(left, right, (((1,), (0,)), ((), ())), preferred_element_type=jnp.float32)


def dot_nt(left, right):
    return lax.dot_general(left, right, (((1,), (1,)), ((), ())), preferred_element_type=jnp.float32)


def dot_tn(left, right):
    return lax.dot_general(left, right, (((0,), (0,)), ((), ())), preferred_element_type=jnp.float32)


def layer_norm(values):
    center = values - jnp.mean(values, axis=-1, keepdims=True)
    factor = lax.rsqrt(jnp.mean(center * center, axis=-1, keepdims=True) + 1e-06)
    return center * factor, factor


def norm_back(grad_hat, normed, factor):
    return factor * (
        grad_hat
        - jnp.mean(grad_hat, axis=-1, keepdims=True)
        - normed * jnp.mean(grad_hat * normed, axis=-1, keepdims=True)
    )


def column_sum(values):
    return jnp.sum(values, axis=0, keepdims=True)


def images_of(padded):
    return [(image, slice(image * PAD, (image + 1) * PAD)) for image in range(padded.shape[0] // PAD)]


def compute_kernel(
    tokens, cot, w_qkv, w_out, w_up, w_down, tail,
    result, grad_tokens, g_qkv, g_out, g_up, g_down, g_tail,
    xbuf, dybuf, xhat, a16, qkv16, probs, o16, h, xhat2, c16, acc, dc, dy16, dh, dh16, do16, dqkv16, s1, s2,
):
    load(tokens, xbuf)
    load(cot, dybuf)
    attention_in(xbuf, tail, xhat, s1, a16, w_qkv, qkv16)
    attention(qkv16, probs, o16)
    middle(xbuf, o16, w_out, tail, h, xhat2, s2, c16, dybuf, dy16)
    feed_forward(c16, dy16, w_up, w_down, tail, acc, dc, g_up, g_down, g_tail)
    feed_forward_end(h, acc, tail, dc, xhat2, s2, dybuf, result, dh, dh16, g_tail)
    attention_out_back(o16, dh16, w_out, g_out, do16)
    attention_back(qkv16, probs, do16, dqkv16, g_tail)
    attention_in_back(a16, dqkv16, w_qkv, g_qkv, tail, xhat, s1, dh, grad_tokens, g_tail)


def load(source, padded):
    for image in range(source.shape[0]):
        at = image * PAD
        padded[at + PAD - 16 : at + PAD, :] = jnp.zeros((16, D), jnp.float32)
        padded[at : at + SEQ, :] = source[image]


def attention_in(xbuf, tail, xhat, s1, a16, w_qkv, qkv16):
    for _, rows in images_of(xbuf):
        normed, factor = layer_norm(xbuf[rows, :])
        xhat[rows, :] = normed
        s1[rows, :] = factor
        a16[rows, :] = (normed * tail[0:1, :] + tail[1:2, :]).astype(jnp.bfloat16)
    for piece in range(3):
        cols = slice(piece * D, (piece + 1) * D)
        value = dot_nn(a16[...], w_qkv[:, cols])
        if piece == 0:
            value = value + tail[2:3, :]
        if piece == 2:
            value = value + tail[3:4, :]
        qkv16[:, cols] = value.astype(jnp.bfloat16)


def half_of(values, half):
    lane = lax.broadcasted_iota(jnp.int32, values.shape, 1)
    return jnp.where((lane < 64) if half == 0 else (lane >= 64), values, jnp.zeros_like(values))


def views(step):
    image, pair = step // 3, step % 3
    rows = pl.ds(pl.multiple_of(image * PAD, 16), PAD)
    return rows, [pl.ds(pl.multiple_of(part * D + pair * 128, 128), 128) for part in range(3)]


def attention(qkv16, probs, o16):
    def body(step, carry):
        rows, (qs, ks, vs) = views(step)
        query, key, value = qkv16[rows, qs], qkv16[rows, ks], qkv16[rows, vs]
        total = None
        for half in range(2):
            scores = dot_nt(query, half_of(key, half)) * 0.125
            column = lax.broadcasted_iota(jnp.int32, scores.shape, 1)
            scores = jnp.where(column < SEQ, scores, -jnp.inf)
            raised = jnp.exp(scores - jnp.max(scores, axis=-1, keepdims=True))
            prob = raised / jnp.sum(raised, axis=-1, keepdims=True)
            probs[step * 2 + half] = prob
            term = dot_nn(prob.astype(jnp.bfloat16), half_of(value, half))
            total = term if total is None else total + term
        o16[rows, qs] = total.astype(jnp.bfloat16)
        return carry

    lax.fori_loop(0, qkv16.shape[0] // PAD * 3, body, 0)


def middle(xbuf, o16, w_out, tail, h, xhat2, s2, c16, dybuf, dy16):
    for _, rows in images_of(xbuf):
        value = xbuf[rows, :] + (dot_nn(o16[rows, :], w_out[...]) + tail[4:5, :])
        h[rows, :] = value
        normed, factor = layer_norm(value)
        xhat2[rows, :] = normed
        s2[rows, :] = factor
        c16[rows, :] = (normed * tail[5:6, :] + tail[6:7, :]).astype(jnp.bfloat16)
        dy16[rows, :] = dybuf[rows, :].astype(jnp.bfloat16)


CHUNK = 128


def feed_forward(c16, dy16, w_up, w_down, tail, acc, dc, g_up, g_down, g_tail):
    acc[...] = jnp.zeros_like(acc)
    dc[...] = jnp.zeros_like(dc)
    per = D // CHUNK
    for line in range(4):

        def body(step, carry, line=line):
            at = pl.multiple_of(step * CHUNK, CHUNK)
            where = pl.multiple_of(line * D + step * CHUNK, CHUNK)
            cols = pl.ds(where, CHUNK)
            up = w_up[:, cols]
            down = w_down[cols, :]
            pre = dot_nn(c16[...], up) + tail[8 + line : 9 + line, pl.ds(at, CHUNK)]
            phi = 0.5 * (1.0 + lax.erf(pre * 0.7071067811865476))
            slope = phi + pre * jnp.exp(-0.5 * pre * pre) * 0.3989422804014327
            act = (pre * phi).astype(jnp.bfloat16)
            acc[...] += dot_nn(act, down)
            g_down[cols, :] = dot_tn(act, dy16[...])
            grad_pre = dot_nt(dy16[...], down) * slope
            half = grad_pre.astype(jnp.bfloat16)
            g_up[:, cols] = dot_tn(c16[...], half)
            g_tail[8 + line : 9 + line, pl.ds(at, CHUNK)] = column_sum(grad_pre)
            dc[...] += dot_nt(half, up)
            return carry

        lax.fori_loop(0, per, body, 0)


def feed_forward_end(h, acc, tail, dc, xhat2, s2, dybuf, result, dh, dh16, g_tail):
    sums = [0.0] * 4
    for image, rows in images_of(h):
        value = h[rows, :] + (acc[rows, :] + tail[7:8, :])
        result[image] = value[:SEQ]
        grad, normed = dc[rows, :], xhat2[rows, :]
        hidden = dybuf[rows, :] + norm_back(grad * tail[5:6, :], normed, s2[rows, :])
        dh[rows, :] = hidden
        dh16[rows, :] = hidden.astype(jnp.bfloat16)
        terms = (hidden, grad * normed, grad, dybuf[rows, :])
        sums = [old + column_sum(new) for old, new in zip(sums, terms)]
    for index in range(4):
        g_tail[4 + index : 5 + index, :] = sums[index]
    g_tail[12:16, :] = jnp.zeros((4, D), jnp.float32)


def attention_out_back(o16, dh16, w_out, g_out, do16):
    g_out[...] = dot_tn(o16[...], dh16[...])
    do16[...] = dot_nt(dh16[...], w_out[...]).astype(jnp.bfloat16)


def attention_back(qkv16, probs, do16, dqkv16, g_tail):
    g_tail[2:4, :] = jnp.zeros((2, D), jnp.float32)

    def body(step, carry):
        rows, (qs, ks, vs) = views(step)
        query, key, value, grad = qkv16[rows, qs], qkv16[rows, ks], qkv16[rows, vs], do16[rows, qs]
        dq = dk = dv = None
        for half in range(2):
            prob = probs[step * 2 + half]
            dv_term = dot_tn(prob.astype(jnp.bfloat16), half_of(grad, half))
            grad_prob = dot_nt(grad, half_of(value, half))
            delta = jnp.sum(prob * grad_prob, axis=-1, keepdims=True)
            ds = (prob * (grad_prob - delta) * 0.125).astype(jnp.bfloat16)
            dq_term = dot_nn(ds, half_of(key, half))
            dk_term = dot_tn(ds, half_of(query, half))
            if half == 0:
                dq, dk, dv = dq_term, dk_term, dv_term
            else:
                dq, dk, dv = dq + dq_term, dk + dk_term, dv + dv_term
        dqkv16[rows, qs] = dq.astype(jnp.bfloat16)
        dqkv16[rows, ks] = dk.astype(jnp.bfloat16)
        dqkv16[rows, vs] = dv.astype(jnp.bfloat16)
        g_tail[2:3, qs] += column_sum(dq)
        g_tail[3:4, qs] += column_sum(dv)
        return carry

    lax.fori_loop(0, qkv16.shape[0] // PAD * 3, body, 0)


def attention_in_back(a16, dqkv16, w_qkv, g_qkv, tail, xhat, s1, dh, grad_tokens, g_tail):
    for piece in range(3):
        cols = slice(piece * D, (piece + 1) * D)
        g_qkv[:, cols] = dot_tn(a16[...], dqkv16[:, cols])
    sums = [0.0] * 2
    for image, rows in images_of(dh):
        grad, normed = dot_nt(dqkv16[rows, :], w_qkv[...]), xhat[rows, :]
        value = dh[rows, :] + norm_back(grad * tail[0:1, :], normed, s1[rows, :])
        grad_tokens[image] = value[:SEQ]
        sums = [old + column_sum(new) for old, new in zip(sums, (grad * normed, grad))]
    for index in range(2):
        g_tail[index : index + 1, :] = sums[index]


def compute_scratch(images):
    f32, bf16 = jnp.float32, jnp.bfloat16
    rows = images * PAD
    return [
        pltpu.VMEM((rows, D), f32),
        pltpu.VMEM((rows, D), f32),
        pltpu.VMEM((rows, D), f32),
        pltpu.VMEM((rows, D), bf16),
        pltpu.VMEM((rows, 3 * D), bf16),
        pltpu.VMEM((images * HEADS, PAD, PAD), f32),
        pltpu.VMEM((rows, D), bf16),
        pltpu.VMEM((rows, D), f32),
        pltpu.VMEM((rows, D), f32),
        pltpu.VMEM((rows, D), bf16),
        pltpu.VMEM((rows, D), f32),
        pltpu.VMEM((rows, D), f32),
        pltpu.VMEM((rows, D), bf16),
        pltpu.VMEM((rows, D), f32),
        pltpu.VMEM((rows, D), bf16),
        pltpu.VMEM((rows, D), bf16),
        pltpu.VMEM((rows, 3 * D), bf16),
        pltpu.VMEM((rows, 1), f32),
        pltpu.VMEM((rows, 1), f32),
    ]


def compute(tokens, cotangent, weights):
    f32 = jnp.float32
    vmem = pl.BlockSpec(memory_space=pltpu.VMEM)
    return pl.pallas_call(
        compute_kernel,
        out_shape=(
            jax.ShapeDtypeStruct(tokens.shape, f32),
            jax.ShapeDtypeStruct(tokens.shape, f32),
            jax.ShapeDtypeStruct((D, 3 * D), f32),
            jax.ShapeDtypeStruct((D, D), f32),
            jax.ShapeDtypeStruct((D, FF), f32),
            jax.ShapeDtypeStruct((FF, D), f32),
            jax.ShapeDtypeStruct((16, D), f32),
        ),
        in_specs=[vmem] * 7,
        out_specs=[vmem] * 7,
        scratch_shapes=compute_scratch(tokens.shape[0]),
        compiler_params=pltpu.CompilerParams(vmem_limit_bytes=60 * 2**20),
    )(tokens, cotangent, *weights)


def adamw(params, grads, first, second, position):
    first_end = 3 * D * D
    second_end = first_end + D * D
    third_end = second_end + D * FF
    fourth_end = third_end + FF * D
    rate = jnp.where(
        position < first_end,
        0.01,
        jnp.where(
            position < second_end,
            0.1,
            jnp.where(position < third_end, 0.01, jnp.where(position < fourth_end, 0.005, 0.1)),
        ),
    )
    first_new = 0.9 * first + 0.1 * grads
    second_new = 0.999 * second + 0.001 * grads * grads
    update = (
        first_new / (1.0 - 0.9**STEP) / (jnp.sqrt(second_new / (1.0 - 0.999**STEP)) + 1e-08)
        + 0.1 * params
    )
    return (params - rate * update, first_new, second_new)


def per_device(tokens, params, moment1, moment2, cotangent):
    devices = lax.axis_size("dp")
    length = params.shape[0]
    w_qkv, w_out, w_up, w_down, tail = gather_weights(params, devices)
    weights = (w_qkv, w_out, w_up, w_down, tail)
    result, grad_tokens, *grads = compute(tokens, cotangent, weights)
    shares = scatter_grads(grads, devices, length)
    count = tokens.shape[0] * tokens.shape[1] * devices
    grad_params = shares * (1.0 / math.sqrt(count))
    position = lax.axis_index("dp") * length + jnp.arange(length, dtype=jnp.int32)
    new_params, new_first, new_second = adamw(params, grad_params, moment1, moment2, position)
    return (result, grad_tokens, grad_params, new_params, new_first, new_second)


def solution(mesh):
    in_specs = (P("dp", None, None), P("dp"), P("dp"), P("dp"), P("dp", None, None))
    out_specs = (P("dp", None, None), P("dp", None, None), P("dp"), P("dp"), P("dp"), P("dp"))
    return jax.shard_map(
        per_device, mesh=mesh, in_specs=in_specs, out_specs=out_specs, check_vma=False
    )
```

```python
import math

import jax
import jax.numpy as jnp
from jax import lax
from jax.experimental import pallas as pl
from jax.experimental.pallas import tpu as pltpu
import functools
from jax.sharding import PartitionSpec as P

D = 384
HEADS = 6
FF = 1536
SEQ = 197
STEP = 3


LANES = 128
LINES = 4 * 1152 + 12


def plan(devices, share):
    bits = devices.bit_length() - 1
    rows = -(-(share + D - 1) // D)
    rows = -(-rows // 32) * 32
    far = list(range(bits - 1, 2, -1))
    orders = [far + [1, 2, 0], far + [2, 1, 0]]
    half = rows // 2
    if half % 16 == 0 and half > 16:
        first = -(-half // 2 // 16) * 16
        sizes = [first, first, half - first, half - first]
    else:
        sizes = [half, half]
    parts = []
    start = 0
    for index, size in enumerate(sizes):
        parts.append((start, size, orders[index % 2]))
        start += size
    return bits, rows, parts


def place(device, order):
    spot = 0
    for index, bit in enumerate(order):
        spot = spot + ((device // 2**bit) % 2) * 2**index
    return spot


def other(device, bit):
    step = 2**bit
    return device + step - 2 * step * ((device // step) % 2)


def flip(device, column):
    bit = 3
    while column:
        if column % 2:
            device = other(device, bit)
        column //= 2
        bit += 1
    return device


def slot_of(device, devices):
    return (device % 2) * (devices // 2) + device // 2


def meet(me, devices):
    barrier = pltpu.get_barrier_semaphore()
    partners = [other(me, bit) for bit in range(3)] + [flip(me, j) for j in range(1, devices // 8)]
    for partner in partners:
        pl.semaphore_signal(
            barrier, inc=1, device_id=(partner,), device_id_type=pl.DeviceIdType.MESH
        )
    pl.semaphore_wait(barrier, len(partners))


def columns_of(devices):
    order = list(range(devices // 8))
    return [0, 1, 3, 2] if devices == 32 else order


def row_plan(share):
    rows = -(-(share + D - 1) // D)
    rows = -(-rows // 32) * 32
    return rows, rows // 2


COLUMN, ALONG_X, ALONG_Y, TURN_X, TURN_Y, CORE = range(6)


def greet(me, bits):
    barrier = pltpu.get_barrier_semaphore()
    for bit in range(bits):
        pl.semaphore_signal(
            barrier, inc=1, device_id=(other(me, bit),), device_id_type=pl.DeviceIdType.MESH
        )
    pl.semaphore_wait(barrier, bits)


def gather_kernel(devices, share, shard, w_qkv, w_out, w_up, w_down, tail, lines, slots, send_sem, recv_sem):
    rows, half = row_plan(share)
    count = devices // 8
    me = lax.axis_index("dp")
    core, x_side, y_side = other(me, 0), other(me, 1), other(me, 2)
    whole, upper, lower = (0, rows), (0, half), (half, half)
    mine = slots.at[slot_of(me, devices)]
    copies = {}

    def copy(kind, column, source, target, device):
        made = pltpu.make_async_remote_copy(
            src_ref=source,
            dst_ref=target,
            send_sem=send_sem.at[kind * count + column],
            recv_sem=recv_sem.at[kind * count + column],
            device_id=(device,),
            device_id_type=pl.DeviceIdType.MESH,
        )
        made.start()
        copies[kind, column] = made

    def send(kind, column, owner, part, device):
        piece = slots.at[slot_of(owner, devices), pl.ds(part[0], part[1])]
        copy(kind, column, piece, piece, device)

    def along(column):
        copies[COLUMN, column].wait_recv()
        send(ALONG_X, column, flip(me, column), whole, x_side)
        send(ALONG_Y, column, flip(me, column), whole, y_side)

    def turn(column):
        copies[ALONG_X, column].wait_recv()
        send(TURN_Y, column, other(flip(me, column), 1), upper, y_side)
        copies[ALONG_Y, column].wait_recv()
        send(TURN_X, column, other(flip(me, column), 2), lower, x_side)

    def across(column):
        copies[TURN_Y, column].wait_recv()
        copies[TURN_X, column].wait_recv()
        first = (me % 2) * (devices // 2) + (flip(me, column) // 8) * 4
        layer = slots.at[pl.ds(first, 4)]
        copy(CORE, column, layer, layer, core)

    meet(me, devices)
    order = columns_of(devices)
    for index, column in enumerate(order[1:]):
        copy(COLUMN, column, shard, mine, flip(me, column))
        if index == 0:
            copy(ALONG_X, 0, shard, mine, x_side)
            copy(ALONG_Y, 0, shard, mine, y_side)
    mine[...] = shard[...]
    for index in range(len(order) + 2):
        if 1 <= index < len(order):
            along(order[index])
        if 0 <= index - 1 < len(order):
            turn(order[index - 1])
        if 0 <= index - 2 < len(order):
            across(order[index - 2])
    for (kind, column), made in copies.items():
        made.wait_send()
        if kind == CORE:
            made.wait_recv()
    chunks = D // LANES
    for device in range(devices):
        at = device * share // D
        shared = device * share % D != 0
        spot = slot_of(device, devices)
        for chunk in range(chunks):
            if shared:
                before = lines[chunk, at : at + 1, :]
            lines[chunk, at : at + rows, :] = slots[
                spot, :, chunk * LANES : (chunk + 1) * LANES
            ].astype(jnp.float32)
            if shared:
                lines[chunk, at : at + 1, :] = lines[chunk, at : at + 1, :] + before
    spread(lines, 0, w_qkv, 3)
    spread(lines, 1152, w_out, 1)
    spread(lines, 1536, w_up, 4)
    spread(lines, 3072, w_down, 1)
    spread(lines, 4608, tail, 1)


def spread(lines, first, out, times):
    height = out.shape[0]
    for column in range(times):
        for chunk in range(D // LANES):
            if times == 1:
                value = lines[chunk, first : first + height, :]
            else:
                value = lines[chunk, pl.ds(first + column, height, stride=times), :]
            at = column * D + chunk * LANES
            out[:, at : at + LANES] = value.astype(out.dtype)


def gather_weights(params, devices):
    share = params.shape[0]
    rows, _ = row_plan(share)
    offset = (lax.axis_index("dp") * share) % D
    flat = jnp.zeros((rows * D,), jnp.float32)
    flat = lax.dynamic_update_slice(flat, params, (offset,))
    shard = flat.reshape(rows, D).astype(jnp.bfloat16)
    vmem = pl.BlockSpec(memory_space=pltpu.VMEM)
    return pl.pallas_call(
        functools.partial(gather_kernel, devices, share),
        out_shape=(
            jax.ShapeDtypeStruct((D, 3 * D), jnp.bfloat16),
            jax.ShapeDtypeStruct((D, D), jnp.bfloat16),
            jax.ShapeDtypeStruct((D, FF), jnp.bfloat16),
            jax.ShapeDtypeStruct((FF, D), jnp.bfloat16),
            jax.ShapeDtypeStruct((16, D), jnp.float32),
        ),
        in_specs=[vmem],
        out_specs=[vmem] * 5,
        scratch_shapes=[
            pltpu.VMEM((D // LANES, LINES + rows + 24, LANES), jnp.float32),
            pltpu.VMEM((devices, rows, D), jnp.bfloat16),
            pltpu.SemaphoreType.DMA((6 * (devices // 8),)),
            pltpu.SemaphoreType.DMA((6 * (devices // 8),)),
        ],
        compiler_params=pltpu.CompilerParams(
            collective_id=0, has_side_effects=True, vmem_limit_bytes=60 * 2**20
        ),
    )(shard)


def scatter_kernel(devices, share, g_qkv, g_out, g_up, g_down, g_tail, out, lines, *rest):
    bits, rows, parts = plan(devices, share)
    count = len(parts)
    slots, landed, sums = rest[:count], rest[count : 2 * count], rest[2 * count : 3 * count]
    send_sem, recv_sem = rest[3 * count :]
    me = lax.axis_index("dp")
    collect(lines, 0, g_qkv, 3)
    collect(lines, 1152, g_out, 1)
    collect(lines, 1536, g_up, 4)
    collect(lines, 3072, g_down, 1)
    collect(lines, 4608, g_tail, 1)
    lines[:, 4624:, :] = jnp.zeros_like(lines[:, 4624:, :])
    for device in range(devices):
        first = device * share // D
        for index, (start, size, order) in enumerate(parts):
            spot = place(device, order)
            at = first + start
            for chunk in range(D // LANES):
                slots[index][spot, :, chunk * LANES : (chunk + 1) * LANES] = lines[
                    chunk, at : at + size, :
                ].astype(jnp.bfloat16)
    greet(me, bits)
    waiting = [None] * count

    def send(index, stage):
        order = parts[index][2]
        block = 2**stage
        spot = place(me, order) // block
        away = spot + 1 - 2 * (spot % 2)
        copy = pltpu.make_async_remote_copy(
            src_ref=slots[index].at[pl.ds(away * block, block)],
            dst_ref=landed[index].at[pl.ds(block - 1, block)],
            send_sem=send_sem.at[index, stage],
            recv_sem=recv_sem.at[index, stage],
            device_id=(other(me, order[stage]),),
            device_id_type=pl.DeviceIdType.MESH,
        )
        copy.start()
        return copy

    for index in range(count):
        waiting[index] = send(index, bits - 1)
    for stage in range(bits - 1, -1, -1):
        for index, (start, size, order) in enumerate(parts):
            waiting[index].wait()
            block = 2**stage
            begin = (place(me, order) // block) * block
            if stage == 0:
                piece = sums[index][begin] if bits > 1 else slots[index][begin].astype(jnp.float32)
                out[start : start + size, :] = piece + landed[index][0].astype(jnp.float32)
                continue

            def add(step, carry, index=index, begin=begin, block=block, stage=stage):
                spot = begin + step
                if stage == bits - 1:
                    old = slots[index][spot].astype(jnp.float32)
                else:
                    old = sums[index][spot]
                new = old + landed[index][block - 1 + step].astype(jnp.float32)
                sums[index][spot] = new
                slots[index][spot] = new.astype(jnp.bfloat16)
                return carry

            lax.fori_loop(0, block, add, 0)
            waiting[index] = send(index, stage - 1)


def collect(lines, first, grads, times):
    height = grads.shape[0]
    for column in range(times):
        for chunk in range(D // LANES):
            at = column * D + chunk * LANES
            value = grads[:, at : at + LANES]
            if times == 1:
                lines[chunk, first : first + height, :] = value
            else:
                lines[chunk, pl.ds(first + column, height, stride=times), :] = value


def scatter_grads(grads, devices, share):
    bits, rows, parts = plan(devices, share)
    vmem = pl.BlockSpec(memory_space=pltpu.VMEM)
    total = pl.pallas_call(
        functools.partial(scatter_kernel, devices, share),
        out_shape=jax.ShapeDtypeStruct((rows, D), jnp.float32),
        in_specs=[vmem] * 5,
        out_specs=vmem,
        scratch_shapes=[pltpu.VMEM((D // LANES, LINES + rows + 24, LANES), jnp.float32)]
        + [pltpu.VMEM((devices, size, D), jnp.bfloat16) for _, size, _ in parts]
        + [pltpu.VMEM((devices, size, D), jnp.bfloat16) for _, size, _ in parts]
        + [pltpu.VMEM((devices, size, D), jnp.float32) for _, size, _ in parts]
        + [
            pltpu.SemaphoreType.DMA((len(parts), bits)),
            pltpu.SemaphoreType.DMA((len(parts), bits)),
        ],
        compiler_params=pltpu.CompilerParams(
            collective_id=1, has_side_effects=True, vmem_limit_bytes=63 * 2**20
        ),
    )(*grads)
    offset = (lax.axis_index("dp") * share) % D
    return lax.dynamic_slice(total.reshape(-1), (offset,), (share,))


PAD = 208


def dot_nn(left, right):
    return lax.dot_general(left, right, (((1,), (0,)), ((), ())), preferred_element_type=jnp.float32)


def dot_nt(left, right):
    return lax.dot_general(left, right, (((1,), (1,)), ((), ())), preferred_element_type=jnp.float32)


def dot_tn(left, right):
    return lax.dot_general(left, right, (((0,), (0,)), ((), ())), preferred_element_type=jnp.float32)


def layer_norm(values):
    center = values - jnp.mean(values, axis=-1, keepdims=True)
    factor = lax.rsqrt(jnp.mean(center * center, axis=-1, keepdims=True) + 1e-06)
    return center * factor, factor


def norm_back(grad_hat, normed, factor):
    return factor * (
        grad_hat
        - jnp.mean(grad_hat, axis=-1, keepdims=True)
        - normed * jnp.mean(grad_hat * normed, axis=-1, keepdims=True)
    )


def column_sum(values):
    return jnp.sum(values, axis=0, keepdims=True)


def images_of(padded):
    return [(image, slice(image * PAD, (image + 1) * PAD)) for image in range(padded.shape[0] // PAD)]


def compute_kernel(
    tokens, cot, w_qkv, w_out, w_up, w_down, tail,
    result, grad_tokens, g_qkv, g_out, g_up, g_down, g_tail,
    xbuf, dybuf, xhat, a16, qkv16, probs, o16, h, xhat2, c16, acc, dc, dy16, dh, dh16, do16, dqkv16, s1, s2,
):
    load(tokens, xbuf)
    load(cot, dybuf)
    attention_in(xbuf, tail, xhat, s1, a16, w_qkv, qkv16)
    attention(qkv16, probs, o16)
    middle(xbuf, o16, w_out, tail, h, xhat2, s2, c16, dybuf, dy16)
    feed_forward(c16, dy16, w_up, w_down, tail, acc, dc, g_up, g_down, g_tail)
    feed_forward_end(h, acc, tail, dc, xhat2, s2, dybuf, result, dh, dh16, g_tail)
    attention_out_back(o16, dh16, w_out, g_out, do16)
    attention_back(qkv16, probs, do16, dqkv16, g_tail)
    attention_in_back(a16, dqkv16, w_qkv, g_qkv, tail, xhat, s1, dh, grad_tokens, g_tail)


def load(source, padded):
    for image in range(source.shape[1]):
        at = image * PAD
        padded[at + PAD - 16 : at + PAD, :] = jnp.zeros((16, D), jnp.float32)
        padded[at : at + SEQ, :] = source[:, image, :]


def attention_in(xbuf, tail, xhat, s1, a16, w_qkv, qkv16):
    for _, rows in images_of(xbuf):
        normed, factor = layer_norm(xbuf[rows, :])
        xhat[rows, :] = normed
        s1[rows, :] = factor
        a16[rows, :] = (normed * tail[0:1, :] + tail[1:2, :]).astype(jnp.bfloat16)
    for piece in range(3):
        cols = slice(piece * D, (piece + 1) * D)
        value = dot_nn(a16[...], w_qkv[:, cols])
        if piece == 0:
            value = value + tail[2:3, :]
        if piece == 2:
            value = value + tail[3:4, :]
        qkv16[:, cols] = value.astype(jnp.bfloat16)


def half_of(values, half):
    lane = lax.broadcasted_iota(jnp.int32, values.shape, 1)
    return jnp.where((lane < 64) if half == 0 else (lane >= 64), values, jnp.zeros_like(values))


def views(step):
    image, pair = step // 3, step % 3
    rows = pl.ds(pl.multiple_of(image * PAD, 16), PAD)
    return rows, [pl.ds(pl.multiple_of(part * D + pair * 128, 128), 128) for part in range(3)]


def attention(qkv16, probs, o16):
    def body(step, carry):
        rows, (qs, ks, vs) = views(step)
        query, key, value = qkv16[rows, qs], qkv16[rows, ks], qkv16[rows, vs]
        total = None
        for half in range(2):
            scores = dot_nt(query, half_of(key, half)) * 0.125
            column = lax.broadcasted_iota(jnp.int32, scores.shape, 1)
            scores = jnp.where(column < SEQ, scores, -jnp.inf)
            raised = jnp.exp(scores - jnp.max(scores, axis=-1, keepdims=True))
            prob = raised / jnp.sum(raised, axis=-1, keepdims=True)
            probs[step * 2 + half] = prob
            term = dot_nn(prob.astype(jnp.bfloat16), half_of(value, half))
            total = term if total is None else total + term
        o16[rows, qs] = total.astype(jnp.bfloat16)
        return carry

    lax.fori_loop(0, qkv16.shape[0] // PAD * 3, body, 0)


def middle(xbuf, o16, w_out, tail, h, xhat2, s2, c16, dybuf, dy16):
    for _, rows in images_of(xbuf):
        value = xbuf[rows, :] + (dot_nn(o16[rows, :], w_out[...]) + tail[4:5, :])
        h[rows, :] = value
        normed, factor = layer_norm(value)
        xhat2[rows, :] = normed
        s2[rows, :] = factor
        c16[rows, :] = (normed * tail[5:6, :] + tail[6:7, :]).astype(jnp.bfloat16)
        dy16[rows, :] = dybuf[rows, :].astype(jnp.bfloat16)


CHUNK = 128


def feed_forward(c16, dy16, w_up, w_down, tail, acc, dc, g_up, g_down, g_tail):
    acc[...] = jnp.zeros_like(acc)
    dc[...] = jnp.zeros_like(dc)
    per = D // CHUNK
    for line in range(4):

        def body(step, carry, line=line):
            at = pl.multiple_of(step * CHUNK, CHUNK)
            where = pl.multiple_of(line * D + step * CHUNK, CHUNK)
            cols = pl.ds(where, CHUNK)
            up = w_up[:, cols]
            down = w_down[cols, :]
            pre = dot_nn(c16[...], up) + tail[8 + line : 9 + line, pl.ds(at, CHUNK)]
            phi = 0.5 * (1.0 + lax.erf(pre * 0.7071067811865476))
            slope = phi + pre * jnp.exp(-0.5 * pre * pre) * 0.3989422804014327
            act = (pre * phi).astype(jnp.bfloat16)
            acc[...] += dot_nn(act, down)
            g_down[cols, :] = dot_tn(act, dy16[...])
            grad_pre = dot_nt(dy16[...], down) * slope
            half = grad_pre.astype(jnp.bfloat16)
            g_up[:, cols] = dot_tn(c16[...], half)
            g_tail[8 + line : 9 + line, pl.ds(at, CHUNK)] = column_sum(grad_pre)
            dc[...] += dot_nt(half, up)
            return carry

        lax.fori_loop(0, per, body, 0)


def feed_forward_end(h, acc, tail, dc, xhat2, s2, dybuf, result, dh, dh16, g_tail):
    sums = [0.0] * 4
    for image, rows in images_of(h):
        value = h[rows, :] + (acc[rows, :] + tail[7:8, :])
        result[:, image, :] = value[:SEQ]
        grad, normed = dc[rows, :], xhat2[rows, :]
        hidden = dybuf[rows, :] + norm_back(grad * tail[5:6, :], normed, s2[rows, :])
        dh[rows, :] = hidden
        dh16[rows, :] = hidden.astype(jnp.bfloat16)
        terms = (hidden, grad * normed, grad, dybuf[rows, :])
        sums = [old + column_sum(new) for old, new in zip(sums, terms)]
    for index in range(4):
        g_tail[4 + index : 5 + index, :] = sums[index]
    g_tail[12:16, :] = jnp.zeros((4, D), jnp.float32)


def attention_out_back(o16, dh16, w_out, g_out, do16):
    g_out[...] = dot_tn(o16[...], dh16[...])
    do16[...] = dot_nt(dh16[...], w_out[...]).astype(jnp.bfloat16)


def attention_back(qkv16, probs, do16, dqkv16, g_tail):
    g_tail[2:4, :] = jnp.zeros((2, D), jnp.float32)

    def body(step, carry):
        rows, (qs, ks, vs) = views(step)
        query, key, value, grad = qkv16[rows, qs], qkv16[rows, ks], qkv16[rows, vs], do16[rows, qs]
        dq = dk = dv = None
        for half in range(2):
            prob = probs[step * 2 + half]
            dv_term = dot_tn(prob.astype(jnp.bfloat16), half_of(grad, half))
            grad_prob = dot_nt(grad, half_of(value, half))
            delta = jnp.sum(prob * grad_prob, axis=-1, keepdims=True)
            ds = (prob * (grad_prob - delta) * 0.125).astype(jnp.bfloat16)
            dq_term = dot_nn(ds, half_of(key, half))
            dk_term = dot_tn(ds, half_of(query, half))
            if half == 0:
                dq, dk, dv = dq_term, dk_term, dv_term
            else:
                dq, dk, dv = dq + dq_term, dk + dk_term, dv + dv_term
        dqkv16[rows, qs] = dq.astype(jnp.bfloat16)
        dqkv16[rows, ks] = dk.astype(jnp.bfloat16)
        dqkv16[rows, vs] = dv.astype(jnp.bfloat16)
        g_tail[2:3, qs] += column_sum(dq)
        g_tail[3:4, qs] += column_sum(dv)
        return carry

    lax.fori_loop(0, qkv16.shape[0] // PAD * 3, body, 0)


def attention_in_back(a16, dqkv16, w_qkv, g_qkv, tail, xhat, s1, dh, grad_tokens, g_tail):
    for piece in range(3):
        cols = slice(piece * D, (piece + 1) * D)
        g_qkv[:, cols] = dot_tn(a16[...], dqkv16[:, cols])
    sums = [0.0] * 2
    for image, rows in images_of(dh):
        grad, normed = dot_nt(dqkv16[rows, :], w_qkv[...]), xhat[rows, :]
        value = dh[rows, :] + norm_back(grad * tail[0:1, :], normed, s1[rows, :])
        grad_tokens[:, image, :] = value[:SEQ]
        sums = [old + column_sum(new) for old, new in zip(sums, (grad * normed, grad))]
    for index in range(2):
        g_tail[index : index + 1, :] = sums[index]


def compute_scratch(images):
    f32, bf16 = jnp.float32, jnp.bfloat16
    rows = images * PAD
    return [
        pltpu.VMEM((rows, D), f32),
        pltpu.VMEM((rows, D), f32),
        pltpu.VMEM((rows, D), f32),
        pltpu.VMEM((rows, D), bf16),
        pltpu.VMEM((rows, 3 * D), bf16),
        pltpu.VMEM((images * HEADS, PAD, PAD), f32),
        pltpu.VMEM((rows, D), bf16),
        pltpu.VMEM((rows, D), f32),
        pltpu.VMEM((rows, D), f32),
        pltpu.VMEM((rows, D), bf16),
        pltpu.VMEM((rows, D), f32),
        pltpu.VMEM((rows, D), f32),
        pltpu.VMEM((rows, D), bf16),
        pltpu.VMEM((rows, D), f32),
        pltpu.VMEM((rows, D), bf16),
        pltpu.VMEM((rows, D), bf16),
        pltpu.VMEM((rows, 3 * D), bf16),
        pltpu.VMEM((rows, 1), f32),
        pltpu.VMEM((rows, 1), f32),
    ]


def compute(tokens, cotangent, weights):
    f32 = jnp.float32
    vmem = pl.BlockSpec(memory_space=pltpu.VMEM)
    return pl.pallas_call(
        compute_kernel,
        out_shape=(
            jax.ShapeDtypeStruct(tokens.shape, f32),
            jax.ShapeDtypeStruct(tokens.shape, f32),
            jax.ShapeDtypeStruct((D, 3 * D), f32),
            jax.ShapeDtypeStruct((D, D), f32),
            jax.ShapeDtypeStruct((D, FF), f32),
            jax.ShapeDtypeStruct((FF, D), f32),
            jax.ShapeDtypeStruct((16, D), f32),
        ),
        in_specs=[vmem] * 7,
        out_specs=[vmem] * 7,
        scratch_shapes=compute_scratch(tokens.shape[1]),
        compiler_params=pltpu.CompilerParams(vmem_limit_bytes=60 * 2**20),
    )(tokens, cotangent, *weights)


def adamw(params, grads, first, second, position):
    first_end = 3 * D * D
    second_end = first_end + D * D
    third_end = second_end + D * FF
    fourth_end = third_end + FF * D
    rate = jnp.where(
        position < first_end,
        0.01,
        jnp.where(
            position < second_end,
            0.1,
            jnp.where(position < third_end, 0.01, jnp.where(position < fourth_end, 0.005, 0.1)),
        ),
    )
    first_new = 0.9 * first + 0.1 * grads
    second_new = 0.999 * second + 0.001 * grads * grads
    update = (
        first_new / (1.0 - 0.9**STEP) / (jnp.sqrt(second_new / (1.0 - 0.999**STEP)) + 1e-08)
        + 0.1 * params
    )
    return (params - rate * update, first_new, second_new)


def per_device(tokens, params, moment1, moment2, cotangent):
    devices = lax.axis_size("dp")
    length = params.shape[0]
    w_qkv, w_out, w_up, w_down, tail = gather_weights(params, devices)
    weights = (w_qkv, w_out, w_up, w_down, tail)
    result, grad_tokens, *grads = compute(
        tokens.transpose(1, 0, 2), cotangent.transpose(1, 0, 2), weights
    )
    result, grad_tokens = result.transpose(1, 0, 2), grad_tokens.transpose(1, 0, 2)
    shares = scatter_grads(grads, devices, length)
    count = tokens.shape[0] * tokens.shape[1] * devices
    grad_params = shares * (1.0 / math.sqrt(count))
    position = lax.axis_index("dp") * length + jnp.arange(length, dtype=jnp.int32)
    new_params, new_first, new_second = adamw(params, grad_params, moment1, moment2, position)
    return (result, grad_tokens, grad_params, new_params, new_first, new_second)


def solution(mesh):
    in_specs = (P("dp", None, None), P("dp"), P("dp"), P("dp"), P("dp", None, None))
    out_specs = (P("dp", None, None), P("dp", None, None), P("dp"), P("dp"), P("dp"), P("dp"))
    return jax.shard_map(
        per_device, mesh=mesh, in_specs=in_specs, out_specs=out_specs, check_vma=False
    )
```

```python
import math

import jax
import jax.numpy as jnp
from jax import lax
from jax.experimental import pallas as pl
from jax.experimental.pallas import tpu as pltpu
import functools
from jax.sharding import PartitionSpec as P

D = 384
HEADS = 6
FF = 1536
SEQ = 197
STEP = 3


LANES = 128
LINES = 4 * 1152 + 12


def other(device, bit):
    step = 2**bit
    return device + step - 2 * step * ((device // step) % 2)


def flip(device, column):
    bit = 3
    while column:
        if column % 2:
            device = other(device, bit)
        column //= 2
        bit += 1
    return device


def slot_of(device, devices):
    return (device % 2) * (devices // 2) + device // 2


def partners_of(me, devices):
    return [other(me, bit) for bit in range(3)] + [flip(me, j) for j in range(1, devices // 8)]


def greet_partners(me, devices):
    for partner in partners_of(me, devices):
        pl.semaphore_signal(
            pltpu.get_barrier_semaphore(),
            inc=1,
            device_id=(partner,),
            device_id_type=pl.DeviceIdType.MESH,
        )


def wait_partners(devices):
    pl.semaphore_wait(pltpu.get_barrier_semaphore(), 2 + devices // 8)


def columns_of(devices):
    order = list(range(devices // 8))
    return [0, 1, 3, 2] if devices == 32 else order


def row_plan(share):
    rows = -(-(share + D - 1) // D)
    rows = -(-rows // 32) * 32
    return rows, rows // 2


COLUMN, ALONG_X, ALONG_Y, TURN_X, TURN_Y, CORE = range(6)


def greet(me, bits):
    barrier = pltpu.get_barrier_semaphore()
    for bit in range(bits):
        pl.semaphore_signal(
            barrier, inc=1, device_id=(other(me, bit),), device_id_type=pl.DeviceIdType.MESH
        )
    pl.semaphore_wait(barrier, bits)


def gather_kernel(devices, share, shard, w_qkv, w_out, w_up, w_down, tail, lines, slots, send_sem, recv_sem):
    rows, half = row_plan(share)
    count = devices // 8
    me = lax.axis_index("dp")
    core, x_side, y_side = other(me, 0), other(me, 1), other(me, 2)
    whole, upper, lower = (0, rows), (0, half), (half, half)
    mine = slots.at[slot_of(me, devices)]
    copies = {}

    def copy(kind, column, source, target, device):
        made = pltpu.make_async_remote_copy(
            src_ref=source,
            dst_ref=target,
            send_sem=send_sem.at[kind * count + column],
            recv_sem=recv_sem.at[kind * count + column],
            device_id=(device,),
            device_id_type=pl.DeviceIdType.MESH,
        )
        made.start()
        copies[kind, column] = made

    def send(kind, column, owner, part, device):
        piece = slots.at[slot_of(owner, devices), pl.ds(part[0], part[1])]
        copy(kind, column, piece, piece, device)

    def along(column):
        copies[COLUMN, column].wait_recv()
        send(ALONG_X, column, flip(me, column), whole, x_side)
        send(ALONG_Y, column, flip(me, column), whole, y_side)

    def turn(column):
        copies[ALONG_X, column].wait_recv()
        send(TURN_Y, column, other(flip(me, column), 1), upper, y_side)
        copies[ALONG_Y, column].wait_recv()
        send(TURN_X, column, other(flip(me, column), 2), lower, x_side)

    def across(column):
        copies[TURN_Y, column].wait_recv()
        copies[TURN_X, column].wait_recv()
        first = (me % 2) * (devices // 2) + (flip(me, column) // 8) * 4
        layer = slots.at[pl.ds(first, 4)]
        copy(CORE, column, layer, layer, core)

    greet_partners(me, devices)
    wait_partners(devices)
    order = columns_of(devices)
    for index, column in enumerate(order[1:]):
        copy(COLUMN, column, shard, mine, flip(me, column))
        if index == 0:
            copy(ALONG_X, 0, shard, mine, x_side)
            copy(ALONG_Y, 0, shard, mine, y_side)
    mine[...] = shard[...]
    for index in range(len(order) + 2):
        if 1 <= index < len(order):
            along(order[index])
        if 0 <= index - 1 < len(order):
            turn(order[index - 1])
        if 0 <= index - 2 < len(order):
            across(order[index - 2])
    for (kind, column), made in copies.items():
        made.wait_send()
        if kind == CORE:
            made.wait_recv()
    chunks = D // LANES
    for device in range(devices):
        at = device * share // D
        shared = device * share % D != 0
        spot = slot_of(device, devices)
        for chunk in range(chunks):
            if shared:
                before = lines[chunk, at : at + 1, :]
            lines[chunk, at : at + rows, :] = slots[
                spot, :, chunk * LANES : (chunk + 1) * LANES
            ].astype(jnp.float32)
            if shared:
                lines[chunk, at : at + 1, :] = lines[chunk, at : at + 1, :] + before
    spread(lines, 0, w_qkv, 3)
    spread(lines, 1152, w_out, 1)
    spread(lines, 1536, w_up, 4)
    spread(lines, 3072, w_down, 1)
    spread(lines, 4608, tail, 1)


def spread(lines, first, out, times):
    height = out.shape[0]
    for column in range(times):
        for chunk in range(D // LANES):
            if times == 1:
                value = lines[chunk, first : first + height, :]
            else:
                value = lines[chunk, pl.ds(first + column, height, stride=times), :]
            at = column * D + chunk * LANES
            out[:, at : at + LANES] = value.astype(out.dtype)


def gather_weights(params, devices):
    share = params.shape[0]
    rows, _ = row_plan(share)
    offset = (lax.axis_index("dp") * share) % D
    flat = jnp.zeros((rows * D,), jnp.float32)
    flat = lax.dynamic_update_slice(flat, params, (offset,))
    shard = flat.reshape(rows, D).astype(jnp.bfloat16)
    vmem = pl.BlockSpec(memory_space=pltpu.VMEM)
    return pl.pallas_call(
        functools.partial(gather_kernel, devices, share),
        out_shape=(
            jax.ShapeDtypeStruct((D, 3 * D), jnp.bfloat16),
            jax.ShapeDtypeStruct((D, D), jnp.bfloat16),
            jax.ShapeDtypeStruct((D, FF), jnp.bfloat16),
            jax.ShapeDtypeStruct((FF, D), jnp.bfloat16),
            jax.ShapeDtypeStruct((16, D), jnp.float32),
        ),
        in_specs=[vmem],
        out_specs=[vmem] * 5,
        scratch_shapes=[
            pltpu.VMEM((D // LANES, LINES + rows + 24, LANES), jnp.float32),
            pltpu.VMEM((devices, rows, D), jnp.bfloat16),
            pltpu.SemaphoreType.DMA((6 * (devices // 8),)),
            pltpu.SemaphoreType.DMA((6 * (devices // 8),)),
        ],
        compiler_params=pltpu.CompilerParams(
            collective_id=0, has_side_effects=True, vmem_limit_bytes=60 * 2**20
        ),
    )(shard)


PAD = 208


def dot_nn(left, right):
    return lax.dot_general(left, right, (((1,), (0,)), ((), ())), preferred_element_type=jnp.float32)


def dot_nt(left, right):
    return lax.dot_general(left, right, (((1,), (1,)), ((), ())), preferred_element_type=jnp.float32)


def dot_tn(left, right):
    return lax.dot_general(left, right, (((0,), (0,)), ((), ())), preferred_element_type=jnp.float32)


def layer_norm(values):
    center = values - jnp.mean(values, axis=-1, keepdims=True)
    factor = lax.rsqrt(jnp.mean(center * center, axis=-1, keepdims=True) + 1e-06)
    return center * factor, factor


def norm_back(grad_hat, normed, factor):
    return factor * (
        grad_hat
        - jnp.mean(grad_hat, axis=-1, keepdims=True)
        - normed * jnp.mean(grad_hat * normed, axis=-1, keepdims=True)
    )


def column_sum(values):
    return jnp.sum(values, axis=0, keepdims=True)


def images_of(padded):
    return [(image, slice(image * PAD, (image + 1) * PAD)) for image in range(padded.shape[0] // PAD)]


TAIL = 4608
HOPS = 7
TO_CORE, TURN_UP, TURN_LOW, TO_X, TO_Y, TO_LAYER, TAIL_OUT = range(HOPS)


def units_of(devices, share):
    early, late = [], []
    for layer in range(devices // 8 - 1, -1, -1):
        if layer * 8 * share // D >= 3 * D:
            early.append((layer, (0, 1, 2), False))
        else:
            late.extend((layer, (chunk,), layer == 0 and chunk == 2) for chunk in range(3))
    late.sort(key=lambda unit: unit[1])
    return early, late


def unit_scratch(devices, share):
    rows, half = row_plan(share)
    early, late = units_of(devices, share)
    shapes = []
    for _, chunks, tail in early + late:
        wide = len(chunks) * LANES
        tall = rows + (48 if tail else 0)
        shapes += [(4, tall, wide)] * 2
        shapes += [(half, wide), (tall - half, wide)] * 2
        shapes += [(tall, wide)] * 5
    return [pltpu.VMEM(shape, jnp.bfloat16) for shape in shapes]


class Unit:
    def __init__(self, index, plan, devices, share, refs, shared):
        self.index, self.devices, self.share = index, devices, share
        self.layer, self.chunks, self.tail = plan
        (
            self.core_out, self.core_in, self.up_out, self.low_out, self.up_in, self.low_in,
            self.x_out, self.y_out, self.x_in, self.y_in, self.z_out,
        ) = refs
        (
            self.lines, self.g_tail, self.total, self.tail_total, self.z_in, self.tail_in,
            self.send_sem, self.recv_sem, self.z_sem, self.tail_sem,
        ) = shared
        self.rows, self.half = row_plan(share)
        self.stage = 0
        self.copies = {}
        me = lax.axis_index("dp")
        self.me = me
        self.z = me // 8
        self.core, self.x_side, self.y_side = other(me, 0), other(me, 1), other(me, 2)

    def copy(self, kind, source, target, device, recv=None):
        made = pltpu.make_async_remote_copy(
            src_ref=source,
            dst_ref=target,
            send_sem=self.send_sem.at[self.index, kind],
            recv_sem=self.recv_sem.at[self.index, kind] if recv is None else recv,
            device_id=(device,),
            device_id_type=pl.DeviceIdType.MESH,
        )
        return made

    def send(self, kind, source, target, device):
        self.copies[kind] = self.copy(kind, source, target, device)
        self.copies[kind].start()

    def advance(self):
        (self.pack, self.turn, self.along, self.arrive)[self.stage]()
        self.stage += 1

    def block(self, owner, spot, begin, end, index):
        first = owner * self.share // D
        chunk = self.chunks[index]
        lanes = slice(index * LANES, (index + 1) * LANES)
        value = self.lines[chunk, pl.ds(first + begin, end - begin), :]
        if spot is not None:
            value = value + self.core_in[spot, begin:end, lanes].astype(jnp.float32)
        return value

    def tail_block(self, spot, index):
        value = self.g_tail[:, index * LANES : (index + 1) * LANES]
        if spot is not None:
            at = self.rows + 16 * index
            value = value + self.core_in[spot, at : at + 16, :].astype(jnp.float32)
        return value

    def owner(self, spot, core):
        return self.layer * 8 + spot * 2 + core

    def pack(self):
        core = self.me % 2
        for spot in range(4):
            for index in range(len(self.chunks)):
                lanes = slice(index * LANES, (index + 1) * LANES)
                value = self.block(self.owner(spot, 1 - core), None, 0, self.rows, index)
                self.core_out[spot, : self.rows, lanes] = value.astype(jnp.bfloat16)
            if self.tail:
                for index in range(3):
                    at = self.rows + 16 * index
                    self.core_out[spot, at : at + 16, :] = self.tail_block(None, index).astype(
                        jnp.bfloat16
                    )
        self.send(TO_CORE, self.core_out, self.core_in, self.core)

    def spot_of(self, device):
        return device // 2 % 4

    def turn(self):
        self.copies[TO_CORE].wait_recv()
        spot = self.spot_of(other(self.x_side, 2))
        owner = self.owner(spot, self.me % 2)
        half, rows = self.half, self.rows
        for index in range(len(self.chunks)):
            lanes = slice(index * LANES, (index + 1) * LANES)
            self.up_out[:, lanes] = self.block(owner, spot, 0, half, index).astype(jnp.bfloat16)
            self.low_out[: rows - half, lanes] = self.block(
                owner, spot, half, rows, index
            ).astype(jnp.bfloat16)
        if self.tail:
            for index in range(3):
                at = rows - half + 16 * index
                self.low_out[at : at + 16, :] = self.tail_block(spot, index).astype(jnp.bfloat16)
        self.send(TURN_UP, self.up_out, self.up_in, self.y_side)
        self.send(TURN_LOW, self.low_out, self.low_in, self.x_side)

    def along(self):
        half, rows = self.half, self.rows
        for kind, device, out, into in (
            (TURN_UP, self.x_side, self.x_out, self.x_in),
            (TURN_LOW, self.y_side, self.y_out, self.y_in),
        ):
            self.copies[kind].wait_recv()
            spot = self.spot_of(device)
            owner = self.owner(spot, self.me % 2)
            for index in range(len(self.chunks)):
                lanes = slice(index * LANES, (index + 1) * LANES)
                upper = self.block(owner, spot, 0, half, index)
                lower = self.block(owner, spot, half, rows, index)
                if kind == TURN_UP:
                    upper = upper + self.up_in[:, lanes].astype(jnp.float32)
                else:
                    lower = lower + self.low_in[: rows - half, lanes].astype(jnp.float32)
                out[:half, lanes] = upper.astype(jnp.bfloat16)
                out[half:rows, lanes] = lower.astype(jnp.bfloat16)
            if self.tail:
                for index in range(3):
                    at = rows + 16 * index
                    value = self.tail_block(spot, index)
                    if kind == TURN_LOW:
                        value = value + self.low_in[at - half : at - half + 16, :].astype(
                            jnp.float32
                        )
                    out[at : at + 16, :] = value.astype(jnp.bfloat16)
            self.send(TO_X if kind == TURN_UP else TO_Y, out, into, device)

    def away(self, source):
        first, last = self.chunks[0] * LANES, (self.chunks[-1] + 1) * LANES
        return self.copy(
            TO_LAYER,
            self.z_out.at[pl.ds(0, self.rows)],
            self.z_in.at[source, :, pl.ds(first, last - first)],
            self.layer * 8 + self.me % 8,
            self.z_sem.at[self.index, source],
        )

    def tail_away(self, source):
        return self.copy(
            TAIL_OUT,
            self.z_out.at[pl.ds(self.rows, 48)],
            self.tail_in.at[source],
            self.devices - 8 + self.me % 8,
            self.tail_sem.at[source],
        )

    def arrive(self):
        self.copies[TO_X].wait_recv()
        self.copies[TO_Y].wait_recv()
        spot = self.spot_of(self.me)
        owner = self.owner(spot, self.me % 2)
        rows = self.rows
        for index, chunk in enumerate(self.chunks):
            lanes = slice(index * LANES, (index + 1) * LANES)
            value = self.block(owner, spot, 0, rows, index)
            value = value + self.x_in[:rows, lanes].astype(jnp.float32)
            value = value + self.y_in[:rows, lanes].astype(jnp.float32)
            self.z_out[:rows, lanes] = value.astype(jnp.bfloat16)

            @pl.when(self.z == self.layer)
            def _(value=value, chunk=chunk):
                self.total[:, chunk * LANES : (chunk + 1) * LANES] = value

        @pl.when(self.z != self.layer)
        def _():
            self.away(self.z).start()

        if self.tail:
            last = self.devices // 8 - 1
            for index in range(3):
                at = rows + 16 * index
                value = self.tail_block(spot, index)
                value = value + self.x_in[at : at + 16, :].astype(jnp.float32)
                value = value + self.y_in[at : at + 16, :].astype(jnp.float32)
                self.z_out[at : at + 16, :] = value.astype(jnp.bfloat16)
                self.tail_total[:, index * LANES : (index + 1) * LANES] = value

            @pl.when(self.z != last)
            def _():
                self.tail_away(self.z).start()

    def finish(self):
        last = self.devices // 8 - 1
        for made in self.copies.values():
            made.wait_send()

        @pl.when(self.z != self.layer)
        def _():
            self.away(self.z).wait_send()

        first, end = self.chunks[0] * LANES, (self.chunks[-1] + 1) * LANES
        for source in range(last + 1):
            if source != self.layer:

                @pl.when(self.z == self.layer)
                def _(source=source):
                    self.away(source).wait_recv()
                    self.total[:, first:end] += self.z_in[source, :, first:end].astype(jnp.float32)

        if self.tail:

            @pl.when(self.z != last)
            def _():
                self.tail_away(self.z).wait_send()

            for source in range(last):

                @pl.when(self.z == last)
                def _(source=source):
                    self.tail_away(source).wait_recv()
                    for index in range(3):
                        self.tail_total[:, index * LANES : (index + 1) * LANES] += self.tail_in[
                            source, 16 * index : 16 * index + 16, :
                        ].astype(jnp.float32)


def step_kernel(
    devices, share, tokens, cot, w_qkv, w_out, w_up, w_down, tail, result, grad_tokens, out,
    xbuf, dybuf, xhat, a16, qkv16, probs, o16, h, xhat2, c16, acc, dc, dy16, dh, dh16, do16, dqkv16,
    s1, s2, lines, g_tail, total, tail_total, z_in, tail_in, send_sem, recv_sem, z_sem, tail_sem, *refs,
):
    me = lax.axis_index("dp")
    greet_partners(me, devices)
    early, late = units_of(devices, share)
    shared = (
        lines, g_tail, total, tail_total, z_in, tail_in, send_sem, recv_sem, z_sem, tail_sem,
    )
    units = [
        Unit(index, plan, devices, share, refs[index * 11 : index * 11 + 11], shared)
        for index, plan in enumerate(early + late)
    ]
    count = len(early)
    early, late = units[:count], units[count:]
    behind = [unit for unit in early if unit.layer * 8 * share // D >= 4 * D]
    mixed = [unit for unit in early if unit not in behind]

    load(tokens, xbuf)
    load(cot, dybuf)
    lines[:, TAIL:, :] = jnp.zeros_like(lines[:, TAIL:, :])
    attention_in(xbuf, tail, xhat, s1, a16, w_qkv, qkv16)
    attention(qkv16, probs, o16)
    middle(xbuf, o16, w_out, tail, h, xhat2, s2, c16, dybuf, dy16)
    feed_forward(c16, dy16, w_up, w_down, tail, acc, dc, lines, g_tail)
    wait_partners(devices)
    advance(behind)
    feed_forward_end(h, acc, tail, dc, xhat2, s2, dybuf, result, dh, dh16, g_tail)
    advance(behind)
    attention_out_back(o16, dh16, w_out, lines, do16)
    advance(mixed)
    g_tail[2:4, :] = jnp.zeros((2, D), jnp.float32)
    for pair in range(3):
        attention_back(pair, qkv16, probs, do16, dqkv16, g_tail)
        if pair == 0:
            advance(behind)
            advance(mixed)
        if pair == 1:
            advance(behind)
            advance(mixed)
            advance([unit for unit in late if unit.chunks[0] == 0])
        if pair == 2:
            advance(mixed)
            advance([unit for unit in late if unit.chunks[0] < 2])
        attention_in_back(pair, a16, dqkv16, w_qkv, lines, acc)
        if pair < 2:
            advance([unit for unit in late if unit.chunks[0] == pair])
    input_sums(acc, xhat, g_tail)
    advance([unit for unit in late if unit.chunks[0] == 2])
    grad_input(acc, tail, xhat, s1, dh, grad_tokens)
    while any(unit.stage < 4 for unit in late):
        advance([unit for unit in late if unit.stage < 4])
    for unit in units:
        unit.finish()
    at = TAIL - (devices - 1) * share // D
    out[...] = total[...]

    @pl.when(me == devices - 1)
    def _():
        out[at : at + 12, :] = total[at : at + 12, :] + tail_total[0:12, :]


def advance(units):
    for unit in units:
        unit.advance()


def load(source, padded):
    for image in range(source.shape[1]):
        at = image * PAD
        padded[at + PAD - 16 : at + PAD, :] = jnp.zeros((16, D), jnp.float32)
        padded[at : at + SEQ, :] = source[:, image, :]


def attention_in(xbuf, tail, xhat, s1, a16, w_qkv, qkv16):
    for _, rows in images_of(xbuf):
        normed, factor = layer_norm(xbuf[rows, :])
        xhat[rows, :] = normed
        s1[rows, :] = factor
        a16[rows, :] = (normed * tail[0:1, :] + tail[1:2, :]).astype(jnp.bfloat16)
    for piece in range(3):
        cols = slice(piece * D, (piece + 1) * D)
        value = dot_nn(a16[...], w_qkv[:, cols])
        if piece == 0:
            value = value + tail[2:3, :]
        if piece == 2:
            value = value + tail[3:4, :]
        qkv16[:, cols] = value.astype(jnp.bfloat16)


def half_of(values, half):
    lane = lax.broadcasted_iota(jnp.int32, values.shape, 1)
    return jnp.where((lane < 64) if half == 0 else (lane >= 64), values, jnp.zeros_like(values))


def views(step):
    image, pair = step // 3, step % 3
    rows = pl.ds(pl.multiple_of(image * PAD, 16), PAD)
    return rows, [pl.ds(pl.multiple_of(part * D + pair * 128, 128), 128) for part in range(3)]


def attention(qkv16, probs, o16):
    def body(step, carry):
        rows, (qs, ks, vs) = views(step)
        query, key, value = qkv16[rows, qs], qkv16[rows, ks], qkv16[rows, vs]
        total = None
        for half in range(2):
            scores = dot_nt(query, half_of(key, half)) * 0.125
            column = lax.broadcasted_iota(jnp.int32, scores.shape, 1)
            scores = jnp.where(column < SEQ, scores, -jnp.inf)
            raised = jnp.exp(scores - jnp.max(scores, axis=-1, keepdims=True))
            prob = raised / jnp.sum(raised, axis=-1, keepdims=True)
            probs[step * 2 + half] = prob
            term = dot_nn(prob.astype(jnp.bfloat16), half_of(value, half))
            total = term if total is None else total + term
        o16[rows, qs] = total.astype(jnp.bfloat16)
        return carry

    lax.fori_loop(0, qkv16.shape[0] // PAD * 3, body, 0)


def middle(xbuf, o16, w_out, tail, h, xhat2, s2, c16, dybuf, dy16):
    for _, rows in images_of(xbuf):
        value = xbuf[rows, :] + (dot_nn(o16[rows, :], w_out[...]) + tail[4:5, :])
        h[rows, :] = value
        normed, factor = layer_norm(value)
        xhat2[rows, :] = normed
        s2[rows, :] = factor
        c16[rows, :] = (normed * tail[5:6, :] + tail[6:7, :]).astype(jnp.bfloat16)
        dy16[rows, :] = dybuf[rows, :].astype(jnp.bfloat16)


CHUNK = 128


def feed_forward(c16, dy16, w_up, w_down, tail, acc, dc, lines, g_tail):
    acc[...] = jnp.zeros_like(acc)
    dc[...] = jnp.zeros_like(dc)
    per = D // CHUNK
    for line in range(4):

        def body(step, carry, line=line):
            at = pl.multiple_of(step * CHUNK, CHUNK)
            where = pl.multiple_of(line * D + step * CHUNK, CHUNK)
            cols = pl.ds(where, CHUNK)
            up = w_up[:, cols]
            down = w_down[cols, :]
            pre = dot_nn(c16[...], up) + tail[8 + line : 9 + line, pl.ds(at, CHUNK)]
            phi = 0.5 * (1.0 + lax.erf(pre * 0.7071067811865476))
            slope = phi + pre * jnp.exp(-0.5 * pre * pre) * 0.3989422804014327
            act = (pre * phi).astype(jnp.bfloat16)
            acc[...] += dot_nn(act, down)
            grad_down = dot_tn(act, dy16[...])
            for chunk in range(D // LANES):
                lines[chunk, pl.ds(8 * D + where, CHUNK), :] = grad_down[
                    :, chunk * LANES : (chunk + 1) * LANES
                ]
            grad_pre = dot_nt(dy16[...], down) * slope
            half = grad_pre.astype(jnp.bfloat16)
            lines[step, pl.ds(4 * D + line, D, stride=4), :] = dot_tn(c16[...], half)
            g_tail[8 + line : 9 + line, pl.ds(at, CHUNK)] = column_sum(grad_pre)
            dc[...] += dot_nt(half, up)
            return carry

        lax.fori_loop(0, per, body, 0)


def feed_forward_end(h, acc, tail, dc, xhat2, s2, dybuf, result, dh, dh16, g_tail):
    sums = [0.0] * 4
    for image, rows in images_of(h):
        value = h[rows, :] + (acc[rows, :] + tail[7:8, :])
        result[:, image, :] = value[:SEQ]
        grad, normed = dc[rows, :], xhat2[rows, :]
        hidden = dybuf[rows, :] + norm_back(grad * tail[5:6, :], normed, s2[rows, :])
        dh[rows, :] = hidden
        dh16[rows, :] = hidden.astype(jnp.bfloat16)
        terms = (hidden, grad * normed, grad, dybuf[rows, :])
        sums = [old + column_sum(new) for old, new in zip(sums, terms)]
    for index in range(4):
        g_tail[4 + index : 5 + index, :] = sums[index]
    g_tail[12:16, :] = jnp.zeros((4, D), jnp.float32)


def attention_out_back(o16, dh16, w_out, lines, do16):
    grad_out = dot_tn(o16[...], dh16[...])
    for chunk in range(D // LANES):
        lines[chunk, 3 * D : 4 * D, :] = grad_out[:, chunk * LANES : (chunk + 1) * LANES]
    do16[...] = dot_nt(dh16[...], w_out[...]).astype(jnp.bfloat16)


def attention_back(pair, qkv16, probs, do16, dqkv16, g_tail):
    def body(image, carry):
        step = image * 3 + pair
        rows, (qs, ks, vs) = views(step)
        query, key, value, grad = qkv16[rows, qs], qkv16[rows, ks], qkv16[rows, vs], do16[rows, qs]
        dq = dk = dv = None
        for half in range(2):
            prob = probs[step * 2 + half]
            dv_term = dot_tn(prob.astype(jnp.bfloat16), half_of(grad, half))
            grad_prob = dot_nt(grad, half_of(value, half))
            delta = jnp.sum(prob * grad_prob, axis=-1, keepdims=True)
            ds = (prob * (grad_prob - delta) * 0.125).astype(jnp.bfloat16)
            dq_term = dot_nn(ds, half_of(key, half))
            dk_term = dot_tn(ds, half_of(query, half))
            if half == 0:
                dq, dk, dv = dq_term, dk_term, dv_term
            else:
                dq, dk, dv = dq + dq_term, dk + dk_term, dv + dv_term
        dqkv16[rows, qs] = dq.astype(jnp.bfloat16)
        dqkv16[rows, ks] = dk.astype(jnp.bfloat16)
        dqkv16[rows, vs] = dv.astype(jnp.bfloat16)
        g_tail[2:3, qs] += column_sum(dq)
        g_tail[3:4, qs] += column_sum(dv)
        return carry

    lax.fori_loop(0, qkv16.shape[0] // PAD, body, 0)


def attention_in_back(pair, a16, dqkv16, w_qkv, lines, acc):
    parts = [slice(part * D + pair * LANES, part * D + (pair + 1) * LANES) for part in range(3)]
    grads = jnp.concatenate([dqkv16[:, part] for part in parts], axis=1)
    weights = jnp.concatenate([w_qkv[:, part] for part in parts], axis=1)
    grad_w = dot_tn(a16[...], grads)
    for part in range(3):
        lines[pair, pl.ds(part, D, stride=3), :] = grad_w[:, part * LANES : (part + 1) * LANES]
    value = dot_nt(grads, weights)
    acc[...] = value if pair == 0 else acc[...] + value


def input_sums(acc, xhat, g_tail):
    sums = [0.0] * 2
    for _, rows in images_of(acc):
        grad = acc[rows, :]
        sums = [old + column_sum(new) for old, new in zip(sums, (grad * xhat[rows, :], grad))]
    for index in range(2):
        g_tail[index : index + 1, :] = sums[index]


def grad_input(acc, tail, xhat, s1, dh, grad_tokens):
    for image, rows in images_of(acc):
        value = dh[rows, :] + norm_back(acc[rows, :] * tail[0:1, :], xhat[rows, :], s1[rows, :])
        grad_tokens[:, image, :] = value[:SEQ]


def compute_scratch(images):
    f32, bf16 = jnp.float32, jnp.bfloat16
    rows = images * PAD
    return [
        pltpu.VMEM((rows, D), f32),
        pltpu.VMEM((rows, D), f32),
        pltpu.VMEM((rows, D), f32),
        pltpu.VMEM((rows, D), bf16),
        pltpu.VMEM((rows, 3 * D), bf16),
        pltpu.VMEM((images * HEADS, PAD, PAD), f32),
        pltpu.VMEM((rows, D), bf16),
        pltpu.VMEM((rows, D), f32),
        pltpu.VMEM((rows, D), f32),
        pltpu.VMEM((rows, D), bf16),
        pltpu.VMEM((rows, D), f32),
        pltpu.VMEM((rows, D), f32),
        pltpu.VMEM((rows, D), bf16),
        pltpu.VMEM((rows, D), f32),
        pltpu.VMEM((rows, D), bf16),
        pltpu.VMEM((rows, D), bf16),
        pltpu.VMEM((rows, 3 * D), bf16),
        pltpu.VMEM((rows, 1), f32),
        pltpu.VMEM((rows, 1), f32),
    ]


def compute(tokens, cotangent, weights, devices, share):
    f32 = jnp.float32
    rows, _ = row_plan(share)
    layers = devices // 8
    early, late = units_of(devices, share)
    count = len(early) + len(late)
    vmem = pl.BlockSpec(memory_space=pltpu.VMEM)
    result, grad_tokens, total = pl.pallas_call(
        functools.partial(step_kernel, devices, share),
        out_shape=(
            jax.ShapeDtypeStruct(tokens.shape, f32),
            jax.ShapeDtypeStruct(tokens.shape, f32),
            jax.ShapeDtypeStruct((rows, D), f32),
        ),
        in_specs=[vmem] * 7,
        out_specs=[vmem] * 3,
        scratch_shapes=compute_scratch(tokens.shape[1])
        + [
            pltpu.VMEM((D // LANES, LINES + rows + 24, LANES), f32),
            pltpu.VMEM((16, D), f32),
            pltpu.VMEM((rows, D), f32),
            pltpu.VMEM((16, D), f32),
            pltpu.VMEM((layers, rows, D), jnp.bfloat16),
            pltpu.VMEM((layers, 48, LANES), jnp.bfloat16),
            pltpu.SemaphoreType.DMA((count, HOPS)),
            pltpu.SemaphoreType.DMA((count, HOPS)),
            pltpu.SemaphoreType.DMA((count, layers)),
            pltpu.SemaphoreType.DMA((layers,)),
        ]
        + unit_scratch(devices, share),
        compiler_params=pltpu.CompilerParams(
            collective_id=1, has_side_effects=True, vmem_limit_bytes=60 * 2**20
        ),
    )(tokens, cotangent, *weights)
    offset = (lax.axis_index("dp") * share) % D
    return result, grad_tokens, lax.dynamic_slice(total.reshape(-1), (offset,), (share,))


def adamw(params, grads, first, second, position):
    first_end = 3 * D * D
    second_end = first_end + D * D
    third_end = second_end + D * FF
    fourth_end = third_end + FF * D
    rate = jnp.where(
        position < first_end,
        0.01,
        jnp.where(
            position < second_end,
            0.1,
            jnp.where(position < third_end, 0.01, jnp.where(position < fourth_end, 0.005, 0.1)),
        ),
    )
    first_new = 0.9 * first + 0.1 * grads
    second_new = 0.999 * second + 0.001 * grads * grads
    update = (
        first_new / (1.0 - 0.9**STEP) / (jnp.sqrt(second_new / (1.0 - 0.999**STEP)) + 1e-08)
        + 0.1 * params
    )
    return (params - rate * update, first_new, second_new)


def per_device(tokens, params, moment1, moment2, cotangent):
    devices = lax.axis_size("dp")
    length = params.shape[0]
    w_qkv, w_out, w_up, w_down, tail = gather_weights(params, devices)
    weights = (w_qkv, w_out, w_up, w_down, tail)
    result, grad_tokens, shares = compute(
        tokens.transpose(1, 0, 2), cotangent.transpose(1, 0, 2), weights, devices, length
    )
    result, grad_tokens = result.transpose(1, 0, 2), grad_tokens.transpose(1, 0, 2)
    count = tokens.shape[0] * tokens.shape[1] * devices
    grad_params = shares * (1.0 / math.sqrt(count))
    position = lax.axis_index("dp") * length + jnp.arange(length, dtype=jnp.int32)
    new_params, new_first, new_second = adamw(params, grad_params, moment1, moment2, position)
    return (result, grad_tokens, grad_params, new_params, new_first, new_second)


def solution(mesh):
    in_specs = (P("dp", None, None), P("dp"), P("dp"), P("dp"), P("dp", None, None))
    out_specs = (P("dp", None, None), P("dp", None, None), P("dp"), P("dp"), P("dp"), P("dp"))
    return jax.shard_map(
        per_device, mesh=mesh, in_specs=in_specs, out_specs=out_specs, check_vma=False
    )
```

```python
import math

import jax
import jax.numpy as jnp
from jax import lax
from jax.experimental import pallas as pl
from jax.experimental.pallas import tpu as pltpu
import functools
from jax.sharding import PartitionSpec as P

D = 384
HEADS = 6
FF = 1536
SEQ = 197
STEP = 3


LANES = 128
LINES = 4 * 1152 + 12


def other(device, bit):
    step = 2**bit
    return device + step - 2 * step * ((device // step) % 2)


def flip(device, column):
    bit = 3
    while column:
        if column % 2:
            device = other(device, bit)
        column //= 2
        bit += 1
    return device


def slot_of(device, devices):
    return (device % 2) * (devices // 2) + device // 2


def partners_of(me, devices):
    return [other(me, bit) for bit in range(3)] + [flip(me, j) for j in range(1, devices // 8)]


def greet_partners(me, devices):
    for partner in partners_of(me, devices):
        pl.semaphore_signal(
            pltpu.get_barrier_semaphore(),
            inc=1,
            device_id=(partner,),
            device_id_type=pl.DeviceIdType.MESH,
        )


def wait_partners(devices):
    pl.semaphore_wait(pltpu.get_barrier_semaphore(), 2 + devices // 8)


def columns_of(devices):
    order = list(range(devices // 8))
    return [0, 1, 3, 2] if devices == 32 else order


def row_plan(share):
    rows = -(-(share + D - 1) // D)
    rows = -(-rows // 32) * 32
    return rows, rows // 2


COLUMN, ALONG_X, ALONG_Y, TURN_X, TURN_Y, CORE = range(6)


def greet(me, bits):
    barrier = pltpu.get_barrier_semaphore()
    for bit in range(bits):
        pl.semaphore_signal(
            barrier, inc=1, device_id=(other(me, bit),), device_id_type=pl.DeviceIdType.MESH
        )
    pl.semaphore_wait(barrier, bits)


def gather_kernel(devices, share, shard, w_qkv, w_out, w_up, w_down, tail, lines, slots, send_sem, recv_sem):
    rows, half = row_plan(share)
    count = devices // 8
    me = lax.axis_index("dp")
    core, x_side, y_side = other(me, 0), other(me, 1), other(me, 2)
    whole, upper, lower = (0, rows), (0, half), (half, half)
    mine = slots.at[slot_of(me, devices)]
    copies = {}

    def copy(kind, column, source, target, device):
        made = pltpu.make_async_remote_copy(
            src_ref=source,
            dst_ref=target,
            send_sem=send_sem.at[kind * count + column],
            recv_sem=recv_sem.at[kind * count + column],
            device_id=(device,),
            device_id_type=pl.DeviceIdType.MESH,
        )
        made.start()
        copies[kind, column] = made

    def send(kind, column, owner, part, device):
        piece = slots.at[slot_of(owner, devices), pl.ds(part[0], part[1])]
        copy(kind, column, piece, piece, device)

    def along(column):
        copies[COLUMN, column].wait_recv()
        send(ALONG_X, column, flip(me, column), whole, x_side)
        send(ALONG_Y, column, flip(me, column), whole, y_side)

    def turn(column):
        copies[ALONG_X, column].wait_recv()
        send(TURN_Y, column, other(flip(me, column), 1), upper, y_side)
        copies[ALONG_Y, column].wait_recv()
        send(TURN_X, column, other(flip(me, column), 2), lower, x_side)

    def across(column):
        copies[TURN_Y, column].wait_recv()
        copies[TURN_X, column].wait_recv()
        first = (me % 2) * (devices // 2) + (flip(me, column) // 8) * 4
        layer = slots.at[pl.ds(first, 4)]
        copy(CORE, column, layer, layer, core)

    greet_partners(me, devices)
    wait_partners(devices)
    order = columns_of(devices)
    for index, column in enumerate(order[1:]):
        copy(COLUMN, column, shard, mine, flip(me, column))
        if index == 0:
            copy(ALONG_X, 0, shard, mine, x_side)
            copy(ALONG_Y, 0, shard, mine, y_side)
    mine[...] = shard[...]
    for index in range(len(order) + 2):
        if 1 <= index < len(order):
            along(order[index])
        if 0 <= index - 1 < len(order):
            turn(order[index - 1])
        if 0 <= index - 2 < len(order):
            across(order[index - 2])
    for (kind, column), made in copies.items():
        made.wait_send()
        if kind == CORE:
            made.wait_recv()
    chunks = D // LANES
    for device in range(devices):
        at = device * share // D
        shared = device * share % D != 0
        spot = slot_of(device, devices)
        for chunk in range(chunks):
            if shared:
                before = lines[chunk, at : at + 1, :]
            lines[chunk, at : at + rows, :] = slots[
                spot, :, chunk * LANES : (chunk + 1) * LANES
            ].astype(jnp.float32)
            if shared:
                lines[chunk, at : at + 1, :] = lines[chunk, at : at + 1, :] + before
    spread(lines, 0, w_qkv, 3)
    spread(lines, 1152, w_out, 1)
    spread(lines, 1536, w_up, 4)
    spread(lines, 3072, w_down, 1)
    spread(lines, 4608, tail, 1)


def spread(lines, first, out, times):
    height = out.shape[0]
    for column in range(times):
        for chunk in range(D // LANES):
            if times == 1:
                value = lines[chunk, first : first + height, :]
            else:
                value = lines[chunk, pl.ds(first + column, height, stride=times), :]
            at = column * D + chunk * LANES
            out[:, at : at + LANES] = value.astype(out.dtype)


def gather_weights(params, devices):
    share = params.shape[0]
    rows, _ = row_plan(share)
    offset = (lax.axis_index("dp") * share) % D
    flat = jnp.zeros((rows * D,), jnp.float32)
    flat = lax.dynamic_update_slice(flat, params, (offset,))
    shard = flat.reshape(rows, D).astype(jnp.bfloat16)
    vmem = pl.BlockSpec(memory_space=pltpu.VMEM)
    return pl.pallas_call(
        functools.partial(gather_kernel, devices, share),
        out_shape=(
            jax.ShapeDtypeStruct((D, 3 * D), jnp.bfloat16),
            jax.ShapeDtypeStruct((D, D), jnp.bfloat16),
            jax.ShapeDtypeStruct((D, FF), jnp.bfloat16),
            jax.ShapeDtypeStruct((FF, D), jnp.bfloat16),
            jax.ShapeDtypeStruct((16, D), jnp.float32),
        ),
        in_specs=[vmem],
        out_specs=[vmem] * 5,
        scratch_shapes=[
            pltpu.VMEM((D // LANES, LINES + rows + 24, LANES), jnp.float32),
            pltpu.VMEM((devices, rows, D), jnp.bfloat16),
            pltpu.SemaphoreType.DMA((6 * (devices // 8),)),
            pltpu.SemaphoreType.DMA((6 * (devices // 8),)),
        ],
        compiler_params=pltpu.CompilerParams(
            collective_id=0, has_side_effects=True, vmem_limit_bytes=60 * 2**20
        ),
    )(shard)


PAD = 208


def dot_nn(left, right):
    return lax.dot_general(left, right, (((1,), (0,)), ((), ())), preferred_element_type=jnp.float32)


def dot_nt(left, right):
    return lax.dot_general(left, right, (((1,), (1,)), ((), ())), preferred_element_type=jnp.float32)


def dot_tn(left, right):
    return lax.dot_general(left, right, (((0,), (0,)), ((), ())), preferred_element_type=jnp.float32)


def layer_norm(values):
    center = values - jnp.mean(values, axis=-1, keepdims=True)
    factor = lax.rsqrt(jnp.mean(center * center, axis=-1, keepdims=True) + 1e-06)
    return center * factor, factor


def norm_back(grad_hat, normed, factor):
    return factor * (
        grad_hat
        - jnp.mean(grad_hat, axis=-1, keepdims=True)
        - normed * jnp.mean(grad_hat * normed, axis=-1, keepdims=True)
    )


def column_sum(values):
    return jnp.sum(values, axis=0, keepdims=True)


def images_of(padded):
    return [(image, slice(image * PAD, (image + 1) * PAD)) for image in range(padded.shape[0] // PAD)]


TAIL = 4608
HOPS = 7
TO_CORE, TURN_UP, TURN_LOW, TO_X, TO_Y, TO_LAYER, TAIL_OUT = range(HOPS)


def units_of(devices, share):
    early, late = [], []
    for layer in range(devices // 8 - 1, -1, -1):
        if layer * 8 * share // D >= 3 * D:
            early.append((layer, (0, 1, 2), False))
        else:
            late.extend((layer, (chunk,), layer == 0 and chunk == 2) for chunk in range(3))
    late.sort(key=lambda unit: unit[1])
    return early, late


def unit_scratch(devices, share):
    rows, half = row_plan(share)
    early, late = units_of(devices, share)
    shapes = []
    for _, chunks, tail in early + late:
        wide = len(chunks) * LANES
        tall = rows + (48 if tail else 0)
        shapes += [(4, tall, wide)] * 2
        shapes += [(half, wide), (tall - half, wide)] * 2
        shapes += [(tall, wide)] * 5
    return [pltpu.VMEM(shape, jnp.bfloat16) for shape in shapes]


class Unit:
    def __init__(self, index, plan, devices, share, refs, shared):
        self.index, self.devices, self.share = index, devices, share
        self.layer, self.chunks, self.tail = plan
        (
            self.core_out, self.core_in, self.up_out, self.low_out, self.up_in, self.low_in,
            self.x_out, self.y_out, self.x_in, self.y_in, self.z_out,
        ) = refs
        (
            self.lines, self.g_tail, self.total, self.tail_total, self.z_in, self.tail_in,
            self.send_sem, self.recv_sem, self.z_sem, self.tail_sem,
        ) = shared
        self.rows, self.half = row_plan(share)
        self.stage = 0
        self.copies = {}
        me = lax.axis_index("dp")
        self.me = me
        self.z = me // 8
        self.core, self.x_side, self.y_side = other(me, 0), other(me, 1), other(me, 2)

    def copy(self, kind, source, target, device, recv=None):
        made = pltpu.make_async_remote_copy(
            src_ref=source,
            dst_ref=target,
            send_sem=self.send_sem.at[self.index, kind],
            recv_sem=self.recv_sem.at[self.index, kind] if recv is None else recv,
            device_id=(device,),
            device_id_type=pl.DeviceIdType.MESH,
        )
        return made

    def send(self, kind, source, target, device):
        self.copies[kind] = self.copy(kind, source, target, device)
        self.copies[kind].start()

    def advance(self):
        (self.pack, self.turn, self.along, self.arrive)[self.stage]()
        self.stage += 1

    def block(self, owner, spot, begin, end, index):
        first = owner * self.share // D
        chunk = self.chunks[index]
        lanes = slice(index * LANES, (index + 1) * LANES)
        value = self.lines[chunk, pl.ds(first + begin, end - begin), :]
        if spot is not None:
            value = value + self.core_in[spot, begin:end, lanes].astype(jnp.float32)
        return value

    def tail_block(self, spot, index):
        value = self.g_tail[:, index * LANES : (index + 1) * LANES]
        if spot is not None:
            at = self.rows + 16 * index
            value = value + self.core_in[spot, at : at + 16, :].astype(jnp.float32)
        return value

    def owner(self, spot, core):
        return self.layer * 8 + spot * 2 + core

    def pack(self):
        core = self.me % 2
        for spot in range(4):
            for index in range(len(self.chunks)):
                lanes = slice(index * LANES, (index + 1) * LANES)
                value = self.block(self.owner(spot, 1 - core), None, 0, self.rows, index)
                self.core_out[spot, : self.rows, lanes] = value.astype(jnp.bfloat16)
            if self.tail:
                for index in range(3):
                    at = self.rows + 16 * index
                    self.core_out[spot, at : at + 16, :] = self.tail_block(None, index).astype(
                        jnp.bfloat16
                    )
        self.send(TO_CORE, self.core_out, self.core_in, self.core)

    def spot_of(self, device):
        return device // 2 % 4

    def turn(self):
        self.copies[TO_CORE].wait_recv()
        spot = self.spot_of(other(self.x_side, 2))
        owner = self.owner(spot, self.me % 2)
        half, rows = self.half, self.rows
        for index in range(len(self.chunks)):
            lanes = slice(index * LANES, (index + 1) * LANES)
            self.up_out[:, lanes] = self.block(owner, spot, 0, half, index).astype(jnp.bfloat16)
            self.low_out[: rows - half, lanes] = self.block(
                owner, spot, half, rows, index
            ).astype(jnp.bfloat16)
        if self.tail:
            for index in range(3):
                at = rows - half + 16 * index
                self.low_out[at : at + 16, :] = self.tail_block(spot, index).astype(jnp.bfloat16)
        self.send(TURN_UP, self.up_out, self.up_in, self.y_side)
        self.send(TURN_LOW, self.low_out, self.low_in, self.x_side)

    def along(self):
        half, rows = self.half, self.rows
        for kind, device, out, into in (
            (TURN_UP, self.x_side, self.x_out, self.x_in),
            (TURN_LOW, self.y_side, self.y_out, self.y_in),
        ):
            self.copies[kind].wait_recv()
            spot = self.spot_of(device)
            owner = self.owner(spot, self.me % 2)
            for index in range(len(self.chunks)):
                lanes = slice(index * LANES, (index + 1) * LANES)
                upper = self.block(owner, spot, 0, half, index)
                lower = self.block(owner, spot, half, rows, index)
                if kind == TURN_UP:
                    upper = upper + self.up_in[:, lanes].astype(jnp.float32)
                else:
                    lower = lower + self.low_in[: rows - half, lanes].astype(jnp.float32)
                out[:half, lanes] = upper.astype(jnp.bfloat16)
                out[half:rows, lanes] = lower.astype(jnp.bfloat16)
            if self.tail:
                for index in range(3):
                    at = rows + 16 * index
                    value = self.tail_block(spot, index)
                    if kind == TURN_LOW:
                        value = value + self.low_in[at - half : at - half + 16, :].astype(
                            jnp.float32
                        )
                    out[at : at + 16, :] = value.astype(jnp.bfloat16)
            self.send(TO_X if kind == TURN_UP else TO_Y, out, into, device)

    def away(self, source):
        first, last = self.chunks[0] * LANES, (self.chunks[-1] + 1) * LANES
        return self.copy(
            TO_LAYER,
            self.z_out.at[pl.ds(0, self.rows)],
            self.z_in.at[source, :, pl.ds(first, last - first)],
            self.layer * 8 + self.me % 8,
            self.z_sem.at[self.index, source],
        )

    def tail_away(self, source):
        return self.copy(
            TAIL_OUT,
            self.z_out.at[pl.ds(self.rows, 48)],
            self.tail_in.at[source],
            self.devices - 8 + self.me % 8,
            self.tail_sem.at[source],
        )

    def arrive(self):
        self.copies[TO_X].wait_recv()
        self.copies[TO_Y].wait_recv()
        spot = self.spot_of(self.me)
        owner = self.owner(spot, self.me % 2)
        rows = self.rows
        for index, chunk in enumerate(self.chunks):
            lanes = slice(index * LANES, (index + 1) * LANES)
            value = self.block(owner, spot, 0, rows, index)
            value = value + self.x_in[:rows, lanes].astype(jnp.float32)
            value = value + self.y_in[:rows, lanes].astype(jnp.float32)
            self.z_out[:rows, lanes] = value.astype(jnp.bfloat16)

            @pl.when(self.z == self.layer)
            def _(value=value, chunk=chunk):
                self.total[:, chunk * LANES : (chunk + 1) * LANES] = value

        @pl.when(self.z != self.layer)
        def _():
            self.away(self.z).start()

        if self.tail:
            last = self.devices // 8 - 1
            for index in range(3):
                at = rows + 16 * index
                value = self.tail_block(spot, index)
                value = value + self.x_in[at : at + 16, :].astype(jnp.float32)
                value = value + self.y_in[at : at + 16, :].astype(jnp.float32)
                self.z_out[at : at + 16, :] = value.astype(jnp.bfloat16)
                self.tail_total[:, index * LANES : (index + 1) * LANES] = value

            @pl.when(self.z != last)
            def _():
                self.tail_away(self.z).start()

    def finish(self):
        last = self.devices // 8 - 1
        for made in self.copies.values():
            made.wait_send()

        @pl.when(self.z != self.layer)
        def _():
            self.away(self.z).wait_send()

        first, end = self.chunks[0] * LANES, (self.chunks[-1] + 1) * LANES
        for source in range(last + 1):
            if source != self.layer:

                @pl.when(self.z == self.layer)
                def _(source=source):
                    self.away(source).wait_recv()
                    self.total[:, first:end] += self.z_in[source, :, first:end].astype(jnp.float32)

        if self.tail:

            @pl.when(self.z != last)
            def _():
                self.tail_away(self.z).wait_send()

            for source in range(last):

                @pl.when(self.z == last)
                def _(source=source):
                    self.tail_away(source).wait_recv()
                    for index in range(3):
                        self.tail_total[:, index * LANES : (index + 1) * LANES] += self.tail_in[
                            source, 16 * index : 16 * index + 16, :
                        ].astype(jnp.float32)


def step_kernel(
    devices, share, tokens, cot, w_qkv, w_out, w_up, w_down, tail, result, grad_tokens, out,
    xbuf, dybuf, xhat, a16, qkv16, probs, o16, h, xhat2, c16, acc, dc, dy16, dh, dh16, do16, dqkv16,
    s1, s2, slope, lines, g_tail, total, tail_total, z_in, tail_in, send_sem, recv_sem, z_sem, tail_sem, *refs,
):
    me = lax.axis_index("dp")
    greet_partners(me, devices)
    early, late = units_of(devices, share)
    shared = (
        lines, g_tail, total, tail_total, z_in, tail_in, send_sem, recv_sem, z_sem, tail_sem,
    )
    units = [
        Unit(index, plan, devices, share, refs[index * 11 : index * 11 + 11], shared)
        for index, plan in enumerate(early + late)
    ]
    count = len(early)
    early, late = units[:count], units[count:]
    firsts = {unit: unit.layer * 8 * share // D for unit in early}
    down = [unit for unit in early if firsts[unit] >= 8 * D]
    up = [unit for unit in early if 4 * D <= firsts[unit] < 8 * D]
    mixed = [unit for unit in early if firsts[unit] < 4 * D]
    first, second, third = ([unit for unit in late if unit.chunks[0] == pair] for pair in range(3))

    load(tokens, xbuf)
    load(cot, dybuf)
    lines[:, TAIL:, :] = jnp.zeros_like(lines[:, TAIL:, :])
    attention_in(xbuf, tail, xhat, s1, a16, w_qkv, qkv16)
    attention(qkv16, probs, o16)
    middle(xbuf, o16, w_out, tail, h, xhat2, s2, c16, dybuf, dy16)
    feed_forward(c16, dy16, w_up, w_down, tail, acc, slope, lines)
    wait_partners(devices)
    advance(down)
    feed_forward_back(c16, dy16, w_up, w_down, slope, dc, lines, g_tail)
    advance(up)
    advance(down)
    feed_forward_end(h, acc, tail, dc, xhat2, s2, dybuf, result, dh, dh16, g_tail)
    advance(up)
    attention_out_back(o16, dh16, w_out, lines, do16)
    advance(mixed)
    advance(down)
    g_tail[2:4, :] = jnp.zeros((2, D), jnp.float32)
    attention_back(0, qkv16, probs, do16, dqkv16, g_tail)
    advance(mixed)
    attention_in_back(0, a16, dqkv16, w_qkv, lines, acc)
    advance(first)
    advance(up)
    attention_back(1, qkv16, probs, do16, dqkv16, g_tail)
    advance(first)
    attention_in_back(1, a16, dqkv16, w_qkv, lines, acc)
    advance(second)
    advance(mixed)
    advance(down)
    attention_back(2, qkv16, probs, do16, dqkv16, g_tail)
    advance(second)
    attention_in_back(2, a16, dqkv16, w_qkv, lines, acc)
    input_sums(acc, xhat, g_tail)
    advance(third)
    advance(first)
    grad_input(acc, tail, xhat, s1, dh, grad_tokens)
    advance(up)
    advance(third)
    advance(second)
    advance(mixed)
    advance(first)
    advance(third)
    advance(second)
    advance(third)
    for unit in units:
        unit.finish()
    at = TAIL - (devices - 1) * share // D
    out[...] = total[...]

    @pl.when(me == devices - 1)
    def _():
        out[at : at + 12, :] = total[at : at + 12, :] + tail_total[0:12, :]


def advance(units):
    for unit in units:
        unit.advance()


def load(source, padded):
    for image in range(source.shape[1]):
        at = image * PAD
        padded[at + PAD - 16 : at + PAD, :] = jnp.zeros((16, D), jnp.float32)
        padded[at : at + SEQ, :] = source[:, image, :]


def attention_in(xbuf, tail, xhat, s1, a16, w_qkv, qkv16):
    for _, rows in images_of(xbuf):
        normed, factor = layer_norm(xbuf[rows, :])
        xhat[rows, :] = normed
        s1[rows, :] = factor
        a16[rows, :] = (normed * tail[0:1, :] + tail[1:2, :]).astype(jnp.bfloat16)
    for piece in range(3):
        cols = slice(piece * D, (piece + 1) * D)
        value = dot_nn(a16[...], w_qkv[:, cols])
        if piece == 0:
            value = value + tail[2:3, :]
        if piece == 2:
            value = value + tail[3:4, :]
        qkv16[:, cols] = value.astype(jnp.bfloat16)


def half_of(values, half):
    lane = lax.broadcasted_iota(jnp.int32, values.shape, 1)
    return jnp.where((lane < 64) if half == 0 else (lane >= 64), values, jnp.zeros_like(values))


def views(step):
    image, pair = step // 3, step % 3
    rows = pl.ds(pl.multiple_of(image * PAD, 16), PAD)
    return rows, [pl.ds(pl.multiple_of(part * D + pair * 128, 128), 128) for part in range(3)]


def attention(qkv16, probs, o16):
    def body(step, carry):
        rows, (qs, ks, vs) = views(step)
        query, key, value = qkv16[rows, qs], qkv16[rows, ks], qkv16[rows, vs]
        total = None
        for half in range(2):
            scores = dot_nt(query, half_of(key, half)) * 0.125
            column = lax.broadcasted_iota(jnp.int32, scores.shape, 1)
            scores = jnp.where(column < SEQ, scores, -jnp.inf)
            raised = jnp.exp(scores - jnp.max(scores, axis=-1, keepdims=True))
            prob = raised / jnp.sum(raised, axis=-1, keepdims=True)
            probs[step * 2 + half] = prob
            term = dot_nn(prob.astype(jnp.bfloat16), half_of(value, half))
            total = term if total is None else total + term
        o16[rows, qs] = total.astype(jnp.bfloat16)
        return carry

    lax.fori_loop(0, qkv16.shape[0] // PAD * 3, body, 0, unroll=True)


def middle(xbuf, o16, w_out, tail, h, xhat2, s2, c16, dybuf, dy16):
    for _, rows in images_of(xbuf):
        value = xbuf[rows, :] + (dot_nn(o16[rows, :], w_out[...]) + tail[4:5, :])
        h[rows, :] = value
        normed, factor = layer_norm(value)
        xhat2[rows, :] = normed
        s2[rows, :] = factor
        c16[rows, :] = (normed * tail[5:6, :] + tail[6:7, :]).astype(jnp.bfloat16)
        dy16[rows, :] = dybuf[rows, :].astype(jnp.bfloat16)


def lanes_of(index, width):
    return slice(index * width, (index + 1) * width)


def feed_forward(c16, dy16, w_up, w_down, tail, acc, slope, lines):
    for line in range(FF // D):
        cols = lanes_of(line, D)
        pre = dot_nn(c16[...], w_up[:, cols]) + tail[8 + line : 9 + line, :]
        phi = 0.5 * (1.0 + lax.erf(pre * 0.7071067811865476))
        slope[:, cols] = phi + pre * jnp.exp(-0.5 * pre * pre) * 0.3989422804014327
        act = (pre * phi).astype(jnp.bfloat16)
        value = dot_nn(act, w_down[cols, :])
        acc[...] = value if line == 0 else acc[...] + value
        grad_down = dot_tn(act, dy16[...])
        first = 8 * D + line * D
        for chunk in range(D // LANES):
            lines[chunk, first : first + D, :] = grad_down[:, lanes_of(chunk, LANES)]


def feed_forward_back(c16, dy16, w_up, w_down, slope, dc, lines, g_tail):
    for line in range(FF // D):
        cols = lanes_of(line, D)
        grad_pre = dot_nt(dy16[...], w_down[cols, :]) * slope[:, cols]
        half = grad_pre.astype(jnp.bfloat16)
        grad_up = dot_tn(c16[...], half)
        for chunk in range(D // LANES):
            lines[chunk, pl.ds(4 * D + line, D, stride=4), :] = grad_up[:, lanes_of(chunk, LANES)]
        g_tail[8 + line : 9 + line, :] = column_sum(grad_pre)
        value = dot_nt(half, w_up[:, cols])
        dc[...] = value if line == 0 else dc[...] + value


def feed_forward_end(h, acc, tail, dc, xhat2, s2, dybuf, result, dh, dh16, g_tail):
    sums = [0.0] * 4
    for image, rows in images_of(h):
        value = h[rows, :] + (acc[rows, :] + tail[7:8, :])
        result[:, image, :] = value[:SEQ]
        grad, normed = dc[rows, :], xhat2[rows, :]
        hidden = dybuf[rows, :] + norm_back(grad * tail[5:6, :], normed, s2[rows, :])
        dh[rows, :] = hidden
        dh16[rows, :] = hidden.astype(jnp.bfloat16)
        terms = (hidden, grad * normed, grad, dybuf[rows, :])
        sums = [old + column_sum(new) for old, new in zip(sums, terms)]
    for index in range(4):
        g_tail[4 + index : 5 + index, :] = sums[index]
    g_tail[12:16, :] = jnp.zeros((4, D), jnp.float32)


def attention_out_back(o16, dh16, w_out, lines, do16):
    grad_out = dot_tn(o16[...], dh16[...])
    for chunk in range(D // LANES):
        lines[chunk, 3 * D : 4 * D, :] = grad_out[:, chunk * LANES : (chunk + 1) * LANES]
    do16[...] = dot_nt(dh16[...], w_out[...]).astype(jnp.bfloat16)


def attention_back(pair, qkv16, probs, do16, dqkv16, g_tail):
    def body(image, carry):
        step = image * 3 + pair
        rows, (qs, ks, vs) = views(step)
        query, key, value, grad = qkv16[rows, qs], qkv16[rows, ks], qkv16[rows, vs], do16[rows, qs]
        dq = dk = dv = None
        for half in range(2):
            prob = probs[step * 2 + half]
            dv_term = dot_tn(prob.astype(jnp.bfloat16), half_of(grad, half))
            grad_prob = dot_nt(grad, half_of(value, half))
            delta = jnp.sum(prob * grad_prob, axis=-1, keepdims=True)
            ds = (prob * (grad_prob - delta) * 0.125).astype(jnp.bfloat16)
            dq_term = dot_nn(ds, half_of(key, half))
            dk_term = dot_tn(ds, half_of(query, half))
            if half == 0:
                dq, dk, dv = dq_term, dk_term, dv_term
            else:
                dq, dk, dv = dq + dq_term, dk + dk_term, dv + dv_term
        dqkv16[rows, qs] = dq.astype(jnp.bfloat16)
        dqkv16[rows, ks] = dk.astype(jnp.bfloat16)
        dqkv16[rows, vs] = dv.astype(jnp.bfloat16)
        g_tail[2:3, qs] += column_sum(dq)
        g_tail[3:4, qs] += column_sum(dv)
        return carry

    lax.fori_loop(0, qkv16.shape[0] // PAD, body, 0, unroll=True)


def attention_in_back(pair, a16, dqkv16, w_qkv, lines, acc):
    parts = [slice(part * D + pair * LANES, part * D + (pair + 1) * LANES) for part in range(3)]
    grads = jnp.concatenate([dqkv16[:, part] for part in parts], axis=1)
    weights = jnp.concatenate([w_qkv[:, part] for part in parts], axis=1)
    grad_w = dot_tn(a16[...], grads)
    for part in range(3):
        lines[pair, pl.ds(part, D, stride=3), :] = grad_w[:, part * LANES : (part + 1) * LANES]
    value = dot_nt(grads, weights)
    acc[...] = value if pair == 0 else acc[...] + value


def input_sums(acc, xhat, g_tail):
    sums = [0.0] * 2
    for _, rows in images_of(acc):
        grad = acc[rows, :]
        sums = [old + column_sum(new) for old, new in zip(sums, (grad * xhat[rows, :], grad))]
    for index in range(2):
        g_tail[index : index + 1, :] = sums[index]


def grad_input(acc, tail, xhat, s1, dh, grad_tokens):
    for image, rows in images_of(acc):
        value = dh[rows, :] + norm_back(acc[rows, :] * tail[0:1, :], xhat[rows, :], s1[rows, :])
        grad_tokens[:, image, :] = value[:SEQ]


def compute_scratch(images):
    f32, bf16 = jnp.float32, jnp.bfloat16
    rows = images * PAD
    return [
        pltpu.VMEM((rows, D), f32),
        pltpu.VMEM((rows, D), f32),
        pltpu.VMEM((rows, D), f32),
        pltpu.VMEM((rows, D), bf16),
        pltpu.VMEM((rows, 3 * D), bf16),
        pltpu.VMEM((images * HEADS, PAD, PAD), f32),
        pltpu.VMEM((rows, D), bf16),
        pltpu.VMEM((rows, D), f32),
        pltpu.VMEM((rows, D), f32),
        pltpu.VMEM((rows, D), bf16),
        pltpu.VMEM((rows, D), f32),
        pltpu.VMEM((rows, D), f32),
        pltpu.VMEM((rows, D), bf16),
        pltpu.VMEM((rows, D), f32),
        pltpu.VMEM((rows, D), bf16),
        pltpu.VMEM((rows, D), bf16),
        pltpu.VMEM((rows, 3 * D), bf16),
        pltpu.VMEM((rows, 1), f32),
        pltpu.VMEM((rows, 1), f32),
        pltpu.VMEM((rows, FF), f32),
    ]


def compute(tokens, cotangent, weights, devices, share):
    f32 = jnp.float32
    rows, _ = row_plan(share)
    layers = devices // 8
    early, late = units_of(devices, share)
    count = len(early) + len(late)
    vmem = pl.BlockSpec(memory_space=pltpu.VMEM)
    result, grad_tokens, total = pl.pallas_call(
        functools.partial(step_kernel, devices, share),
        out_shape=(
            jax.ShapeDtypeStruct(tokens.shape, f32),
            jax.ShapeDtypeStruct(tokens.shape, f32),
            jax.ShapeDtypeStruct((rows, D), f32),
        ),
        in_specs=[vmem] * 7,
        out_specs=[vmem] * 3,
        scratch_shapes=compute_scratch(tokens.shape[1])
        + [
            pltpu.VMEM((D // LANES, LINES + rows + 24, LANES), f32),
            pltpu.VMEM((16, D), f32),
            pltpu.VMEM((rows, D), f32),
            pltpu.VMEM((16, D), f32),
            pltpu.VMEM((layers, rows, D), jnp.bfloat16),
            pltpu.VMEM((layers, 48, LANES), jnp.bfloat16),
            pltpu.SemaphoreType.DMA((count, HOPS)),
            pltpu.SemaphoreType.DMA((count, HOPS)),
            pltpu.SemaphoreType.DMA((count, layers)),
            pltpu.SemaphoreType.DMA((layers,)),
        ]
        + unit_scratch(devices, share),
        compiler_params=pltpu.CompilerParams(
            collective_id=1, has_side_effects=True, vmem_limit_bytes=60 * 2**20
        ),
    )(tokens, cotangent, *weights)
    offset = (lax.axis_index("dp") * share) % D
    return result, grad_tokens, lax.dynamic_slice(total.reshape(-1), (offset,), (share,))


def adamw(params, grads, first, second, position):
    first_end = 3 * D * D
    second_end = first_end + D * D
    third_end = second_end + D * FF
    fourth_end = third_end + FF * D
    rate = jnp.where(
        position < first_end,
        0.01,
        jnp.where(
            position < second_end,
            0.1,
            jnp.where(position < third_end, 0.01, jnp.where(position < fourth_end, 0.005, 0.1)),
        ),
    )
    first_new = 0.9 * first + 0.1 * grads
    second_new = 0.999 * second + 0.001 * grads * grads
    update = (
        first_new / (1.0 - 0.9**STEP) / (jnp.sqrt(second_new / (1.0 - 0.999**STEP)) + 1e-08)
        + 0.1 * params
    )
    return (params - rate * update, first_new, second_new)


def per_device(tokens, params, moment1, moment2, cotangent):
    devices = lax.axis_size("dp")
    length = params.shape[0]
    w_qkv, w_out, w_up, w_down, tail = gather_weights(params, devices)
    weights = (w_qkv, w_out, w_up, w_down, tail)
    result, grad_tokens, shares = compute(
        tokens.transpose(1, 0, 2), cotangent.transpose(1, 0, 2), weights, devices, length
    )
    result, grad_tokens = result.transpose(1, 0, 2), grad_tokens.transpose(1, 0, 2)
    count = tokens.shape[0] * tokens.shape[1] * devices
    grad_params = shares * (1.0 / math.sqrt(count))
    position = lax.axis_index("dp") * length + jnp.arange(length, dtype=jnp.int32)
    new_params, new_first, new_second = adamw(params, grad_params, moment1, moment2, position)
    return (result, grad_tokens, grad_params, new_params, new_first, new_second)


def solution(mesh):
    in_specs = (P("dp", None, None), P("dp"), P("dp"), P("dp"), P("dp", None, None))
    out_specs = (P("dp", None, None), P("dp", None, None), P("dp"), P("dp"), P("dp"), P("dp"))
    return jax.shard_map(
        per_device, mesh=mesh, in_specs=in_specs, out_specs=out_specs, check_vma=False
    )
```

```python
import math

import jax
import jax.numpy as jnp
from jax import lax
from jax.experimental import pallas as pl
from jax.experimental.pallas import tpu as pltpu
import functools
from jax.sharding import PartitionSpec as P

D = 384
HEADS = 6
FF = 1536
SEQ = 197
STEP = 3


LANES = 128
LINES = 4 * 1152 + 12


def other(device, bit):
    step = 2**bit
    return device + step - 2 * step * ((device // step) % 2)


def flip(device, column):
    bit = 3
    while column:
        if column % 2:
            device = other(device, bit)
        column //= 2
        bit += 1
    return device


def slot_of(device, devices):
    return (device % 2) * (devices // 2) + device // 2


def partners_of(me, devices):
    return [other(me, bit) for bit in range(3)] + [flip(me, j) for j in range(1, devices // 8)]


def greet_partners(me, devices):
    for partner in partners_of(me, devices):
        pl.semaphore_signal(
            pltpu.get_barrier_semaphore(),
            inc=1,
            device_id=(partner,),
            device_id_type=pl.DeviceIdType.MESH,
        )


def wait_partners(devices):
    pl.semaphore_wait(pltpu.get_barrier_semaphore(), 2 + devices // 8)


def columns_of(devices):
    order = list(range(devices // 8))
    return [0, 1, 3, 2] if devices == 32 else order


def row_plan(share):
    rows = -(-(share + D - 1) // D)
    rows = -(-rows // 32) * 32
    return rows, rows // 2


COLUMN, ALONG_X, ALONG_Y, TURN_X, TURN_Y, CORE, LATER_X, LATER_Y = range(8)


def greet(me, bits):
    barrier = pltpu.get_barrier_semaphore()
    for bit in range(bits):
        pl.semaphore_signal(
            barrier, inc=1, device_id=(other(me, bit),), device_id_type=pl.DeviceIdType.MESH
        )
    pl.semaphore_wait(barrier, bits)


def align(share, raw, wide, mine):
    rows, _ = row_plan(share)
    offset = (lax.axis_index("dp") * share) % D
    source = lax.broadcasted_iota(jnp.int32, (D, 2 * D), 0)
    target = lax.broadcasted_iota(jnp.int32, (D, 2 * D), 1)
    moved = (target == source + offset).astype(jnp.bfloat16)
    both = jnp.dot(raw[...], moved, preferred_element_type=jnp.float32)
    wide[0:8, :] = jnp.zeros((8, D), jnp.float32)
    wide[8 : 8 + rows, :] = both[:, D:]
    mine[...] = (both[:, :D] + wide[7 : 7 + rows, :]).astype(jnp.bfloat16)


class Gather:
    def __init__(self, devices, share, lines, shard, slots, send_sem, recv_sem):
        self.devices, self.share = devices, share
        self.lines, self.shard, self.slots = lines, shard, slots
        self.send_sem, self.recv_sem = send_sem, recv_sem
        self.rows, self.half = row_plan(share)
        me = lax.axis_index("dp")
        self.me = me
        self.core, self.x_side, self.y_side = other(me, 0), other(me, 1), other(me, 2)
        self.copies = {}

    def copy(self, kind, column, source, target, device):
        spot = kind * (self.devices // 8) + column
        made = pltpu.make_async_remote_copy(
            src_ref=source,
            dst_ref=target,
            send_sem=self.send_sem.at[spot],
            recv_sem=self.recv_sem.at[spot],
            device_id=(device,),
            device_id_type=pl.DeviceIdType.MESH,
        )
        made.start()
        self.copies[kind, column] = made

    def send(self, kind, column, owner, begin, size, device):
        piece = self.slots.at[slot_of(owner, self.devices), pl.ds(begin, size)]
        self.copy(kind, column, piece, piece, device)

    def begin(self, order):
        mine = self.slots.at[slot_of(self.me, self.devices)]
        for index, column in enumerate(order[1:]):
            self.copy(COLUMN, column, self.shard, mine, flip(self.me, column))
            if index == 0:
                upper, lower = pl.ds(0, self.half), pl.ds(self.half, self.half)
                shard = self.shard
                self.copy(ALONG_X, 0, shard.at[upper], mine.at[upper], self.x_side)
                self.copy(ALONG_Y, 0, shard.at[lower], mine.at[lower], self.y_side)
                self.copy(LATER_X, 0, shard.at[lower], mine.at[lower], self.x_side)
                self.copy(LATER_Y, 0, shard.at[upper], mine.at[upper], self.y_side)
        mine[...] = self.shard[...]

    def along(self, column):
        self.copies[COLUMN, column].wait_recv()
        half, owner = self.half, flip(self.me, column)
        self.send(ALONG_X, column, owner, 0, half, self.x_side)
        self.send(ALONG_Y, column, owner, half, half, self.y_side)
        self.send(LATER_X, column, owner, half, half, self.x_side)
        self.send(LATER_Y, column, owner, 0, half, self.y_side)

    def turn(self, column):
        half = self.half
        self.copies[ALONG_X, column].wait_recv()
        self.send(TURN_Y, column, other(flip(self.me, column), 1), 0, half, self.y_side)
        self.copies[ALONG_Y, column].wait_recv()
        self.send(TURN_X, column, other(flip(self.me, column), 2), half, half, self.x_side)

    def across(self, column):
        self.copies[TURN_Y, column].wait_recv()
        self.copies[TURN_X, column].wait_recv()
        self.copies[LATER_X, column].wait_recv()
        self.copies[LATER_Y, column].wait_recv()
        first = (self.me % 2) * (self.devices // 2) + (flip(self.me, column) // 8) * 4
        layer = self.slots.at[pl.ds(first, 4)]
        self.copy(CORE, column, layer, layer, self.core)
        self.unpack(column, self.me % 2)

    def end(self, column):
        self.copies[CORE, column].wait_recv()
        self.unpack(column, 1 - self.me % 2)

    def unpack(self, column, core):
        layer = flip(self.me, column) // 8
        for spot in range(4):
            device = layer * 8 + spot * 2 + core
            where = pl.ds(device * self.share // D, self.rows)
            place = core * (self.devices // 2) + layer * 4 + spot
            for chunk in range(D // LANES):
                self.lines[chunk, where, :] += self.slots[
                    place, :, chunk * LANES : (chunk + 1) * LANES
                ].astype(jnp.float32)

    def finish(self):
        for made in self.copies.values():
            made.wait_send()


def gather_weights(gather, order, w_qkv, w_out, w_up, w_down, tail):
    count = len(order)
    for index in range(1, count + 3):
        if index < count:
            gather.along(order[index])
        if 0 <= index - 1 < count:
            gather.turn(order[index - 1])
        if 0 <= index - 2 < count:
            gather.across(order[index - 2])
        if 0 <= index - 3 < count:
            gather.end(order[index - 3])
    lines = gather.lines
    spread(lines, 0, w_qkv, 3)
    spread(lines, 1152, w_out, 1)
    spread(lines, 1536, w_up, 4)
    spread(lines, 3072, w_down, 1)
    spread(lines, 4608, tail, 1)
    gather.finish()


def spread(lines, first, out, times):
    height = out.shape[0]
    for column in range(times):
        for chunk in range(D // LANES):
            if times == 1:
                value = lines[chunk, first : first + height, :]
            else:
                value = lines[chunk, pl.ds(first + column, height, stride=times), :]
            at = column * D + chunk * LANES
            out[:, at : at + LANES] = value.astype(out.dtype)


PAD = 208


def dot_nn(left, right):
    return lax.dot_general(left, right, (((1,), (0,)), ((), ())), preferred_element_type=jnp.float32)


def dot_nt(left, right):
    return lax.dot_general(left, right, (((1,), (1,)), ((), ())), preferred_element_type=jnp.float32)


def dot_tn(left, right):
    return lax.dot_general(left, right, (((0,), (0,)), ((), ())), preferred_element_type=jnp.float32)


def layer_norm(values):
    center = values - jnp.mean(values, axis=-1, keepdims=True)
    factor = lax.rsqrt(jnp.mean(center * center, axis=-1, keepdims=True) + 1e-06)
    return center * factor, factor


def norm_back(grad_hat, normed, factor):
    return factor * (
        grad_hat
        - jnp.mean(grad_hat, axis=-1, keepdims=True)
        - normed * jnp.mean(grad_hat * normed, axis=-1, keepdims=True)
    )


def column_sum(values):
    return jnp.sum(values, axis=0, keepdims=True)


def images_of(padded):
    return [(image, slice(image * PAD, (image + 1) * PAD)) for image in range(padded.shape[0] // PAD)]


TAIL = 4608
HOPS = 9
TO_CORE, TURN_UP, TURN_LOW, TO_X, TO_Y, TO_LAYER, TAIL_OUT, SOON_X, SOON_Y = range(HOPS)


def units_of(devices, share):
    early, late = [], []
    for layer in range(devices // 8 - 1, -1, -1):
        if layer * 8 * share // D >= 3 * D:
            early.append((layer, (0, 1, 2), False))
        else:
            late.extend((layer, (chunk,), layer == 0 and chunk == 2) for chunk in range(3))
    late.sort(key=lambda unit: unit[1])
    return early, late


def unit_scratch(devices, share):
    rows, half = row_plan(share)
    early, late = units_of(devices, share)
    shapes = []
    for _, chunks, tail in early + late:
        wide = len(chunks) * LANES
        tall = rows + (48 if tail else 0)
        shapes += [(4, tall, wide)] * 2
        shapes += [(half, wide), (tall - half, wide)] * 2
        shapes += [(tall, wide)] * 5
    return [pltpu.VMEM(shape, jnp.bfloat16) for shape in shapes]


class Unit:
    def __init__(self, index, plan, devices, share, refs, shared):
        self.index, self.devices, self.share = index, devices, share
        self.layer, self.chunks, self.tail = plan
        (
            self.core_out, self.core_in, self.up_out, self.low_out, self.up_in, self.low_in,
            self.x_out, self.y_out, self.x_in, self.y_in, self.z_out,
        ) = refs
        (
            self.lines, self.g_tail, self.total, self.tail_total, self.z_in, self.tail_in,
            self.send_sem, self.recv_sem, self.z_sem, self.tail_sem,
        ) = shared
        self.rows, self.half = row_plan(share)
        self.stage = 0
        self.copies = {}
        me = lax.axis_index("dp")
        self.me = me
        self.z = me // 8
        self.core, self.x_side, self.y_side = other(me, 0), other(me, 1), other(me, 2)

    def copy(self, kind, source, target, device, recv=None):
        made = pltpu.make_async_remote_copy(
            src_ref=source,
            dst_ref=target,
            send_sem=self.send_sem.at[self.index, kind],
            recv_sem=self.recv_sem.at[self.index, kind] if recv is None else recv,
            device_id=(device,),
            device_id_type=pl.DeviceIdType.MESH,
        )
        return made

    def send(self, kind, source, target, device):
        self.copies[kind] = self.copy(kind, source, target, device)
        self.copies[kind].start()

    def advance(self):
        (self.pack, self.turn, self.along, self.arrive)[self.stage]()
        self.stage += 1

    def block(self, owner, spot, begin, end, index):
        first = owner * self.share // D
        chunk = self.chunks[index]
        lanes = slice(index * LANES, (index + 1) * LANES)
        value = self.lines[chunk, pl.ds(first + begin, end - begin), :]
        if spot is not None:
            value = value + self.core_in[spot, begin:end, lanes].astype(jnp.float32)
        return value

    def tail_block(self, spot, index):
        value = self.g_tail[:, index * LANES : (index + 1) * LANES]
        if spot is not None:
            at = self.rows + 16 * index
            value = value + self.core_in[spot, at : at + 16, :].astype(jnp.float32)
        return value

    def owner(self, spot, core):
        return self.layer * 8 + spot * 2 + core

    def pack(self):
        core = self.me % 2
        for spot in range(4):
            for index in range(len(self.chunks)):
                lanes = slice(index * LANES, (index + 1) * LANES)
                value = self.block(self.owner(spot, 1 - core), None, 0, self.rows, index)
                self.core_out[spot, : self.rows, lanes] = value.astype(jnp.bfloat16)
            if self.tail:
                for index in range(3):
                    at = self.rows + 16 * index
                    self.core_out[spot, at : at + 16, :] = self.tail_block(None, index).astype(
                        jnp.bfloat16
                    )
        self.send(TO_CORE, self.core_out, self.core_in, self.core)

    def spot_of(self, device):
        return device // 2 % 4

    def turn(self):
        self.copies[TO_CORE].wait_recv()
        spot = self.spot_of(other(self.x_side, 2))
        owner = self.owner(spot, self.me % 2)
        half, rows = self.half, self.rows
        for index in range(len(self.chunks)):
            lanes = slice(index * LANES, (index + 1) * LANES)
            self.up_out[:, lanes] = self.block(owner, spot, 0, half, index).astype(jnp.bfloat16)
            self.low_out[: rows - half, lanes] = self.block(
                owner, spot, half, rows, index
            ).astype(jnp.bfloat16)
        if self.tail:
            for index in range(3):
                at = rows - half + 16 * index
                self.low_out[at : at + 16, :] = self.tail_block(spot, index).astype(jnp.bfloat16)
        self.send(TURN_UP, self.up_out, self.up_in, self.y_side)
        self.send(TURN_LOW, self.low_out, self.low_in, self.x_side)
        self.soon(SOON_X, self.x_side, self.x_out, self.x_in, half, rows)
        self.soon(SOON_Y, self.y_side, self.y_out, self.y_in, 0, half)

    def soon(self, kind, device, out, into, begin, end):
        spot = self.spot_of(device)
        owner = self.owner(spot, self.me % 2)
        for index in range(len(self.chunks)):
            lanes = slice(index * LANES, (index + 1) * LANES)
            out[begin:end, lanes] = self.block(owner, spot, begin, end, index).astype(jnp.bfloat16)
        size = end - begin
        if self.tail and begin:
            size += 48
            for index in range(3):
                at = end + 16 * index
                out[at : at + 16, :] = self.tail_block(spot, index).astype(jnp.bfloat16)
        self.send(kind, out.at[pl.ds(begin, size)], into.at[pl.ds(begin, size)], device)

    def along(self):
        half, rows = self.half, self.rows
        tall = rows - half + (48 if self.tail else 0)
        for kind, device, out, into, begin, end, size in (
            (TURN_UP, self.x_side, self.x_out, self.x_in, 0, half, half),
            (TURN_LOW, self.y_side, self.y_out, self.y_in, half, rows, tall),
        ):
            self.copies[kind].wait_recv()
            spot = self.spot_of(device)
            owner = self.owner(spot, self.me % 2)
            turned = self.up_in if kind == TURN_UP else self.low_in
            for index in range(len(self.chunks)):
                lanes = slice(index * LANES, (index + 1) * LANES)
                value = self.block(owner, spot, begin, end, index)
                value = value + turned[: end - begin, lanes].astype(jnp.float32)
                out[begin:end, lanes] = value.astype(jnp.bfloat16)
            if self.tail and begin:
                for index in range(3):
                    at = rows + 16 * index
                    value = self.tail_block(spot, index)
                    value = value + turned[at - half : at - half + 16, :].astype(jnp.float32)
                    out[at : at + 16, :] = value.astype(jnp.bfloat16)
            self.send(
                TO_X if kind == TURN_UP else TO_Y,
                out.at[pl.ds(begin, size)],
                into.at[pl.ds(begin, size)],
                device,
            )

    def away(self, source):
        first, last = self.chunks[0] * LANES, (self.chunks[-1] + 1) * LANES
        return self.copy(
            TO_LAYER,
            self.z_out.at[pl.ds(0, self.rows)],
            self.z_in.at[source, :, pl.ds(first, last - first)],
            self.layer * 8 + self.me % 8,
            self.z_sem.at[self.index, source],
        )

    def tail_away(self, source):
        return self.copy(
            TAIL_OUT,
            self.z_out.at[pl.ds(self.rows, 48)],
            self.tail_in.at[source],
            self.devices - 8 + self.me % 8,
            self.tail_sem.at[source],
        )

    def arrive(self):
        for kind in (TO_X, TO_Y, SOON_X, SOON_Y):
            self.copies[kind].wait_recv()
        spot = self.spot_of(self.me)
        owner = self.owner(spot, self.me % 2)
        rows = self.rows
        for index, chunk in enumerate(self.chunks):
            lanes = slice(index * LANES, (index + 1) * LANES)
            value = self.block(owner, spot, 0, rows, index)
            value = value + self.x_in[:rows, lanes].astype(jnp.float32)
            value = value + self.y_in[:rows, lanes].astype(jnp.float32)
            self.z_out[:rows, lanes] = value.astype(jnp.bfloat16)

            @pl.when(self.z == self.layer)
            def _(value=value, chunk=chunk):
                self.total[:rows, chunk * LANES : (chunk + 1) * LANES] = value

        @pl.when(self.z != self.layer)
        def _():
            self.away(self.z).start()

        if self.tail:
            last = self.devices // 8 - 1
            for index in range(3):
                at = rows + 16 * index
                value = self.tail_block(spot, index)
                value = value + self.x_in[at : at + 16, :].astype(jnp.float32)
                value = value + self.y_in[at : at + 16, :].astype(jnp.float32)
                self.z_out[at : at + 16, :] = value.astype(jnp.bfloat16)
                self.tail_total[:, index * LANES : (index + 1) * LANES] = value

            @pl.when(self.z != last)
            def _():
                self.tail_away(self.z).start()

    def finish(self):
        last = self.devices // 8 - 1
        for made in self.copies.values():
            made.wait_send()

        @pl.when(self.z != self.layer)
        def _():
            self.away(self.z).wait_send()

        first, end = self.chunks[0] * LANES, (self.chunks[-1] + 1) * LANES
        for source in range(last + 1):
            if source != self.layer:

                @pl.when(self.z == self.layer)
                def _(source=source):
                    self.away(source).wait_recv()
                    self.total[: self.rows, first:end] += self.z_in[source, :, first:end].astype(jnp.float32)

        if self.tail:

            @pl.when(self.z != last)
            def _():
                self.tail_away(self.z).wait_send()

            for source in range(last):

                @pl.when(self.z == last)
                def _(source=source):
                    self.tail_away(source).wait_recv()
                    for index in range(3):
                        self.tail_total[:, index * LANES : (index + 1) * LANES] += self.tail_in[
                            source, 16 * index : 16 * index + 16, :
                        ].astype(jnp.float32)


def step_kernel(
    devices, share, tokens, cot, raw, result, grad_tokens, out,
    w_qkv, w_out, w_up, w_down, tail, shard, slots, pull_send, pull_recv,
    xbuf, dybuf, xhat, a16, qkv16, probs, o16, h, xhat2, c16, acc, dc, dy16, dh, dh16, do16, dqkv16,
    s1, s2, slope, lines, g_tail, total, tail_total, z_in, tail_in, send_sem, recv_sem, z_sem, tail_sem, *refs,
):
    me = lax.axis_index("dp")
    greet_partners(me, devices)
    early, late = units_of(devices, share)
    shared = (
        lines, g_tail, total, tail_total, z_in, tail_in, send_sem, recv_sem, z_sem, tail_sem,
    )
    units = [
        Unit(index, plan, devices, share, refs[index * 11 : index * 11 + 11], shared)
        for index, plan in enumerate(early + late)
    ]
    count = len(early)
    early, late = units[:count], units[count:]
    firsts = {unit: unit.layer * 8 * share // D for unit in early}
    down = [unit for unit in early if firsts[unit] >= 8 * D]
    up = [unit for unit in early if 4 * D <= firsts[unit] < 8 * D]
    mixed = [unit for unit in early if firsts[unit] < 4 * D]
    first, second, third = ([unit for unit in late if unit.chunks[0] == pair] for pair in range(3))

    align(share, raw, total, shard)
    wait_partners(devices)
    gather = Gather(devices, share, lines, shard, slots, pull_send, pull_recv)
    order = columns_of(devices)
    gather.begin(order)
    lines[...] = jnp.zeros_like(lines)
    load(tokens, xbuf)
    load(cot, dybuf)
    normalize(xbuf, xhat, s1)
    gather_weights(gather, order, w_qkv, w_out, w_up, w_down, tail)
    lines[:, TAIL:, :] = jnp.zeros_like(lines[:, TAIL:, :])
    attention_in(xhat, tail, a16, w_qkv, qkv16)
    attention(qkv16, probs, o16)
    middle(xbuf, o16, w_out, tail, h, xhat2, s2, c16, dybuf, dy16)
    feed_forward(c16, dy16, w_up, w_down, tail, acc, slope, lines)
    advance(down)
    feed_forward_back(c16, dy16, w_up, w_down, slope, dc, lines, g_tail)
    advance(up)
    advance(down)
    feed_forward_end(h, acc, tail, dc, xhat2, s2, dybuf, result, dh, dh16, g_tail)
    advance(up)
    attention_out_back(o16, dh16, w_out, lines, do16)
    advance(mixed)
    advance(down)
    g_tail[2:4, :] = jnp.zeros((2, D), jnp.float32)
    attention_back(0, qkv16, probs, do16, dqkv16, g_tail)
    advance(mixed)
    attention_in_back(0, a16, dqkv16, w_qkv, lines, acc)
    advance(first)
    advance(up)
    attention_back(1, qkv16, probs, do16, dqkv16, g_tail)
    advance(first)
    attention_in_back(1, a16, dqkv16, w_qkv, lines, acc)
    advance(second)
    advance(mixed)
    advance(down)
    attention_back(2, qkv16, probs, do16, dqkv16, g_tail)
    advance(second)
    attention_in_back(2, a16, dqkv16, w_qkv, lines, acc)
    input_sums(acc, xhat, g_tail)
    advance(third)
    advance(first)
    grad_input(acc, tail, xhat, s1, dh, grad_tokens)
    advance(up)
    advance(third)
    advance(second)
    advance(mixed)
    advance(first)
    advance(third)
    advance(second)
    advance(third)
    for unit in units:
        unit.finish()
    at = TAIL - (devices - 1) * share // D
    out[...] = total[0 : out.shape[0], :]

    @pl.when(me == devices - 1)
    def _():
        out[at : at + 12, :] = total[at : at + 12, :] + tail_total[0:12, :]


def advance(units):
    for unit in units:
        unit.advance()


def load(source, padded):
    for image in range(source.shape[1]):
        at = image * PAD
        padded[at + PAD - 16 : at + PAD, :] = jnp.zeros((16, D), jnp.float32)
        padded[at : at + SEQ, :] = source[:, image, :]


def normalize(xbuf, xhat, s1):
    for _, rows in images_of(xbuf):
        normed, factor = layer_norm(xbuf[rows, :])
        xhat[rows, :] = normed
        s1[rows, :] = factor


def attention_in(xhat, tail, a16, w_qkv, qkv16):
    for _, rows in images_of(xhat):
        a16[rows, :] = (xhat[rows, :] * tail[0:1, :] + tail[1:2, :]).astype(jnp.bfloat16)
    for piece in range(3):
        cols = slice(piece * D, (piece + 1) * D)
        value = dot_nn(a16[...], w_qkv[:, cols])
        if piece == 0:
            value = value + tail[2:3, :]
        if piece == 2:
            value = value + tail[3:4, :]
        qkv16[:, cols] = value.astype(jnp.bfloat16)


def half_of(values, half):
    lane = lax.broadcasted_iota(jnp.int32, values.shape, 1)
    return jnp.where((lane < 64) if half == 0 else (lane >= 64), values, jnp.zeros_like(values))


def views(step):
    image, pair = step // 3, step % 3
    rows = pl.ds(pl.multiple_of(image * PAD, 16), PAD)
    return rows, [pl.ds(pl.multiple_of(part * D + pair * 128, 128), 128) for part in range(3)]


def attention(qkv16, probs, o16):
    def body(step, carry):
        rows, (qs, ks, vs) = views(step)
        query, key, value = qkv16[rows, qs], qkv16[rows, ks], qkv16[rows, vs]
        total = None
        for half in range(2):
            scores = dot_nt(query, half_of(key, half)) * 0.125
            column = lax.broadcasted_iota(jnp.int32, scores.shape, 1)
            scores = jnp.where(column < SEQ, scores, -jnp.inf)
            raised = jnp.exp(scores - jnp.max(scores, axis=-1, keepdims=True))
            prob = raised / jnp.sum(raised, axis=-1, keepdims=True)
            probs[step * 2 + half] = prob
            term = dot_nn(prob.astype(jnp.bfloat16), half_of(value, half))
            total = term if total is None else total + term
        o16[rows, qs] = total.astype(jnp.bfloat16)
        return carry

    lax.fori_loop(0, qkv16.shape[0] // PAD * 3, body, 0, unroll=True)


def middle(xbuf, o16, w_out, tail, h, xhat2, s2, c16, dybuf, dy16):
    for _, rows in images_of(xbuf):
        value = xbuf[rows, :] + (dot_nn(o16[rows, :], w_out[...]) + tail[4:5, :])
        h[rows, :] = value
        normed, factor = layer_norm(value)
        xhat2[rows, :] = normed
        s2[rows, :] = factor
        c16[rows, :] = (normed * tail[5:6, :] + tail[6:7, :]).astype(jnp.bfloat16)
        dy16[rows, :] = dybuf[rows, :].astype(jnp.bfloat16)


def lanes_of(index, width):
    return slice(index * width, (index + 1) * width)


def feed_forward(c16, dy16, w_up, w_down, tail, acc, slope, lines):
    for line in range(FF // D):
        cols = lanes_of(line, D)
        pre = dot_nn(c16[...], w_up[:, cols]) + tail[8 + line : 9 + line, :]
        phi = 0.5 * (1.0 + lax.erf(pre * 0.7071067811865476))
        slope[:, cols] = phi + pre * jnp.exp(-0.5 * pre * pre) * 0.3989422804014327
        act = (pre * phi).astype(jnp.bfloat16)
        value = dot_nn(act, w_down[cols, :])
        acc[...] = value if line == 0 else acc[...] + value
        grad_down = dot_tn(act, dy16[...])
        first = 8 * D + line * D
        for chunk in range(D // LANES):
            lines[chunk, first : first + D, :] = grad_down[:, lanes_of(chunk, LANES)]


def feed_forward_back(c16, dy16, w_up, w_down, slope, dc, lines, g_tail):
    for line in range(FF // D):
        cols = lanes_of(line, D)
        grad_pre = dot_nt(dy16[...], w_down[cols, :]) * slope[:, cols]
        half = grad_pre.astype(jnp.bfloat16)
        grad_up = dot_tn(c16[...], half)
        for chunk in range(D // LANES):
            lines[chunk, pl.ds(4 * D + line, D, stride=4), :] = grad_up[:, lanes_of(chunk, LANES)]
        g_tail[8 + line : 9 + line, :] = column_sum(grad_pre)
        value = dot_nt(half, w_up[:, cols])
        dc[...] = value if line == 0 else dc[...] + value


def feed_forward_end(h, acc, tail, dc, xhat2, s2, dybuf, result, dh, dh16, g_tail):
    sums = [0.0] * 4
    for image, rows in images_of(h):
        value = h[rows, :] + (acc[rows, :] + tail[7:8, :])
        result[:, image, :] = value[:SEQ]
        grad, normed = dc[rows, :], xhat2[rows, :]
        hidden = dybuf[rows, :] + norm_back(grad * tail[5:6, :], normed, s2[rows, :])
        dh[rows, :] = hidden
        dh16[rows, :] = hidden.astype(jnp.bfloat16)
        terms = (hidden, grad * normed, grad, dybuf[rows, :])
        sums = [old + column_sum(new) for old, new in zip(sums, terms)]
    for index in range(4):
        g_tail[4 + index : 5 + index, :] = sums[index]
    g_tail[12:16, :] = jnp.zeros((4, D), jnp.float32)


def attention_out_back(o16, dh16, w_out, lines, do16):
    grad_out = dot_tn(o16[...], dh16[...])
    for chunk in range(D // LANES):
        lines[chunk, 3 * D : 4 * D, :] = grad_out[:, chunk * LANES : (chunk + 1) * LANES]
    do16[...] = dot_nt(dh16[...], w_out[...]).astype(jnp.bfloat16)


def attention_back(pair, qkv16, probs, do16, dqkv16, g_tail):
    def body(image, carry):
        step = image * 3 + pair
        rows, (qs, ks, vs) = views(step)
        query, key, value, grad = qkv16[rows, qs], qkv16[rows, ks], qkv16[rows, vs], do16[rows, qs]
        dq = dk = dv = None
        for half in range(2):
            prob = probs[step * 2 + half]
            dv_term = dot_tn(prob.astype(jnp.bfloat16), half_of(grad, half))
            grad_prob = dot_nt(grad, half_of(value, half))
            delta = jnp.sum(prob * grad_prob, axis=-1, keepdims=True)
            ds = (prob * (grad_prob - delta) * 0.125).astype(jnp.bfloat16)
            dq_term = dot_nn(ds, half_of(key, half))
            dk_term = dot_tn(ds, half_of(query, half))
            if half == 0:
                dq, dk, dv = dq_term, dk_term, dv_term
            else:
                dq, dk, dv = dq + dq_term, dk + dk_term, dv + dv_term
        dqkv16[rows, qs] = dq.astype(jnp.bfloat16)
        dqkv16[rows, ks] = dk.astype(jnp.bfloat16)
        dqkv16[rows, vs] = dv.astype(jnp.bfloat16)
        g_tail[2:3, qs] += column_sum(dq)
        g_tail[3:4, qs] += column_sum(dv)
        return carry

    lax.fori_loop(0, qkv16.shape[0] // PAD, body, 0, unroll=True)


def attention_in_back(pair, a16, dqkv16, w_qkv, lines, acc):
    parts = [slice(part * D + pair * LANES, part * D + (pair + 1) * LANES) for part in range(3)]
    grads = jnp.concatenate([dqkv16[:, part] for part in parts], axis=1)
    weights = jnp.concatenate([w_qkv[:, part] for part in parts], axis=1)
    grad_w = dot_tn(a16[...], grads)
    for part in range(3):
        lines[pair, pl.ds(part, D, stride=3), :] = grad_w[:, part * LANES : (part + 1) * LANES]
    value = dot_nt(grads, weights)
    acc[...] = value if pair == 0 else acc[...] + value


def input_sums(acc, xhat, g_tail):
    sums = [0.0] * 2
    for _, rows in images_of(acc):
        grad = acc[rows, :]
        sums = [old + column_sum(new) for old, new in zip(sums, (grad * xhat[rows, :], grad))]
    for index in range(2):
        g_tail[index : index + 1, :] = sums[index]


def grad_input(acc, tail, xhat, s1, dh, grad_tokens):
    for image, rows in images_of(acc):
        value = dh[rows, :] + norm_back(acc[rows, :] * tail[0:1, :], xhat[rows, :], s1[rows, :])
        grad_tokens[:, image, :] = value[:SEQ]


def compute_scratch(images):
    f32, bf16 = jnp.float32, jnp.bfloat16
    rows = images * PAD
    return [
        pltpu.VMEM((rows, D), f32),
        pltpu.VMEM((rows, D), f32),
        pltpu.VMEM((rows, D), f32),
        pltpu.VMEM((rows, D), bf16),
        pltpu.VMEM((rows, 3 * D), bf16),
        pltpu.VMEM((images * HEADS, PAD, PAD), f32),
        pltpu.VMEM((rows, D), bf16),
        pltpu.VMEM((rows, D), f32),
        pltpu.VMEM((rows, D), f32),
        pltpu.VMEM((rows, D), bf16),
        pltpu.VMEM((rows, D), f32),
        pltpu.VMEM((rows, D), f32),
        pltpu.VMEM((rows, D), bf16),
        pltpu.VMEM((rows, D), f32),
        pltpu.VMEM((rows, D), bf16),
        pltpu.VMEM((rows, D), bf16),
        pltpu.VMEM((rows, 3 * D), bf16),
        pltpu.VMEM((rows, 1), f32),
        pltpu.VMEM((rows, 1), f32),
        pltpu.VMEM((rows, FF), f32),
    ]


def compute(tokens, cotangent, raw, devices, share):
    f32, bf16 = jnp.float32, jnp.bfloat16
    rows, _ = row_plan(share)
    layers = devices // 8
    early, late = units_of(devices, share)
    count = len(early) + len(late)
    vmem = pl.BlockSpec(memory_space=pltpu.VMEM)
    result, grad_tokens, total = pl.pallas_call(
        functools.partial(step_kernel, devices, share),
        out_shape=(
            jax.ShapeDtypeStruct(tokens.shape, f32),
            jax.ShapeDtypeStruct(tokens.shape, f32),
            jax.ShapeDtypeStruct((rows, D), f32),
        ),
        in_specs=[vmem] * 3,
        out_specs=[vmem] * 3,
        scratch_shapes=[
            pltpu.VMEM((D, 3 * D), bf16),
            pltpu.VMEM((D, D), bf16),
            pltpu.VMEM((D, FF), bf16),
            pltpu.VMEM((FF, D), bf16),
            pltpu.VMEM((16, D), f32),
            pltpu.VMEM((rows, D), bf16),
            pltpu.VMEM((devices, rows, D), bf16),
            pltpu.SemaphoreType.DMA((8 * layers,)),
            pltpu.SemaphoreType.DMA((8 * layers,)),
        ]
        + compute_scratch(tokens.shape[1])
        + [
            pltpu.VMEM((D // LANES, LINES + rows + 24, LANES), f32),
            pltpu.VMEM((16, D), f32),
            pltpu.VMEM((rows + 8, D), f32),
            pltpu.VMEM((16, D), f32),
            pltpu.VMEM((layers, rows, D), jnp.bfloat16),
            pltpu.VMEM((layers, 48, LANES), jnp.bfloat16),
            pltpu.SemaphoreType.DMA((count, HOPS)),
            pltpu.SemaphoreType.DMA((count, HOPS)),
            pltpu.SemaphoreType.DMA((count, layers)),
            pltpu.SemaphoreType.DMA((layers,)),
        ]
        + unit_scratch(devices, share),
        compiler_params=pltpu.CompilerParams(
            collective_id=0, has_side_effects=True, vmem_limit_bytes=60 * 2**20
        ),
    )(tokens, cotangent, raw)
    offset = (lax.axis_index("dp") * share) % D
    return result, grad_tokens, lax.dynamic_slice(total.reshape(-1), (offset,), (share,))


def adamw(params, grads, first, second, position):
    first_end = 3 * D * D
    second_end = first_end + D * D
    third_end = second_end + D * FF
    fourth_end = third_end + FF * D
    rate = jnp.where(
        position < first_end,
        0.01,
        jnp.where(
            position < second_end,
            0.1,
            jnp.where(position < third_end, 0.01, jnp.where(position < fourth_end, 0.005, 0.1)),
        ),
    )
    first_new = 0.9 * first + 0.1 * grads
    second_new = 0.999 * second + 0.001 * grads * grads
    update = (
        first_new / (1.0 - 0.9**STEP) / (jnp.sqrt(second_new / (1.0 - 0.999**STEP)) + 1e-08)
        + 0.1 * params
    )
    return (params - rate * update, first_new, second_new)


def per_device(tokens, params, moment1, moment2, cotangent):
    devices = lax.axis_size("dp")
    length = params.shape[0]
    rows, _ = row_plan(length)
    raw = jnp.pad(params, (0, rows * D - length)).astype(jnp.bfloat16).reshape(rows, D)
    result, grad_tokens, shares = compute(
        tokens.transpose(1, 0, 2), cotangent.transpose(1, 0, 2), raw, devices, length
    )
    result, grad_tokens = result.transpose(1, 0, 2), grad_tokens.transpose(1, 0, 2)
    count = tokens.shape[0] * tokens.shape[1] * devices
    grad_params = shares * (1.0 / math.sqrt(count))
    position = lax.axis_index("dp") * length + jnp.arange(length, dtype=jnp.int32)
    new_params, new_first, new_second = adamw(params, grad_params, moment1, moment2, position)
    return (result, grad_tokens, grad_params, new_params, new_first, new_second)


def solution(mesh):
    in_specs = (P("dp", None, None), P("dp"), P("dp"), P("dp"), P("dp", None, None))
    out_specs = (P("dp", None, None), P("dp", None, None), P("dp"), P("dp"), P("dp"), P("dp"))
    return jax.shard_map(
        per_device, mesh=mesh, in_specs=in_specs, out_specs=out_specs, check_vma=False
    )
```

```python
import math

import jax
import jax.numpy as jnp
from jax import lax
from jax.experimental import pallas as pl
from jax.experimental.pallas import tpu as pltpu
import functools
from jax.sharding import PartitionSpec as P

D = 384
HEADS = 6
FF = 1536
SEQ = 197
STEP = 3


LANES = 128
LINES = 4 * 1152 + 12


def other(device, bit):
    step = 2**bit
    return device + step - 2 * step * ((device // step) % 2)


def flip(device, column):
    bit = 3
    while column:
        if column % 2:
            device = other(device, bit)
        column //= 2
        bit += 1
    return device


def slot_of(device, devices):
    return (device % 2) * (devices // 2) + device // 2


def partners_of(me, devices):
    return [other(me, bit) for bit in range(3)] + [flip(me, j) for j in range(1, devices // 8)]


def greet_partners(me, devices):
    for partner in partners_of(me, devices):
        pl.semaphore_signal(
            pltpu.get_barrier_semaphore(),
            inc=1,
            device_id=(partner,),
            device_id_type=pl.DeviceIdType.MESH,
        )


def wait_partners(devices):
    pl.semaphore_wait(pltpu.get_barrier_semaphore(), 2 + devices // 8)


def columns_of(devices):
    order = list(range(devices // 8))
    return [0, 1, 3, 2] if devices == 32 else order


def row_plan(share):
    rows = -(-(share + D - 1) // D)
    rows = -(-rows // 32) * 32
    return rows, rows // 2


COLUMN, ALONG_X, ALONG_Y, TURN_X, TURN_Y, CORE, LATER_X, LATER_Y = range(8)


def greet(me, bits):
    barrier = pltpu.get_barrier_semaphore()
    for bit in range(bits):
        pl.semaphore_signal(
            barrier, inc=1, device_id=(other(me, bit),), device_id_type=pl.DeviceIdType.MESH
        )
    pl.semaphore_wait(barrier, bits)


def align(share, raw, wide, mine):
    rows, _ = row_plan(share)
    offset = (lax.axis_index("dp") * share) % D
    source = lax.broadcasted_iota(jnp.int32, (D, 2 * D), 0)
    target = lax.broadcasted_iota(jnp.int32, (D, 2 * D), 1)
    moved = (target == source + offset).astype(jnp.bfloat16)
    both = jnp.dot(raw[...], moved, preferred_element_type=jnp.float32)
    wide[0:8, :] = jnp.zeros((8, D), jnp.float32)
    wide[8 : 8 + rows, :] = both[:, D:]
    mine[...] = (both[:, :D] + wide[7 : 7 + rows, :]).astype(jnp.bfloat16)


class Gather:
    def __init__(self, devices, share, lines, shard, slots, send_sem, recv_sem):
        self.devices, self.share = devices, share
        self.lines, self.shard, self.slots = lines, shard, slots
        self.send_sem, self.recv_sem = send_sem, recv_sem
        self.rows, self.half = row_plan(share)
        me = lax.axis_index("dp")
        self.me = me
        self.core, self.x_side, self.y_side = other(me, 0), other(me, 1), other(me, 2)
        self.copies = {}

    def copy(self, kind, column, source, target, device):
        spot = kind * (self.devices // 8) + column
        made = pltpu.make_async_remote_copy(
            src_ref=source,
            dst_ref=target,
            send_sem=self.send_sem.at[spot],
            recv_sem=self.recv_sem.at[spot],
            device_id=(device,),
            device_id_type=pl.DeviceIdType.MESH,
        )
        made.start()
        self.copies[kind, column] = made

    def send(self, kind, column, owner, begin, size, device):
        piece = self.slots.at[slot_of(owner, self.devices), pl.ds(begin, size)]
        self.copy(kind, column, piece, piece, device)

    def begin(self, order):
        mine = self.slots.at[slot_of(self.me, self.devices)]
        for index, column in enumerate(order[1:]):
            self.copy(COLUMN, column, self.shard, mine, flip(self.me, column))
            if index == 0:
                upper, lower = pl.ds(0, self.half), pl.ds(self.half, self.half)
                shard = self.shard
                self.copy(ALONG_X, 0, shard.at[upper], mine.at[upper], self.x_side)
                self.copy(ALONG_Y, 0, shard.at[lower], mine.at[lower], self.y_side)
                self.copy(LATER_X, 0, shard.at[lower], mine.at[lower], self.x_side)
                self.copy(LATER_Y, 0, shard.at[upper], mine.at[upper], self.y_side)
        mine[...] = self.shard[...]

    def along(self, column):
        self.copies[COLUMN, column].wait_recv()
        half, owner = self.half, flip(self.me, column)
        self.send(ALONG_X, column, owner, 0, half, self.x_side)
        self.send(ALONG_Y, column, owner, half, half, self.y_side)
        self.send(LATER_X, column, owner, half, half, self.x_side)
        self.send(LATER_Y, column, owner, 0, half, self.y_side)

    def turn(self, column):
        half = self.half
        self.copies[ALONG_X, column].wait_recv()
        self.send(TURN_Y, column, other(flip(self.me, column), 1), 0, half, self.y_side)
        self.copies[ALONG_Y, column].wait_recv()
        self.send(TURN_X, column, other(flip(self.me, column), 2), half, half, self.x_side)

    def across(self, column):
        self.copies[TURN_Y, column].wait_recv()
        self.copies[TURN_X, column].wait_recv()
        self.copies[LATER_X, column].wait_recv()
        self.copies[LATER_Y, column].wait_recv()
        first = (self.me % 2) * (self.devices // 2) + (flip(self.me, column) // 8) * 4
        layer = self.slots.at[pl.ds(first, 4)]
        self.copy(CORE, column, layer, layer, self.core)
        self.unpack(column, self.me % 2)

    def end(self, column):
        self.copies[CORE, column].wait_recv()
        self.unpack(column, 1 - self.me % 2)

    def unpack(self, column, core):
        layer = flip(self.me, column) // 8
        for spot in range(4):
            device = layer * 8 + spot * 2 + core
            where = pl.ds(device * self.share // D, self.rows)
            place = core * (self.devices // 2) + layer * 4 + spot
            for chunk in range(D // LANES):
                self.lines[chunk, where, :] += self.slots[
                    place, :, chunk * LANES : (chunk + 1) * LANES
                ].astype(jnp.float32)

    def finish(self):
        for made in self.copies.values():
            made.wait_send()


def gather_weights(gather, order, w_qkv, w_out, w_up, w_down, tail):
    count = len(order)
    for index in range(1, count + 3):
        if index < count:
            gather.along(order[index])
        if 0 <= index - 1 < count:
            gather.turn(order[index - 1])
        if 0 <= index - 2 < count:
            gather.across(order[index - 2])
        if 0 <= index - 3 < count:
            gather.end(order[index - 3])
    lines = gather.lines
    spread(lines, 0, w_qkv, 3)
    spread(lines, 1152, w_out, 1)
    spread(lines, 1536, w_up, 4)
    spread(lines, 3072, w_down, 1)
    spread(lines, 4608, tail, 1)
    gather.finish()


def spread(lines, first, out, times):
    height = out.shape[0]
    for column in range(times):
        for chunk in range(D // LANES):
            if times == 1:
                value = lines[chunk, first : first + height, :]
            else:
                value = lines[chunk, pl.ds(first + column, height, stride=times), :]
            at = column * D + chunk * LANES
            out[:, at : at + LANES] = value.astype(out.dtype)


PAD = 208


def dot_nn(left, right):
    return lax.dot_general(left, right, (((1,), (0,)), ((), ())), preferred_element_type=jnp.float32)


def dot_nt(left, right):
    return lax.dot_general(left, right, (((1,), (1,)), ((), ())), preferred_element_type=jnp.float32)


def dot_tn(left, right):
    return lax.dot_general(left, right, (((0,), (0,)), ((), ())), preferred_element_type=jnp.float32)


def layer_norm(values):
    center = values - jnp.mean(values, axis=-1, keepdims=True)
    factor = lax.rsqrt(jnp.mean(center * center, axis=-1, keepdims=True) + 1e-06)
    return center * factor, factor


def norm_back(grad_hat, normed, factor):
    return factor * (
        grad_hat
        - jnp.mean(grad_hat, axis=-1, keepdims=True)
        - normed * jnp.mean(grad_hat * normed, axis=-1, keepdims=True)
    )


def column_sum(values):
    return jnp.sum(values, axis=0, keepdims=True)


def images_of(padded):
    return [(image, slice(image * PAD, (image + 1) * PAD)) for image in range(padded.shape[0] // PAD)]


TAIL = 4608
HOPS = 9
TO_CORE, TURN_UP, TURN_LOW, TO_X, TO_Y, TO_LAYER, TAIL_OUT, SOON_X, SOON_Y = range(HOPS)


def units_of(devices, share):
    early, late = [], []
    for layer in range(devices // 8 - 1, -1, -1):
        if layer * 8 * share // D >= 3 * D:
            early.append((layer, (0, 1, 2), False))
        else:
            late.extend((layer, (chunk,), layer == 0 and chunk == 2) for chunk in range(3))
    late.sort(key=lambda unit: unit[1])
    return early, late


def unit_scratch(devices, share):
    rows, half = row_plan(share)
    early, late = units_of(devices, share)
    shapes = []
    for _, chunks, tail in early + late:
        wide = len(chunks) * LANES
        tall = rows + (48 if tail else 0)
        shapes += [(4, tall, wide)] * 2
        shapes += [(half, wide), (tall - half, wide)] * 2
        shapes += [(tall, wide)] * 5
    return [pltpu.VMEM(shape, jnp.bfloat16) for shape in shapes]


class Unit:
    def __init__(self, index, plan, devices, share, refs, shared):
        self.index, self.devices, self.share = index, devices, share
        self.layer, self.chunks, self.tail = plan
        (
            self.core_out, self.core_in, self.up_out, self.low_out, self.up_in, self.low_in,
            self.x_out, self.y_out, self.x_in, self.y_in, self.z_out,
        ) = refs
        (
            self.lines, self.g_tail, self.total, self.tail_total, self.z_in, self.tail_in,
            self.send_sem, self.recv_sem, self.z_sem, self.tail_sem,
        ) = shared
        self.rows, self.half = row_plan(share)
        self.stage = 0
        self.copies = {}
        me = lax.axis_index("dp")
        self.me = me
        self.z = me // 8
        self.core, self.x_side, self.y_side = other(me, 0), other(me, 1), other(me, 2)

    def copy(self, kind, source, target, device, recv=None):
        made = pltpu.make_async_remote_copy(
            src_ref=source,
            dst_ref=target,
            send_sem=self.send_sem.at[self.index, kind],
            recv_sem=self.recv_sem.at[self.index, kind] if recv is None else recv,
            device_id=(device,),
            device_id_type=pl.DeviceIdType.MESH,
        )
        return made

    def send(self, kind, source, target, device):
        self.copies[kind] = self.copy(kind, source, target, device)
        self.copies[kind].start()

    def advance(self):
        (self.pack, self.turn, self.along, self.arrive)[self.stage]()
        self.stage += 1

    def block(self, owner, spot, begin, end, index):
        first = owner * self.share // D
        chunk = self.chunks[index]
        lanes = slice(index * LANES, (index + 1) * LANES)
        value = self.lines[chunk, pl.ds(first + begin, end - begin), :]
        if spot is not None:
            value = value + self.core_in[spot, begin:end, lanes].astype(jnp.float32)
        return value

    def tail_block(self, spot, index):
        value = self.g_tail[:, index * LANES : (index + 1) * LANES]
        if spot is not None:
            at = self.rows + 16 * index
            value = value + self.core_in[spot, at : at + 16, :].astype(jnp.float32)
        return value

    def owner(self, spot, core):
        return self.layer * 8 + spot * 2 + core

    def pack(self):
        core = self.me % 2
        for spot in range(4):
            for index in range(len(self.chunks)):
                lanes = slice(index * LANES, (index + 1) * LANES)
                value = self.block(self.owner(spot, 1 - core), None, 0, self.rows, index)
                self.core_out[spot, : self.rows, lanes] = value.astype(jnp.bfloat16)
            if self.tail:
                for index in range(3):
                    at = self.rows + 16 * index
                    self.core_out[spot, at : at + 16, :] = self.tail_block(None, index).astype(
                        jnp.bfloat16
                    )
        self.send(TO_CORE, self.core_out, self.core_in, self.core)

    def spot_of(self, device):
        return device // 2 % 4

    def turn(self):
        self.copies[TO_CORE].wait_recv()
        spot = self.spot_of(other(self.x_side, 2))
        owner = self.owner(spot, self.me % 2)
        half, rows = self.half, self.rows
        for index in range(len(self.chunks)):
            lanes = slice(index * LANES, (index + 1) * LANES)
            self.up_out[:, lanes] = self.block(owner, spot, 0, half, index).astype(jnp.bfloat16)
            self.low_out[: rows - half, lanes] = self.block(
                owner, spot, half, rows, index
            ).astype(jnp.bfloat16)
        if self.tail:
            for index in range(3):
                at = rows - half + 16 * index
                self.low_out[at : at + 16, :] = self.tail_block(spot, index).astype(jnp.bfloat16)
        self.send(TURN_UP, self.up_out, self.up_in, self.y_side)
        self.send(TURN_LOW, self.low_out, self.low_in, self.x_side)
        self.soon(SOON_X, self.x_side, self.x_out, self.x_in, half, rows)
        self.soon(SOON_Y, self.y_side, self.y_out, self.y_in, 0, half)

    def soon(self, kind, device, out, into, begin, end):
        spot = self.spot_of(device)
        owner = self.owner(spot, self.me % 2)
        for index in range(len(self.chunks)):
            lanes = slice(index * LANES, (index + 1) * LANES)
            out[begin:end, lanes] = self.block(owner, spot, begin, end, index).astype(jnp.bfloat16)
        size = end - begin
        if self.tail and begin:
            size += 48
            for index in range(3):
                at = end + 16 * index
                out[at : at + 16, :] = self.tail_block(spot, index).astype(jnp.bfloat16)
        self.send(kind, out.at[pl.ds(begin, size)], into.at[pl.ds(begin, size)], device)

    def along(self):
        half, rows = self.half, self.rows
        tall = rows - half + (48 if self.tail else 0)
        for kind, device, out, into, begin, end, size in (
            (TURN_UP, self.x_side, self.x_out, self.x_in, 0, half, half),
            (TURN_LOW, self.y_side, self.y_out, self.y_in, half, rows, tall),
        ):
            self.copies[kind].wait_recv()
            spot = self.spot_of(device)
            owner = self.owner(spot, self.me % 2)
            turned = self.up_in if kind == TURN_UP else self.low_in
            for index in range(len(self.chunks)):
                lanes = slice(index * LANES, (index + 1) * LANES)
                value = self.block(owner, spot, begin, end, index)
                value = value + turned[: end - begin, lanes].astype(jnp.float32)
                out[begin:end, lanes] = value.astype(jnp.bfloat16)
            if self.tail and begin:
                for index in range(3):
                    at = rows + 16 * index
                    value = self.tail_block(spot, index)
                    value = value + turned[at - half : at - half + 16, :].astype(jnp.float32)
                    out[at : at + 16, :] = value.astype(jnp.bfloat16)
            self.send(
                TO_X if kind == TURN_UP else TO_Y,
                out.at[pl.ds(begin, size)],
                into.at[pl.ds(begin, size)],
                device,
            )

    def away(self, source):
        first, last = self.chunks[0] * LANES, (self.chunks[-1] + 1) * LANES
        return self.copy(
            TO_LAYER,
            self.z_out.at[pl.ds(0, self.rows)],
            self.z_in.at[source, :, pl.ds(first, last - first)],
            self.layer * 8 + self.me % 8,
            self.z_sem.at[self.index, source],
        )

    def tail_away(self, source):
        return self.copy(
            TAIL_OUT,
            self.z_out.at[pl.ds(self.rows, 48)],
            self.tail_in.at[source],
            self.devices - 8 + self.me % 8,
            self.tail_sem.at[source],
        )

    def arrive(self):
        for kind in (TO_X, TO_Y, SOON_X, SOON_Y):
            self.copies[kind].wait_recv()
        spot = self.spot_of(self.me)
        owner = self.owner(spot, self.me % 2)
        rows = self.rows
        for index, chunk in enumerate(self.chunks):
            lanes = slice(index * LANES, (index + 1) * LANES)
            value = self.block(owner, spot, 0, rows, index)
            value = value + self.x_in[:rows, lanes].astype(jnp.float32)
            value = value + self.y_in[:rows, lanes].astype(jnp.float32)
            self.z_out[:rows, lanes] = value.astype(jnp.bfloat16)

            @pl.when(self.z == self.layer)
            def _(value=value, chunk=chunk):
                self.total[:rows, chunk * LANES : (chunk + 1) * LANES] = value

        @pl.when(self.z != self.layer)
        def _():
            self.away(self.z).start()

        if self.tail:
            last = self.devices // 8 - 1
            for index in range(3):
                at = rows + 16 * index
                value = self.tail_block(spot, index)
                value = value + self.x_in[at : at + 16, :].astype(jnp.float32)
                value = value + self.y_in[at : at + 16, :].astype(jnp.float32)
                self.z_out[at : at + 16, :] = value.astype(jnp.bfloat16)
                self.tail_total[:, index * LANES : (index + 1) * LANES] = value

            @pl.when(self.z != last)
            def _():
                self.tail_away(self.z).start()

    def finish(self):
        last = self.devices // 8 - 1
        for made in self.copies.values():
            made.wait_send()

        @pl.when(self.z != self.layer)
        def _():
            self.away(self.z).wait_send()

        first, end = self.chunks[0] * LANES, (self.chunks[-1] + 1) * LANES
        for source in range(last + 1):
            if source != self.layer:

                @pl.when(self.z == self.layer)
                def _(source=source):
                    self.away(source).wait_recv()
                    self.total[: self.rows, first:end] += self.z_in[source, :, first:end].astype(jnp.float32)

        if self.tail:

            @pl.when(self.z != last)
            def _():
                self.tail_away(self.z).wait_send()

            for source in range(last):

                @pl.when(self.z == last)
                def _(source=source):
                    self.tail_away(source).wait_recv()
                    for index in range(3):
                        self.tail_total[:, index * LANES : (index + 1) * LANES] += self.tail_in[
                            source, 16 * index : 16 * index + 16, :
                        ].astype(jnp.float32)


def step_kernel(
    devices, share, tokens, cot, raw, result, grad_tokens, out,
    w_qkv, w_out, w_up, w_down, tail, shard, slots, pull_send, pull_recv,
    xbuf, dybuf, xhat, a16, qkv16, probs, o16, h, xhat2, c16, acc, dc, dy16, dh, dh16, do16, dqkv16,
    s1, s2, slope, lines, g_tail, total, tail_total, z_in, tail_in, send_sem, recv_sem, z_sem, tail_sem, *refs,
):
    me = lax.axis_index("dp")
    greet_partners(me, devices)
    early, late = units_of(devices, share)
    shared = (
        lines, g_tail, total, tail_total, z_in, tail_in, send_sem, recv_sem, z_sem, tail_sem,
    )
    units = [
        Unit(index, plan, devices, share, refs[index * 11 : index * 11 + 11], shared)
        for index, plan in enumerate(early + late)
    ]
    count = len(early)
    early, late = units[:count], units[count:]
    firsts = {unit: unit.layer * 8 * share // D for unit in early}
    down = [unit for unit in early if firsts[unit] >= 8 * D]
    up = [unit for unit in early if 4 * D <= firsts[unit] < 8 * D]
    mixed = [unit for unit in early if firsts[unit] < 4 * D]
    first, second, third = ([unit for unit in late if unit.chunks[0] == pair] for pair in range(3))

    align(share, raw, total, shard)
    wait_partners(devices)
    gather = Gather(devices, share, lines, shard, slots, pull_send, pull_recv)
    order = columns_of(devices)
    gather.begin(order)
    lines[...] = jnp.zeros_like(lines)
    load(tokens, xbuf)
    load(cot, dybuf)
    normalize(xbuf, xhat, s1)
    gather_weights(gather, order, w_qkv, w_out, w_up, w_down, tail)
    lines[:, TAIL:, :] = jnp.zeros_like(lines[:, TAIL:, :])
    attention_in(xhat, tail, a16, w_qkv, qkv16)
    attention(qkv16, probs, o16)
    middle(xbuf, o16, w_out, tail, h, xhat2, s2, c16, dybuf, dy16)
    feed_forward(c16, dy16, w_up, w_down, tail, acc, slope, lines)
    advance(down)
    feed_forward_back(0, c16, dy16, w_up, w_down, slope, dc, lines, g_tail)
    feed_forward_back(1, c16, dy16, w_up, w_down, slope, dc, lines, g_tail)
    advance(down)
    feed_forward_back(2, c16, dy16, w_up, w_down, slope, dc, lines, g_tail)
    feed_forward_back(3, c16, dy16, w_up, w_down, slope, dc, lines, g_tail)
    advance(up)
    feed_forward_end(h, acc, tail, dc, xhat2, s2, dybuf, result, dh, dh16, g_tail)
    g_tail[2:4, :] = jnp.zeros((2, D), jnp.float32)
    advance(down)
    advance(up)
    attention_out_back(o16, dh16, w_out, lines, do16)
    advance(mixed)
    attention_back(0, qkv16, probs, do16, dqkv16, g_tail)
    advance(down)
    advance(mixed)
    attention_in_back(0, a16, dqkv16, w_qkv, lines, acc)
    advance(first)
    advance(up)
    attention_back(1, qkv16, probs, do16, dqkv16, g_tail)
    advance(first)
    attention_in_back(1, a16, dqkv16, w_qkv, lines, acc)
    advance(second)
    advance(mixed)
    attention_back(2, qkv16, probs, do16, dqkv16, g_tail)
    advance(second)
    attention_in_back(2, a16, dqkv16, w_qkv, lines, acc)
    input_sums(acc, xhat, g_tail)
    advance(third)
    advance(first)
    grad_input(acc, tail, xhat, s1, dh, grad_tokens)
    advance(up)
    advance(third)
    advance(second)
    advance(mixed)
    advance(first)
    advance(third)
    advance(second)
    advance(third)
    for unit in units:
        unit.finish()
    at = TAIL - (devices - 1) * share // D
    out[...] = total[0 : out.shape[0], :]

    @pl.when(me == devices - 1)
    def _():
        out[at : at + 12, :] = total[at : at + 12, :] + tail_total[0:12, :]


def advance(units):
    for unit in units:
        unit.advance()


def load(source, padded):
    for image in range(source.shape[1]):
        at = image * PAD
        padded[at + PAD - 16 : at + PAD, :] = jnp.zeros((16, D), jnp.float32)
        padded[at : at + SEQ, :] = source[:, image, :]


def normalize(xbuf, xhat, s1):
    for _, rows in images_of(xbuf):
        normed, factor = layer_norm(xbuf[rows, :])
        xhat[rows, :] = normed
        s1[rows, :] = factor


def attention_in(xhat, tail, a16, w_qkv, qkv16):
    for _, rows in images_of(xhat):
        a16[rows, :] = (xhat[rows, :] * tail[0:1, :] + tail[1:2, :]).astype(jnp.bfloat16)
    for piece in range(3):
        cols = slice(piece * D, (piece + 1) * D)
        value = dot_nn(a16[...], w_qkv[:, cols])
        if piece == 0:
            value = value + tail[2:3, :]
        if piece == 2:
            value = value + tail[3:4, :]
        qkv16[:, cols] = value.astype(jnp.bfloat16)


def half_of(values, half):
    lane = lax.broadcasted_iota(jnp.int32, values.shape, 1)
    return jnp.where((lane < 64) if half == 0 else (lane >= 64), values, jnp.zeros_like(values))


def views(step):
    image, pair = step // 3, step % 3
    rows = pl.ds(pl.multiple_of(image * PAD, 16), PAD)
    return rows, [pl.ds(pl.multiple_of(part * D + pair * 128, 128), 128) for part in range(3)]


def attention(qkv16, probs, o16):
    def body(step, carry):
        rows, (qs, ks, vs) = views(step)
        query, key, value = qkv16[rows, qs], qkv16[rows, ks], qkv16[rows, vs]
        total = None
        for half in range(2):
            scores = dot_nt(query, half_of(key, half)) * 0.125
            column = lax.broadcasted_iota(jnp.int32, scores.shape, 1)
            scores = jnp.where(column < SEQ, scores, -jnp.inf)
            raised = jnp.exp(scores - jnp.max(scores, axis=-1, keepdims=True))
            prob = raised / jnp.sum(raised, axis=-1, keepdims=True)
            probs[step * 2 + half] = prob
            term = dot_nn(prob.astype(jnp.bfloat16), half_of(value, half))
            total = term if total is None else total + term
        o16[rows, qs] = total.astype(jnp.bfloat16)
        return carry

    lax.fori_loop(0, qkv16.shape[0] // PAD * 3, body, 0, unroll=True)


def middle(xbuf, o16, w_out, tail, h, xhat2, s2, c16, dybuf, dy16):
    for _, rows in images_of(xbuf):
        value = xbuf[rows, :] + (dot_nn(o16[rows, :], w_out[...]) + tail[4:5, :])
        h[rows, :] = value
        normed, factor = layer_norm(value)
        xhat2[rows, :] = normed
        s2[rows, :] = factor
        c16[rows, :] = (normed * tail[5:6, :] + tail[6:7, :]).astype(jnp.bfloat16)
        dy16[rows, :] = dybuf[rows, :].astype(jnp.bfloat16)


def lanes_of(index, width):
    return slice(index * width, (index + 1) * width)


def feed_forward(c16, dy16, w_up, w_down, tail, acc, slope, lines):
    for line in range(FF // D):
        cols = lanes_of(line, D)
        pre = dot_nn(c16[...], w_up[:, cols]) + tail[8 + line : 9 + line, :]
        phi = 0.5 * (1.0 + lax.erf(pre * 0.7071067811865476))
        slope[:, cols] = phi + pre * jnp.exp(-0.5 * pre * pre) * 0.3989422804014327
        act = (pre * phi).astype(jnp.bfloat16)
        value = dot_nn(act, w_down[cols, :])
        acc[...] = value if line == 0 else acc[...] + value
        grad_down = dot_tn(act, dy16[...])
        first = 8 * D + line * D
        for chunk in range(D // LANES):
            lines[chunk, first : first + D, :] = grad_down[:, lanes_of(chunk, LANES)]


def feed_forward_back(line, c16, dy16, w_up, w_down, slope, dc, lines, g_tail):
    cols = lanes_of(line, D)
    grad_pre = dot_nt(dy16[...], w_down[cols, :]) * slope[:, cols]
    half = grad_pre.astype(jnp.bfloat16)
    grad_up = dot_tn(c16[...], half)
    for chunk in range(D // LANES):
        lines[chunk, pl.ds(4 * D + line, D, stride=4), :] = grad_up[:, lanes_of(chunk, LANES)]
    g_tail[8 + line : 9 + line, :] = column_sum(grad_pre)
    value = dot_nt(half, w_up[:, cols])
    dc[...] = value if line == 0 else dc[...] + value


def feed_forward_end(h, acc, tail, dc, xhat2, s2, dybuf, result, dh, dh16, g_tail):
    sums = [0.0] * 4
    for image, rows in images_of(h):
        value = h[rows, :] + (acc[rows, :] + tail[7:8, :])
        result[:, image, :] = value[:SEQ]
        grad, normed = dc[rows, :], xhat2[rows, :]
        hidden = dybuf[rows, :] + norm_back(grad * tail[5:6, :], normed, s2[rows, :])
        dh[rows, :] = hidden
        dh16[rows, :] = hidden.astype(jnp.bfloat16)
        terms = (hidden, grad * normed, grad, dybuf[rows, :])
        sums = [old + column_sum(new) for old, new in zip(sums, terms)]
    for index in range(4):
        g_tail[4 + index : 5 + index, :] = sums[index]
    g_tail[12:16, :] = jnp.zeros((4, D), jnp.float32)


def attention_out_back(o16, dh16, w_out, lines, do16):
    grad_out = dot_tn(o16[...], dh16[...])
    for chunk in range(D // LANES):
        lines[chunk, 3 * D : 4 * D, :] = grad_out[:, chunk * LANES : (chunk + 1) * LANES]
    do16[...] = dot_nt(dh16[...], w_out[...]).astype(jnp.bfloat16)


def attention_back(pair, qkv16, probs, do16, dqkv16, g_tail):
    def body(image, carry):
        step = image * 3 + pair
        rows, (qs, ks, vs) = views(step)
        query, key, value, grad = qkv16[rows, qs], qkv16[rows, ks], qkv16[rows, vs], do16[rows, qs]
        dq = dk = dv = None
        for half in range(2):
            prob = probs[step * 2 + half]
            dv_term = dot_tn(prob.astype(jnp.bfloat16), half_of(grad, half))
            grad_prob = dot_nt(grad, half_of(value, half))
            delta = jnp.sum(prob * grad_prob, axis=-1, keepdims=True)
            ds = (prob * (grad_prob - delta) * 0.125).astype(jnp.bfloat16)
            dq_term = dot_nn(ds, half_of(key, half))
            dk_term = dot_tn(ds, half_of(query, half))
            if half == 0:
                dq, dk, dv = dq_term, dk_term, dv_term
            else:
                dq, dk, dv = dq + dq_term, dk + dk_term, dv + dv_term
        dqkv16[rows, qs] = dq.astype(jnp.bfloat16)
        dqkv16[rows, ks] = dk.astype(jnp.bfloat16)
        dqkv16[rows, vs] = dv.astype(jnp.bfloat16)
        g_tail[2:3, qs] += column_sum(dq)
        g_tail[3:4, qs] += column_sum(dv)
        return carry

    lax.fori_loop(0, qkv16.shape[0] // PAD, body, 0, unroll=True)


def attention_in_back(pair, a16, dqkv16, w_qkv, lines, acc):
    parts = [slice(part * D + pair * LANES, part * D + (pair + 1) * LANES) for part in range(3)]
    grads = jnp.concatenate([dqkv16[:, part] for part in parts], axis=1)
    weights = jnp.concatenate([w_qkv[:, part] for part in parts], axis=1)
    grad_w = dot_tn(a16[...], grads)
    for part in range(3):
        lines[pair, pl.ds(part, D, stride=3), :] = grad_w[:, part * LANES : (part + 1) * LANES]
    value = dot_nt(grads, weights)
    acc[...] = value if pair == 0 else acc[...] + value


def input_sums(acc, xhat, g_tail):
    sums = [0.0] * 2
    for _, rows in images_of(acc):
        grad = acc[rows, :]
        sums = [old + column_sum(new) for old, new in zip(sums, (grad * xhat[rows, :], grad))]
    for index in range(2):
        g_tail[index : index + 1, :] = sums[index]


def grad_input(acc, tail, xhat, s1, dh, grad_tokens):
    for image, rows in images_of(acc):
        value = dh[rows, :] + norm_back(acc[rows, :] * tail[0:1, :], xhat[rows, :], s1[rows, :])
        grad_tokens[:, image, :] = value[:SEQ]


def compute_scratch(images):
    f32, bf16 = jnp.float32, jnp.bfloat16
    rows = images * PAD
    return [
        pltpu.VMEM((rows, D), f32),
        pltpu.VMEM((rows, D), f32),
        pltpu.VMEM((rows, D), f32),
        pltpu.VMEM((rows, D), bf16),
        pltpu.VMEM((rows, 3 * D), bf16),
        pltpu.VMEM((images * HEADS, PAD, PAD), f32),
        pltpu.VMEM((rows, D), bf16),
        pltpu.VMEM((rows, D), f32),
        pltpu.VMEM((rows, D), f32),
        pltpu.VMEM((rows, D), bf16),
        pltpu.VMEM((rows, D), f32),
        pltpu.VMEM((rows, D), f32),
        pltpu.VMEM((rows, D), bf16),
        pltpu.VMEM((rows, D), f32),
        pltpu.VMEM((rows, D), bf16),
        pltpu.VMEM((rows, D), bf16),
        pltpu.VMEM((rows, 3 * D), bf16),
        pltpu.VMEM((rows, 1), f32),
        pltpu.VMEM((rows, 1), f32),
        pltpu.VMEM((rows, FF), f32),
    ]


def compute(tokens, cotangent, raw, devices, share):
    f32, bf16 = jnp.float32, jnp.bfloat16
    rows, _ = row_plan(share)
    layers = devices // 8
    early, late = units_of(devices, share)
    count = len(early) + len(late)
    vmem = pl.BlockSpec(memory_space=pltpu.VMEM)
    result, grad_tokens, total = pl.pallas_call(
        functools.partial(step_kernel, devices, share),
        out_shape=(
            jax.ShapeDtypeStruct(tokens.shape, f32),
            jax.ShapeDtypeStruct(tokens.shape, f32),
            jax.ShapeDtypeStruct((rows, D), f32),
        ),
        in_specs=[vmem] * 3,
        out_specs=[vmem] * 3,
        scratch_shapes=[
            pltpu.VMEM((D, 3 * D), bf16),
            pltpu.VMEM((D, D), bf16),
            pltpu.VMEM((D, FF), bf16),
            pltpu.VMEM((FF, D), bf16),
            pltpu.VMEM((16, D), f32),
            pltpu.VMEM((rows, D), bf16),
            pltpu.VMEM((devices, rows, D), bf16),
            pltpu.SemaphoreType.DMA((8 * layers,)),
            pltpu.SemaphoreType.DMA((8 * layers,)),
        ]
        + compute_scratch(tokens.shape[1])
        + [
            pltpu.VMEM((D // LANES, LINES + rows + 24, LANES), f32),
            pltpu.VMEM((16, D), f32),
            pltpu.VMEM((rows + 8, D), f32),
            pltpu.VMEM((16, D), f32),
            pltpu.VMEM((layers, rows, D), jnp.bfloat16),
            pltpu.VMEM((layers, 48, LANES), jnp.bfloat16),
            pltpu.SemaphoreType.DMA((count, HOPS)),
            pltpu.SemaphoreType.DMA((count, HOPS)),
            pltpu.SemaphoreType.DMA((count, layers)),
            pltpu.SemaphoreType.DMA((layers,)),
        ]
        + unit_scratch(devices, share),
        compiler_params=pltpu.CompilerParams(
            collective_id=0, has_side_effects=True, vmem_limit_bytes=60 * 2**20
        ),
    )(tokens, cotangent, raw)
    offset = (lax.axis_index("dp") * share) % D
    return result, grad_tokens, lax.dynamic_slice(total.reshape(-1), (offset,), (share,))


def adamw(params, grads, first, second, position):
    first_end = 3 * D * D
    second_end = first_end + D * D
    third_end = second_end + D * FF
    fourth_end = third_end + FF * D
    rate = jnp.where(
        position < first_end,
        0.01,
        jnp.where(
            position < second_end,
            0.1,
            jnp.where(position < third_end, 0.01, jnp.where(position < fourth_end, 0.005, 0.1)),
        ),
    )
    first_new = 0.9 * first + 0.1 * grads
    second_new = 0.999 * second + 0.001 * grads * grads
    update = (
        first_new / (1.0 - 0.9**STEP) / (jnp.sqrt(second_new / (1.0 - 0.999**STEP)) + 1e-08)
        + 0.1 * params
    )
    return (params - rate * update, first_new, second_new)


def per_device(tokens, params, moment1, moment2, cotangent):
    devices = lax.axis_size("dp")
    length = params.shape[0]
    rows, _ = row_plan(length)
    raw = jnp.pad(params, (0, rows * D - length)).astype(jnp.bfloat16).reshape(rows, D)
    result, grad_tokens, shares = compute(
        tokens.transpose(1, 0, 2), cotangent.transpose(1, 0, 2), raw, devices, length
    )
    result, grad_tokens = result.transpose(1, 0, 2), grad_tokens.transpose(1, 0, 2)
    count = tokens.shape[0] * tokens.shape[1] * devices
    grad_params = shares * (1.0 / math.sqrt(count))
    position = lax.axis_index("dp") * length + jnp.arange(length, dtype=jnp.int32)
    new_params, new_first, new_second = adamw(params, grad_params, moment1, moment2, position)
    return (result, grad_tokens, grad_params, new_params, new_first, new_second)


def solution(mesh):
    in_specs = (P("dp", None, None), P("dp"), P("dp"), P("dp"), P("dp", None, None))
    out_specs = (P("dp", None, None), P("dp", None, None), P("dp"), P("dp"), P("dp"), P("dp"))
    return jax.shard_map(
        per_device, mesh=mesh, in_specs=in_specs, out_specs=out_specs, check_vma=False
    )
```

```python
import math

import jax
import jax.numpy as jnp
from jax import lax
from jax.experimental import pallas as pl
from jax.experimental.pallas import tpu as pltpu
import functools
from jax.sharding import PartitionSpec as P

D = 384
HEADS = 6
FF = 1536
SEQ = 197
STEP = 3


LANES = 128
LINES = 4 * 1152 + 12


def other(device, bit):
    step = 2**bit
    return device + step - 2 * step * ((device // step) % 2)


def flip(device, column):
    bit = 3
    while column:
        if column % 2:
            device = other(device, bit)
        column //= 2
        bit += 1
    return device


def slot_of(device, devices):
    return (device % 2) * (devices // 2) + device // 2


def partners_of(me, devices):
    return [other(me, bit) for bit in range(3)] + [flip(me, j) for j in range(1, devices // 8)]


def greet_partners(me, devices):
    for partner in partners_of(me, devices):
        pl.semaphore_signal(
            pltpu.get_barrier_semaphore(),
            inc=1,
            device_id=(partner,),
            device_id_type=pl.DeviceIdType.MESH,
        )


def wait_partners(devices):
    pl.semaphore_wait(pltpu.get_barrier_semaphore(), 2 + devices // 8)


def columns_of(devices):
    order = list(range(devices // 8))
    return [0, 1, 3, 2] if devices == 32 else order


def row_plan(share):
    rows = -(-(share + D - 1) // D)
    rows = -(-rows // 32) * 32
    return rows, rows // 2


COLUMN, ALONG_X, ALONG_Y, TURN_X, TURN_Y, CORE, LATER_X, LATER_Y = range(8)


def greet(me, bits):
    barrier = pltpu.get_barrier_semaphore()
    for bit in range(bits):
        pl.semaphore_signal(
            barrier, inc=1, device_id=(other(me, bit),), device_id_type=pl.DeviceIdType.MESH
        )
    pl.semaphore_wait(barrier, bits)


def align(share, raw, wide, mine):
    rows, _ = row_plan(share)
    offset = (lax.axis_index("dp") * share) % D
    source = lax.broadcasted_iota(jnp.int32, (D, 2 * D), 0)
    target = lax.broadcasted_iota(jnp.int32, (D, 2 * D), 1)
    moved = (target == source + offset).astype(jnp.bfloat16)
    chunks = D // LANES
    value = jnp.concatenate(
        [raw[pl.ds(chunk, rows, stride=chunks), :] for chunk in range(chunks)], axis=1
    )
    both = jnp.dot(value.astype(jnp.bfloat16), moved, preferred_element_type=jnp.float32)
    wide[0:8, :] = jnp.zeros((8, D), jnp.float32)
    wide[8 : 8 + rows, :] = both[:, D:]
    mine[...] = (both[:, :D] + wide[7 : 7 + rows, :]).astype(jnp.bfloat16)


class Gather:
    def __init__(self, devices, share, lines, shard, slots, send_sem, recv_sem):
        self.devices, self.share = devices, share
        self.lines, self.shard, self.slots = lines, shard, slots
        self.send_sem, self.recv_sem = send_sem, recv_sem
        self.rows, self.half = row_plan(share)
        me = lax.axis_index("dp")
        self.me = me
        self.core, self.x_side, self.y_side = other(me, 0), other(me, 1), other(me, 2)
        self.copies = {}

    def copy(self, kind, column, source, target, device):
        spot = kind * (self.devices // 8) + column
        made = pltpu.make_async_remote_copy(
            src_ref=source,
            dst_ref=target,
            send_sem=self.send_sem.at[spot],
            recv_sem=self.recv_sem.at[spot],
            device_id=(device,),
            device_id_type=pl.DeviceIdType.MESH,
        )
        made.start()
        self.copies[kind, column] = made

    def send(self, kind, column, owner, begin, size, device):
        piece = self.slots.at[slot_of(owner, self.devices), pl.ds(begin, size)]
        self.copy(kind, column, piece, piece, device)

    def begin(self, order):
        mine = self.slots.at[slot_of(self.me, self.devices)]
        for index, column in enumerate(order[1:]):
            self.copy(COLUMN, column, self.shard, mine, flip(self.me, column))
            if index == 0:
                upper, lower = pl.ds(0, self.half), pl.ds(self.half, self.half)
                shard = self.shard
                self.copy(ALONG_X, 0, shard.at[upper], mine.at[upper], self.x_side)
                self.copy(ALONG_Y, 0, shard.at[lower], mine.at[lower], self.y_side)
                self.copy(LATER_X, 0, shard.at[lower], mine.at[lower], self.x_side)
                self.copy(LATER_Y, 0, shard.at[upper], mine.at[upper], self.y_side)
        mine[...] = self.shard[...]

    def along(self, column):
        self.copies[COLUMN, column].wait_recv()
        half, owner = self.half, flip(self.me, column)
        self.send(ALONG_X, column, owner, 0, half, self.x_side)
        self.send(ALONG_Y, column, owner, half, half, self.y_side)
        self.send(LATER_X, column, owner, half, half, self.x_side)
        self.send(LATER_Y, column, owner, 0, half, self.y_side)

    def turn(self, column):
        half = self.half
        self.copies[ALONG_X, column].wait_recv()
        self.send(TURN_Y, column, other(flip(self.me, column), 1), 0, half, self.y_side)
        self.copies[ALONG_Y, column].wait_recv()
        self.send(TURN_X, column, other(flip(self.me, column), 2), half, half, self.x_side)

    def across(self, column):
        self.copies[TURN_Y, column].wait_recv()
        self.copies[TURN_X, column].wait_recv()
        self.copies[LATER_X, column].wait_recv()
        self.copies[LATER_Y, column].wait_recv()
        first = (self.me % 2) * (self.devices // 2) + (flip(self.me, column) // 8) * 4
        layer = self.slots.at[pl.ds(first, 4)]
        self.copy(CORE, column, layer, layer, self.core)
        self.unpack(column, self.me % 2)

    def end(self, column):
        self.copies[CORE, column].wait_recv()
        self.unpack(column, 1 - self.me % 2)

    def unpack(self, column, core):
        layer = flip(self.me, column) // 8
        for spot in range(4):
            device = layer * 8 + spot * 2 + core
            where = pl.ds(device * self.share // D, self.rows)
            place = core * (self.devices // 2) + layer * 4 + spot
            for chunk in range(D // LANES):
                self.lines[chunk, where, :] += self.slots[
                    place, :, chunk * LANES : (chunk + 1) * LANES
                ].astype(jnp.float32)

    def finish(self):
        for made in self.copies.values():
            made.wait_send()


def gather_weights(gather, order, w_qkv, w_out, w_up, w_down, tail):
    count = len(order)
    for index in range(1, count + 3):
        if index < count:
            gather.along(order[index])
        if 0 <= index - 1 < count:
            gather.turn(order[index - 1])
        if 0 <= index - 2 < count:
            gather.across(order[index - 2])
        if 0 <= index - 3 < count:
            gather.end(order[index - 3])
    lines = gather.lines
    spread(lines, 0, w_qkv, 3)
    spread(lines, 1152, w_out, 1)
    spread(lines, 1536, w_up, 4)
    spread(lines, 3072, w_down, 1)
    spread(lines, 4608, tail, 1)
    gather.finish()


def spread(lines, first, out, times):
    height = out.shape[0]
    for column in range(times):
        for chunk in range(D // LANES):
            if times == 1:
                value = lines[chunk, first : first + height, :]
            else:
                value = lines[chunk, pl.ds(first + column, height, stride=times), :]
            at = column * D + chunk * LANES
            out[:, at : at + LANES] = value.astype(out.dtype)


PAD = 208


def dot_nn(left, right):
    return lax.dot_general(left, right, (((1,), (0,)), ((), ())), preferred_element_type=jnp.float32)


def dot_nt(left, right):
    return lax.dot_general(left, right, (((1,), (1,)), ((), ())), preferred_element_type=jnp.float32)


def dot_tn(left, right):
    return lax.dot_general(left, right, (((0,), (0,)), ((), ())), preferred_element_type=jnp.float32)


def layer_norm(values):
    center = values - jnp.mean(values, axis=-1, keepdims=True)
    factor = lax.rsqrt(jnp.mean(center * center, axis=-1, keepdims=True) + 1e-06)
    return center * factor, factor


def norm_back(grad_hat, normed, factor):
    return factor * (
        grad_hat
        - jnp.mean(grad_hat, axis=-1, keepdims=True)
        - normed * jnp.mean(grad_hat * normed, axis=-1, keepdims=True)
    )


def column_sum(values):
    return jnp.sum(values, axis=0, keepdims=True)


def images_of(padded):
    return [(image, slice(image * PAD, (image + 1) * PAD)) for image in range(padded.shape[0] // PAD)]


TAIL = 4608
HOPS = 9
TO_CORE, TURN_UP, TURN_LOW, TO_X, TO_Y, TO_LAYER, TAIL_OUT, SOON_X, SOON_Y = range(HOPS)


def units_of(devices, share):
    early, late = [], []
    for layer in range(devices // 8 - 1, -1, -1):
        if layer * 8 * share // D >= 3 * D:
            early.append((layer, (0, 1, 2), False))
        else:
            late.extend((layer, (chunk,), layer == 0 and chunk == 2) for chunk in range(3))
    late.sort(key=lambda unit: unit[1])
    return early, late


def unit_scratch(devices, share):
    rows, half = row_plan(share)
    early, late = units_of(devices, share)
    shapes = []
    for _, chunks, tail in early + late:
        wide = len(chunks) * LANES
        tall = rows + (48 if tail else 0)
        shapes += [(4, tall, wide)] * 2
        shapes += [(half, wide), (tall - half, wide)] * 2
        shapes += [(tall, wide)] * 5
    return [pltpu.VMEM(shape, jnp.bfloat16) for shape in shapes]


class Unit:
    def __init__(self, index, plan, devices, share, refs, shared):
        self.index, self.devices, self.share = index, devices, share
        self.layer, self.chunks, self.tail = plan
        (
            self.core_out, self.core_in, self.up_out, self.low_out, self.up_in, self.low_in,
            self.x_out, self.y_out, self.x_in, self.y_in, self.z_out,
        ) = refs
        (
            self.lines, self.g_tail, self.total, self.tail_total, self.z_in, self.tail_in,
            self.send_sem, self.recv_sem, self.z_sem, self.tail_sem,
        ) = shared
        self.rows, self.half = row_plan(share)
        self.stage = 0
        self.copies = {}
        me = lax.axis_index("dp")
        self.me = me
        self.z = me // 8
        self.core, self.x_side, self.y_side = other(me, 0), other(me, 1), other(me, 2)

    def copy(self, kind, source, target, device, recv=None):
        made = pltpu.make_async_remote_copy(
            src_ref=source,
            dst_ref=target,
            send_sem=self.send_sem.at[self.index, kind],
            recv_sem=self.recv_sem.at[self.index, kind] if recv is None else recv,
            device_id=(device,),
            device_id_type=pl.DeviceIdType.MESH,
        )
        return made

    def send(self, kind, source, target, device):
        self.copies[kind] = self.copy(kind, source, target, device)
        self.copies[kind].start()

    def advance(self):
        (self.pack, self.turn, self.along, self.arrive)[self.stage]()
        self.stage += 1

    def block(self, owner, spot, begin, end, index):
        first = owner * self.share // D
        chunk = self.chunks[index]
        lanes = slice(index * LANES, (index + 1) * LANES)
        value = self.lines[chunk, pl.ds(first + begin, end - begin), :]
        if spot is not None:
            value = value + self.core_in[spot, begin:end, lanes].astype(jnp.float32)
        return value

    def tail_block(self, spot, index):
        value = self.g_tail[:, index * LANES : (index + 1) * LANES]
        if spot is not None:
            at = self.rows + 16 * index
            value = value + self.core_in[spot, at : at + 16, :].astype(jnp.float32)
        return value

    def owner(self, spot, core):
        return self.layer * 8 + spot * 2 + core

    def pack(self):
        core = self.me % 2
        for spot in range(4):
            for index in range(len(self.chunks)):
                lanes = slice(index * LANES, (index + 1) * LANES)
                value = self.block(self.owner(spot, 1 - core), None, 0, self.rows, index)
                self.core_out[spot, : self.rows, lanes] = value.astype(jnp.bfloat16)
            if self.tail:
                for index in range(3):
                    at = self.rows + 16 * index
                    self.core_out[spot, at : at + 16, :] = self.tail_block(None, index).astype(
                        jnp.bfloat16
                    )
        self.send(TO_CORE, self.core_out, self.core_in, self.core)

    def spot_of(self, device):
        return device // 2 % 4

    def turn(self):
        self.copies[TO_CORE].wait_recv()
        spot = self.spot_of(other(self.x_side, 2))
        owner = self.owner(spot, self.me % 2)
        half, rows = self.half, self.rows
        for index in range(len(self.chunks)):
            lanes = slice(index * LANES, (index + 1) * LANES)
            self.up_out[:, lanes] = self.block(owner, spot, 0, half, index).astype(jnp.bfloat16)
            self.low_out[: rows - half, lanes] = self.block(
                owner, spot, half, rows, index
            ).astype(jnp.bfloat16)
        if self.tail:
            for index in range(3):
                at = rows - half + 16 * index
                self.low_out[at : at + 16, :] = self.tail_block(spot, index).astype(jnp.bfloat16)
        self.send(TURN_UP, self.up_out, self.up_in, self.y_side)
        self.send(TURN_LOW, self.low_out, self.low_in, self.x_side)
        self.soon(SOON_X, self.x_side, self.x_out, self.x_in, half, rows)
        self.soon(SOON_Y, self.y_side, self.y_out, self.y_in, 0, half)

    def soon(self, kind, device, out, into, begin, end):
        spot = self.spot_of(device)
        owner = self.owner(spot, self.me % 2)
        for index in range(len(self.chunks)):
            lanes = slice(index * LANES, (index + 1) * LANES)
            out[begin:end, lanes] = self.block(owner, spot, begin, end, index).astype(jnp.bfloat16)
        size = end - begin
        if self.tail and begin:
            size += 48
            for index in range(3):
                at = end + 16 * index
                out[at : at + 16, :] = self.tail_block(spot, index).astype(jnp.bfloat16)
        self.send(kind, out.at[pl.ds(begin, size)], into.at[pl.ds(begin, size)], device)

    def along(self):
        half, rows = self.half, self.rows
        tall = rows - half + (48 if self.tail else 0)
        for kind, device, out, into, begin, end, size in (
            (TURN_UP, self.x_side, self.x_out, self.x_in, 0, half, half),
            (TURN_LOW, self.y_side, self.y_out, self.y_in, half, rows, tall),
        ):
            self.copies[kind].wait_recv()
            spot = self.spot_of(device)
            owner = self.owner(spot, self.me % 2)
            turned = self.up_in if kind == TURN_UP else self.low_in
            for index in range(len(self.chunks)):
                lanes = slice(index * LANES, (index + 1) * LANES)
                value = self.block(owner, spot, begin, end, index)
                value = value + turned[: end - begin, lanes].astype(jnp.float32)
                out[begin:end, lanes] = value.astype(jnp.bfloat16)
            if self.tail and begin:
                for index in range(3):
                    at = rows + 16 * index
                    value = self.tail_block(spot, index)
                    value = value + turned[at - half : at - half + 16, :].astype(jnp.float32)
                    out[at : at + 16, :] = value.astype(jnp.bfloat16)
            self.send(
                TO_X if kind == TURN_UP else TO_Y,
                out.at[pl.ds(begin, size)],
                into.at[pl.ds(begin, size)],
                device,
            )

    def away(self, source):
        first, last = self.chunks[0] * LANES, (self.chunks[-1] + 1) * LANES
        return self.copy(
            TO_LAYER,
            self.z_out.at[pl.ds(0, self.rows)],
            self.z_in.at[source, :, pl.ds(first, last - first)],
            self.layer * 8 + self.me % 8,
            self.z_sem.at[self.index, source],
        )

    def tail_away(self, source):
        return self.copy(
            TAIL_OUT,
            self.z_out.at[pl.ds(self.rows, 48)],
            self.tail_in.at[source],
            self.devices - 8 + self.me % 8,
            self.tail_sem.at[source],
        )

    def arrive(self):
        for kind in (TO_X, TO_Y, SOON_X, SOON_Y):
            self.copies[kind].wait_recv()
        spot = self.spot_of(self.me)
        owner = self.owner(spot, self.me % 2)
        rows = self.rows
        for index, chunk in enumerate(self.chunks):
            lanes = slice(index * LANES, (index + 1) * LANES)
            value = self.block(owner, spot, 0, rows, index)
            value = value + self.x_in[:rows, lanes].astype(jnp.float32)
            value = value + self.y_in[:rows, lanes].astype(jnp.float32)
            self.z_out[:rows, lanes] = value.astype(jnp.bfloat16)

            @pl.when(self.z == self.layer)
            def _(value=value, chunk=chunk):
                self.total[:rows, chunk * LANES : (chunk + 1) * LANES] = value

        @pl.when(self.z != self.layer)
        def _():
            self.away(self.z).start()

        if self.tail:
            last = self.devices // 8 - 1
            for index in range(3):
                at = rows + 16 * index
                value = self.tail_block(spot, index)
                value = value + self.x_in[at : at + 16, :].astype(jnp.float32)
                value = value + self.y_in[at : at + 16, :].astype(jnp.float32)
                self.z_out[at : at + 16, :] = value.astype(jnp.bfloat16)
                self.tail_total[:, index * LANES : (index + 1) * LANES] = value

            @pl.when(self.z != last)
            def _():
                self.tail_away(self.z).start()

    def finish(self):
        last = self.devices // 8 - 1
        for made in self.copies.values():
            made.wait_send()

        @pl.when(self.z != self.layer)
        def _():
            self.away(self.z).wait_send()

        first, end = self.chunks[0] * LANES, (self.chunks[-1] + 1) * LANES
        for source in range(last + 1):
            if source != self.layer:

                @pl.when(self.z == self.layer)
                def _(source=source):
                    self.away(source).wait_recv()
                    self.total[: self.rows, first:end] += self.z_in[source, :, first:end].astype(jnp.float32)

        if self.tail:

            @pl.when(self.z != last)
            def _():
                self.tail_away(self.z).wait_send()

            for source in range(last):

                @pl.when(self.z == last)
                def _(source=source):
                    self.tail_away(source).wait_recv()
                    for index in range(3):
                        self.tail_total[:, index * LANES : (index + 1) * LANES] += self.tail_in[
                            source, 16 * index : 16 * index + 16, :
                        ].astype(jnp.float32)


def step_kernel(
    devices, share, tokens, cot, raw, result, grad_tokens, out,
    w_qkv, w_out, w_up, w_down, tail, shard, slots, pull_send, pull_recv,
    xbuf, dybuf, xhat, a16, qkv16, probs, o16, h, xhat2, c16, acc, dc, dy16, dh, dh16, do16, dqkv16,
    s1, s2, slope, lines, g_tail, total, tail_total, z_in, tail_in, send_sem, recv_sem, z_sem, tail_sem, *refs,
):
    me = lax.axis_index("dp")
    greet_partners(me, devices)
    early, late = units_of(devices, share)
    shared = (
        lines, g_tail, total, tail_total, z_in, tail_in, send_sem, recv_sem, z_sem, tail_sem,
    )
    units = [
        Unit(index, plan, devices, share, refs[index * 11 : index * 11 + 11], shared)
        for index, plan in enumerate(early + late)
    ]
    count = len(early)
    early, late = units[:count], units[count:]
    firsts = {unit: unit.layer * 8 * share // D for unit in early}
    down = [unit for unit in early if firsts[unit] >= 8 * D]
    up = [unit for unit in early if 4 * D <= firsts[unit] < 8 * D]
    mixed = [unit for unit in early if firsts[unit] < 4 * D]
    first, second, third = ([unit for unit in late if unit.chunks[0] == pair] for pair in range(3))

    align(share, raw, total, shard)
    wait_partners(devices)
    gather = Gather(devices, share, lines, shard, slots, pull_send, pull_recv)
    order = columns_of(devices)
    gather.begin(order)
    lines[...] = jnp.zeros_like(lines)
    load(tokens, xbuf)
    load(cot, dybuf)
    normalize(xbuf, xhat, s1)
    gather_weights(gather, order, w_qkv, w_out, w_up, w_down, tail)
    lines[:, TAIL:, :] = jnp.zeros_like(lines[:, TAIL:, :])
    attention_in(xhat, tail, a16, w_qkv, qkv16)
    attention(qkv16, probs, o16)
    middle(xbuf, o16, w_out, tail, h, xhat2, s2, c16, dybuf, dy16)
    feed_forward(c16, dy16, w_up, w_down, tail, acc, slope, lines)
    advance(down)
    feed_forward_back(0, c16, dy16, w_up, w_down, slope, dc, lines, g_tail)
    feed_forward_back(1, c16, dy16, w_up, w_down, slope, dc, lines, g_tail)
    advance(down)
    feed_forward_back(2, c16, dy16, w_up, w_down, slope, dc, lines, g_tail)
    feed_forward_back(3, c16, dy16, w_up, w_down, slope, dc, lines, g_tail)
    advance(up)
    feed_forward_end(h, acc, tail, dc, xhat2, s2, dybuf, result, dh, dh16, g_tail)
    g_tail[2:4, :] = jnp.zeros((2, D), jnp.float32)
    advance(down)
    advance(up)
    attention_out_back(o16, dh16, w_out, lines, do16)
    advance(mixed)
    attention_back(0, qkv16, probs, do16, dqkv16, g_tail)
    advance(down)
    advance(mixed)
    attention_in_back(0, a16, dqkv16, w_qkv, lines, acc)
    advance(first)
    advance(up)
    attention_back(1, qkv16, probs, do16, dqkv16, g_tail)
    advance(first)
    attention_in_back(1, a16, dqkv16, w_qkv, lines, acc)
    advance(second)
    advance(mixed)
    attention_back(2, qkv16, probs, do16, dqkv16, g_tail)
    advance(second)
    attention_in_back(2, a16, dqkv16, w_qkv, lines, acc)
    input_sums(acc, xhat, g_tail)
    advance(third)
    advance(first)
    grad_input(acc, tail, xhat, s1, dh, grad_tokens)
    advance(up)
    advance(third)
    advance(second)
    advance(mixed)
    advance(first)
    advance(third)
    advance(second)
    advance(third)
    for unit in units:
        unit.finish()
    at = TAIL - (devices - 1) * share // D

    @pl.when(me == devices - 1)
    def _():
        total[at : at + 12, :] += tail_total[0:12, :]

    rows, _ = row_plan(share)
    chunks = D // LANES
    for chunk in range(chunks):
        out[pl.ds(chunk, rows, stride=chunks), :] = total[:rows, lanes_of(chunk, LANES)]


def advance(units):
    for unit in units:
        unit.advance()


def load(source, padded):
    for image in range(source.shape[1]):
        at = image * PAD
        padded[at + PAD - 16 : at + PAD, :] = jnp.zeros((16, D), jnp.float32)
        padded[at : at + SEQ, :] = source[:, image, :]


def normalize(xbuf, xhat, s1):
    for _, rows in images_of(xbuf):
        normed, factor = layer_norm(xbuf[rows, :])
        xhat[rows, :] = normed
        s1[rows, :] = factor


def attention_in(xhat, tail, a16, w_qkv, qkv16):
    for _, rows in images_of(xhat):
        a16[rows, :] = (xhat[rows, :] * tail[0:1, :] + tail[1:2, :]).astype(jnp.bfloat16)
    for piece in range(3):
        cols = slice(piece * D, (piece + 1) * D)
        value = dot_nn(a16[...], w_qkv[:, cols])
        if piece == 0:
            value = value + tail[2:3, :]
        if piece == 2:
            value = value + tail[3:4, :]
        qkv16[:, cols] = value.astype(jnp.bfloat16)


def half_of(values, half):
    lane = lax.broadcasted_iota(jnp.int32, values.shape, 1)
    return jnp.where((lane < 64) if half == 0 else (lane >= 64), values, jnp.zeros_like(values))


def views(step):
    image, pair = step // 3, step % 3
    rows = pl.ds(pl.multiple_of(image * PAD, 16), PAD)
    return rows, [pl.ds(pl.multiple_of(part * D + pair * 128, 128), 128) for part in range(3)]


def attention(qkv16, probs, o16):
    def body(step, carry):
        rows, (qs, ks, vs) = views(step)
        query, key, value = qkv16[rows, qs], qkv16[rows, ks], qkv16[rows, vs]
        total = None
        for half in range(2):
            scores = dot_nt(query, half_of(key, half)) * 0.125
            column = lax.broadcasted_iota(jnp.int32, scores.shape, 1)
            scores = jnp.where(column < SEQ, scores, -jnp.inf)
            raised = jnp.exp(scores - jnp.max(scores, axis=-1, keepdims=True))
            prob = raised / jnp.sum(raised, axis=-1, keepdims=True)
            probs[step * 2 + half] = prob
            term = dot_nn(prob.astype(jnp.bfloat16), half_of(value, half))
            total = term if total is None else total + term
        o16[rows, qs] = total.astype(jnp.bfloat16)
        return carry

    lax.fori_loop(0, qkv16.shape[0] // PAD * 3, body, 0, unroll=True)


def middle(xbuf, o16, w_out, tail, h, xhat2, s2, c16, dybuf, dy16):
    for _, rows in images_of(xbuf):
        value = xbuf[rows, :] + (dot_nn(o16[rows, :], w_out[...]) + tail[4:5, :])
        h[rows, :] = value
        normed, factor = layer_norm(value)
        xhat2[rows, :] = normed
        s2[rows, :] = factor
        c16[rows, :] = (normed * tail[5:6, :] + tail[6:7, :]).astype(jnp.bfloat16)
        dy16[rows, :] = dybuf[rows, :].astype(jnp.bfloat16)


def lanes_of(index, width):
    return slice(index * width, (index + 1) * width)


def feed_forward(c16, dy16, w_up, w_down, tail, acc, slope, lines):
    for line in range(FF // D):
        cols = lanes_of(line, D)
        pre = dot_nn(c16[...], w_up[:, cols]) + tail[8 + line : 9 + line, :]
        phi = 0.5 * (1.0 + lax.erf(pre * 0.7071067811865476))
        slope[:, cols] = phi + pre * jnp.exp(-0.5 * pre * pre) * 0.3989422804014327
        act = (pre * phi).astype(jnp.bfloat16)
        value = dot_nn(act, w_down[cols, :])
        acc[...] = value if line == 0 else acc[...] + value
        grad_down = dot_tn(act, dy16[...])
        first = 8 * D + line * D
        for chunk in range(D // LANES):
            lines[chunk, first : first + D, :] = grad_down[:, lanes_of(chunk, LANES)]


def feed_forward_back(line, c16, dy16, w_up, w_down, slope, dc, lines, g_tail):
    cols = lanes_of(line, D)
    grad_pre = dot_nt(dy16[...], w_down[cols, :]) * slope[:, cols]
    half = grad_pre.astype(jnp.bfloat16)
    grad_up = dot_tn(c16[...], half)
    for chunk in range(D // LANES):
        lines[chunk, pl.ds(4 * D + line, D, stride=4), :] = grad_up[:, lanes_of(chunk, LANES)]
    g_tail[8 + line : 9 + line, :] = column_sum(grad_pre)
    value = dot_nt(half, w_up[:, cols])
    dc[...] = value if line == 0 else dc[...] + value


def feed_forward_end(h, acc, tail, dc, xhat2, s2, dybuf, result, dh, dh16, g_tail):
    sums = [0.0] * 4
    for image, rows in images_of(h):
        value = h[rows, :] + (acc[rows, :] + tail[7:8, :])
        result[:, image, :] = value[:SEQ]
        grad, normed = dc[rows, :], xhat2[rows, :]
        hidden = dybuf[rows, :] + norm_back(grad * tail[5:6, :], normed, s2[rows, :])
        dh[rows, :] = hidden
        dh16[rows, :] = hidden.astype(jnp.bfloat16)
        terms = (hidden, grad * normed, grad, dybuf[rows, :])
        sums = [old + column_sum(new) for old, new in zip(sums, terms)]
    for index in range(4):
        g_tail[4 + index : 5 + index, :] = sums[index]
    g_tail[12:16, :] = jnp.zeros((4, D), jnp.float32)


def attention_out_back(o16, dh16, w_out, lines, do16):
    grad_out = dot_tn(o16[...], dh16[...])
    for chunk in range(D // LANES):
        lines[chunk, 3 * D : 4 * D, :] = grad_out[:, chunk * LANES : (chunk + 1) * LANES]
    do16[...] = dot_nt(dh16[...], w_out[...]).astype(jnp.bfloat16)


def attention_back(pair, qkv16, probs, do16, dqkv16, g_tail):
    def body(image, carry):
        step = image * 3 + pair
        rows, (qs, ks, vs) = views(step)
        query, key, value, grad = qkv16[rows, qs], qkv16[rows, ks], qkv16[rows, vs], do16[rows, qs]
        dq = dk = dv = None
        for half in range(2):
            prob = probs[step * 2 + half]
            dv_term = dot_tn(prob.astype(jnp.bfloat16), half_of(grad, half))
            grad_prob = dot_nt(grad, half_of(value, half))
            delta = jnp.sum(prob * grad_prob, axis=-1, keepdims=True)
            ds = (prob * (grad_prob - delta) * 0.125).astype(jnp.bfloat16)
            dq_term = dot_nn(ds, half_of(key, half))
            dk_term = dot_tn(ds, half_of(query, half))
            if half == 0:
                dq, dk, dv = dq_term, dk_term, dv_term
            else:
                dq, dk, dv = dq + dq_term, dk + dk_term, dv + dv_term
        dqkv16[rows, qs] = dq.astype(jnp.bfloat16)
        dqkv16[rows, ks] = dk.astype(jnp.bfloat16)
        dqkv16[rows, vs] = dv.astype(jnp.bfloat16)
        g_tail[2:3, qs] += column_sum(dq)
        g_tail[3:4, qs] += column_sum(dv)
        return carry

    lax.fori_loop(0, qkv16.shape[0] // PAD, body, 0, unroll=True)


def attention_in_back(pair, a16, dqkv16, w_qkv, lines, acc):
    parts = [slice(part * D + pair * LANES, part * D + (pair + 1) * LANES) for part in range(3)]
    grads = jnp.concatenate([dqkv16[:, part] for part in parts], axis=1)
    weights = jnp.concatenate([w_qkv[:, part] for part in parts], axis=1)
    grad_w = dot_tn(a16[...], grads)
    for part in range(3):
        lines[pair, pl.ds(part, D, stride=3), :] = grad_w[:, part * LANES : (part + 1) * LANES]
    value = dot_nt(grads, weights)
    acc[...] = value if pair == 0 else acc[...] + value


def input_sums(acc, xhat, g_tail):
    sums = [0.0] * 2
    for _, rows in images_of(acc):
        grad = acc[rows, :]
        sums = [old + column_sum(new) for old, new in zip(sums, (grad * xhat[rows, :], grad))]
    for index in range(2):
        g_tail[index : index + 1, :] = sums[index]


def grad_input(acc, tail, xhat, s1, dh, grad_tokens):
    for image, rows in images_of(acc):
        value = dh[rows, :] + norm_back(acc[rows, :] * tail[0:1, :], xhat[rows, :], s1[rows, :])
        grad_tokens[:, image, :] = value[:SEQ]


def compute_scratch(images):
    f32, bf16 = jnp.float32, jnp.bfloat16
    rows = images * PAD
    return [
        pltpu.VMEM((rows, D), f32),
        pltpu.VMEM((rows, D), f32),
        pltpu.VMEM((rows, D), f32),
        pltpu.VMEM((rows, D), bf16),
        pltpu.VMEM((rows, 3 * D), bf16),
        pltpu.VMEM((images * HEADS, PAD, PAD), f32),
        pltpu.VMEM((rows, D), bf16),
        pltpu.VMEM((rows, D), f32),
        pltpu.VMEM((rows, D), f32),
        pltpu.VMEM((rows, D), bf16),
        pltpu.VMEM((rows, D), f32),
        pltpu.VMEM((rows, D), f32),
        pltpu.VMEM((rows, D), bf16),
        pltpu.VMEM((rows, D), f32),
        pltpu.VMEM((rows, D), bf16),
        pltpu.VMEM((rows, D), bf16),
        pltpu.VMEM((rows, 3 * D), bf16),
        pltpu.VMEM((rows, 1), f32),
        pltpu.VMEM((rows, 1), f32),
        pltpu.VMEM((rows, FF), f32),
    ]


def compute(tokens, cotangent, raw, devices, share):
    f32, bf16 = jnp.float32, jnp.bfloat16
    rows, _ = row_plan(share)
    layers = devices // 8
    early, late = units_of(devices, share)
    count = len(early) + len(late)
    vmem = pl.BlockSpec(memory_space=pltpu.VMEM)
    result, grad_tokens, total = pl.pallas_call(
        functools.partial(step_kernel, devices, share),
        out_shape=(
            jax.ShapeDtypeStruct(tokens.shape, f32),
            jax.ShapeDtypeStruct(tokens.shape, f32),
            jax.ShapeDtypeStruct((rows * D // LANES, LANES), f32),
        ),
        in_specs=[vmem] * 3,
        out_specs=[vmem] * 3,
        scratch_shapes=[
            pltpu.VMEM((D, 3 * D), bf16),
            pltpu.VMEM((D, D), bf16),
            pltpu.VMEM((D, FF), bf16),
            pltpu.VMEM((FF, D), bf16),
            pltpu.VMEM((16, D), f32),
            pltpu.VMEM((rows, D), bf16),
            pltpu.VMEM((devices, rows, D), bf16),
            pltpu.SemaphoreType.DMA((8 * layers,)),
            pltpu.SemaphoreType.DMA((8 * layers,)),
        ]
        + compute_scratch(tokens.shape[1])
        + [
            pltpu.VMEM((D // LANES, LINES + rows + 24, LANES), f32),
            pltpu.VMEM((16, D), f32),
            pltpu.VMEM((rows + 8, D), f32),
            pltpu.VMEM((16, D), f32),
            pltpu.VMEM((layers, rows, D), jnp.bfloat16),
            pltpu.VMEM((layers, 48, LANES), jnp.bfloat16),
            pltpu.SemaphoreType.DMA((count, HOPS)),
            pltpu.SemaphoreType.DMA((count, HOPS)),
            pltpu.SemaphoreType.DMA((count, layers)),
            pltpu.SemaphoreType.DMA((layers,)),
        ]
        + unit_scratch(devices, share),
        compiler_params=pltpu.CompilerParams(
            collective_id=0, has_side_effects=True, vmem_limit_bytes=60 * 2**20
        ),
    )(tokens, cotangent, raw)
    offset = (lax.axis_index("dp") * share) % D
    return result, grad_tokens, lax.dynamic_slice(total.reshape(-1), (offset,), (share,))


def adamw(params, grads, first, second, position):
    first_end = 3 * D * D
    second_end = first_end + D * D
    third_end = second_end + D * FF
    fourth_end = third_end + FF * D
    rate = jnp.where(
        position < first_end,
        0.01,
        jnp.where(
            position < second_end,
            0.1,
            jnp.where(position < third_end, 0.01, jnp.where(position < fourth_end, 0.005, 0.1)),
        ),
    )
    first_new = 0.9 * first + 0.1 * grads
    second_new = 0.999 * second + 0.001 * grads * grads
    update = (
        first_new / (1.0 - 0.9**STEP) / (jnp.sqrt(second_new / (1.0 - 0.999**STEP)) + 1e-08)
        + 0.1 * params
    )
    return (params - rate * update, first_new, second_new)


def per_device(tokens, params, moment1, moment2, cotangent):
    devices = lax.axis_size("dp")
    length = params.shape[0]
    rows, _ = row_plan(length)
    raw = jnp.pad(params, (0, rows * D - length)).reshape(-1, LANES)
    result, grad_tokens, shares = compute(
        tokens.transpose(1, 0, 2), cotangent.transpose(1, 0, 2), raw, devices, length
    )
    result, grad_tokens = result.transpose(1, 0, 2), grad_tokens.transpose(1, 0, 2)
    count = tokens.shape[0] * tokens.shape[1] * devices
    grad_params = shares * (1.0 / math.sqrt(count))
    position = lax.axis_index("dp") * length + jnp.arange(length, dtype=jnp.int32)
    new_params, new_first, new_second = adamw(params, grad_params, moment1, moment2, position)
    return (result, grad_tokens, grad_params, new_params, new_first, new_second)


def solution(mesh):
    in_specs = (P("dp", None, None), P("dp"), P("dp"), P("dp"), P("dp", None, None))
    out_specs = (P("dp", None, None), P("dp", None, None), P("dp"), P("dp"), P("dp"), P("dp"))
    return jax.shard_map(
        per_device, mesh=mesh, in_specs=in_specs, out_specs=out_specs, check_vma=False
    )
```
